512 devices in a mesh: gx: 32 (over x, z), gy: 16 (over y, core).
Axes of the slice: x: 4, y: 8, z: 8, core: 2. Of those that a mesh axis runs over, the one named last changes fastest.
Arguments:
- load: float32 [512, 256, 512], P('gx', 'gy'), may hold values from -130 to 130
- conductivity: bfloat16 [512, 256, 512], P('gx', 'gy'), may hold values from 0.29882812 to 3
- flags: int32 [512, 256, 512], P('gx', 'gy'), may hold values from 0 to 1, as said below
- region: int32 [64, 32, 64], P('gx', 'gy'), may hold values from 0 to 2
- kappa_table: float32 [3], replicated, may hold values from 10 to 100
Outputs:
- solution: float32 [512, 256, 512], P('gx', 'gy')
- residual: float32 [512, 256, 512], P('gx', 'gy')
- direction: float32 [512, 256, 512], P('gx', 'gy')
The draws below stay inside these ranges and needn't reach their ends.
Inputs may be any that keep to these rules, and one draw needn't show every extreme that they name: flags are 1 only at nodes of the first layer along the third dimension, and all copies of one shared node carry the same flag.
All inputs are finite; a program needn't handle non-finite values.
Results may differ from the reference program's by a relative error of at most 0.0003.
Values sent between devices are 32-bit elements; how exact they have to be, the bound alone decides.
No kernel may reach another device: no remote copies, remote signals or barrier semaphores. Data moves between devices by JAX's collectives and lax.ppermute only.
A program may use at most 64 MiB of HBM per device.

```python
import math
import jax
import jax.numpy as jnp
import numpy as np
from jax import lax

NREG = 3
EZ = 64
EXT = 64
EYT = 32
NX = 512
NY = 256
NZ = 512


def draw_load(key, part):
    key_base, key_plane = jax.random.split(key)
    pos_x = jnp.arange(NX, dtype=jnp.float32) / NX
    pos_y = jnp.arange(NY, dtype=jnp.float32) / NY
    amplitude = (1.0 + pos_x)[:, None, None] * (1.0 + pos_y)[None, :, None]
    plane_scale = jnp.exp(jax.random.uniform(key_plane, (NZ,), jnp.float32, 0.0, math.log(10.0)))
    base_values = jnp.clip(jax.random.normal(key_base, (NX, NY, NZ), jnp.float32), -3.0, 3.0)
    return (base_values * amplitude * plane_scale[None, None, :]).astype(jnp.float32)


def draw_flags(key, part):
    phys_nx = 7 * (NX // 8) + 1
    phys_ny = 7 * (NY // 8) + 1
    random_bits = jax.random.randint(key, (phys_nx, phys_ny), 0, 2, dtype=jnp.int32)
    rows_x = jnp.arange(NX, dtype=jnp.int32)
    rows_y = jnp.arange(NY, dtype=jnp.int32)
    phys_x = rows_x // 8 * 7 + rows_x % 8
    phys_y = rows_y // 8 * 7 + rows_y % 8
    plane_bits = random_bits[phys_x][:, phys_y]
    layer_ids = jnp.arange(NZ, dtype=jnp.int32)
    return jnp.where(layer_ids[None, None, :] == 0, plane_bits[:, :, None], 0).astype(jnp.int32)


def set_ends(values, rng, smallest, largest):
    place = [jax.random.randint(jax.random.fold_in(rng, axis), (), 0, length) for axis, length in enumerate(values.shape)]
    longest = values.shape.index(max(values.shape))
    neighbour = place[:longest] + [(place[longest] + 1) % values.shape[longest]] + place[longest + 1:]
    return values.at[tuple(place)].set(smallest).at[tuple(neighbour)].set(largest)


def shard_levels(key, shape, cuts, smallest, largest):
    factor_of = 1.0
    for dim, shards_of in cuts:
        draws = jax.random.uniform(jax.random.fold_in(jax.random.fold_in(key, 6), dim), (shards_of,), jnp.float32, smallest / len(cuts), largest / len(cuts))
        factor_of = factor_of * jnp.repeat(jnp.exp(draws), shape[dim] // shards_of).reshape((-1,) + (1,) * (len(shape) - 1 - dim))
    return factor_of


def setup_inputs(seed: int = 0) -> dict:
    streams_of = jax.random.split(jax.random.key(seed), 6)
    return {
        "load": draw_load(jax.random.fold_in(streams_of[5], 71), 0),
        "conductivity": jnp.clip(jnp.exp(math.log(3.0) - 2.306499 * jax.random.uniform(streams_of[1], (NX, NY, NZ), jnp.float32) ** shard_levels(streams_of[1], (NX, NY, NZ), ((0, 32), (1, 16)), -0.2, 0.2)), 0.29882812, 3.0).astype(jnp.bfloat16),
        "flags": draw_flags(jax.random.fold_in(streams_of[5], 71), 0),
        "region": set_ends(jax.random.randint(streams_of[3], (EXT, EYT, EZ), 0, NREG), jax.random.fold_in(streams_of[3], 1), 0, NREG - 1).astype(jnp.int32),
        "kappa_table": jnp.clip(jnp.exp(jax.random.uniform(streams_of[4], (NREG,), jnp.float32, math.log(10.0), math.log(100.0))), 10.0, 100.0),
    }


CHEB_CENTER = 24.0
CHEB_HALF = 23.0


def gll_tables():
    nodes_gll = np.array([-1.0, -0.8717401485096066, -0.5917001814331423, -0.2092992179024789, 0.2092992179024789, 0.5917001814331423, 0.8717401485096066, 1.0])
    legendre_prev = np.ones(8)
    legendre_now = nodes_gll.copy()
    for degree in range(1, 7):
        legendre_next = ((2 * degree + 1) * nodes_gll * legendre_now - degree * legendre_prev) / (degree + 1)
        legendre_prev = legendre_now
        legendre_now = legendre_next
    weights_gll = 2.0 / (56.0 * legendre_now ** 2)
    diff_table = np.zeros((8, 8))
    for row_index in range(8):
        for col_index in range(8):
            if row_index != col_index:
                diff_table[row_index, col_index] = legendre_now[row_index] / (legendre_now[col_index] * (nodes_gll[row_index] - nodes_gll[col_index]))
    diff_table[0, 0] = -14.0
    diff_table[7, 7] = 14.0
    return diff_table, weights_gll


def pair_fold(padded, which_dim):
    length = padded.shape[which_dim]
    blocks = (length - 2) // 8
    lower_rows = lax.slice_in_dim(padded, 0, length, 8, which_dim)
    upper_rows = lax.slice_in_dim(padded, 1, length, 8, which_dim)
    joined = lower_rows + upper_rows
    inner_rows = lax.slice_in_dim(padded, 1, length - 1, 1, which_dim)
    inner_rows = inner_rows.reshape(inner_rows.shape[:which_dim] + (blocks, 8) + inner_rows.shape[which_dim + 1:])
    first_rows = jnp.expand_dims(lax.slice_in_dim(joined, 0, blocks, 1, which_dim), which_dim + 1)
    last_rows = jnp.expand_dims(lax.slice_in_dim(joined, 1, blocks + 1, 1, which_dim), which_dim + 1)
    middle = lax.slice_in_dim(inner_rows, 1, 7, 1, which_dim + 1)
    result = jnp.concatenate([first_rows, middle, last_rows], axis=which_dim + 1)
    return result.reshape(inner_rows.shape[:which_dim] + (blocks * 8,) + inner_rows.shape[which_dim + 2:])


def apply_local(vector, coefficient, reaction, derivative, block_deriv):
    rows_x, rows_y, rows_z = vector.shape
    block_z = block_deriv.shape[0]
    highest = lax.Precision.HIGHEST
    shape_x = (rows_x // 8, 8, rows_y, rows_z)
    grad_x = jnp.einsum('ab,ebyz->eayz', derivative, vector.reshape(shape_x), precision=highest)
    back_x = jnp.einsum('ab,eayz->ebyz', derivative, grad_x * coefficient.reshape(shape_x), precision=highest)
    shape_y = (rows_x, rows_y // 8, 8, rows_z)
    grad_y = jnp.einsum('ab,xebz->xeaz', derivative, vector.reshape(shape_y), precision=highest)
    back_y = jnp.einsum('ab,xeaz->xebz', derivative, grad_y * coefficient.reshape(shape_y), precision=highest)
    shape_z = (rows_x, rows_y, rows_z // block_z, block_z)
    grad_z = jnp.einsum('xykb,ab->xyka', vector.reshape(shape_z), block_deriv, precision=highest)
    back_z = jnp.einsum('xyka,ab->xykb', grad_z * coefficient.reshape(shape_z), block_deriv, precision=highest)
    return back_x.reshape(vector.shape) + back_y.reshape(vector.shape) + back_z.reshape(vector.shape) + reaction * vector


def diag_local(coefficient, reaction, derivative, block_deriv):
    rows_x, rows_y, rows_z = coefficient.shape
    block_z = block_deriv.shape[0]
    highest = lax.Precision.HIGHEST
    square_d = derivative * derivative
    square_block = block_deriv * block_deriv
    part_x = jnp.einsum('qa,eqyz->eayz', square_d, coefficient.reshape(rows_x // 8, 8, rows_y, rows_z), precision=highest)
    part_y = jnp.einsum('qa,xeqz->xeaz', square_d, coefficient.reshape(rows_x, rows_y // 8, 8, rows_z), precision=highest)
    part_z = jnp.einsum('xykq,qa->xyka', coefficient.reshape(rows_x, rows_y, rows_z // block_z, block_z), square_block, precision=highest)
    return part_x.reshape(coefficient.shape) + part_y.reshape(coefficient.shape) + part_z.reshape(coefficient.shape) + reaction


def share_weights(count, offset, total):
    position = offset + jnp.arange(count, dtype=jnp.int32)
    within = position % 8
    shared = ((within == 7) & (position != total - 1)) | ((within == 0) & (position != 0))
    return jnp.where(shared, 0.5, 1.0).astype(jnp.float32)


def precondition(residual_in, diagonal, operator):
    update = residual_in / (CHEB_CENTER * diagonal)
    approx = update
    rho_prev = CHEB_HALF / CHEB_CENTER
    for sweep_index in range(2):
        rho_next = 1.0 / (2.0 * CHEB_CENTER / CHEB_HALF - rho_prev)
        update = rho_next * rho_prev * update + (2.0 * rho_next / CHEB_HALF) * (residual_in - operator(approx)) / diagonal
        approx = approx + update
        rho_prev = rho_next
    return approx


def node_kappa(region, kappa_table):
    element_kappa = jnp.zeros(region.shape, jnp.float32)
    for region_id in range(NREG):
        element_kappa = element_kappa + (region == region_id).astype(jnp.float32) * kappa_table[region_id]
    return jnp.repeat(jnp.repeat(jnp.repeat(element_kappa, 8, axis=0), 8, axis=1), 8, axis=2)


def assemble_global(vector):
    padded = jnp.pad(vector, 1)
    return pair_fold(pair_fold(pair_fold(padded, 0), 1), 2)


def reference(load, conductivity, flags, region, kappa_table):
    diff_np, weights_np = gll_tables()
    derivative = jnp.asarray(diff_np, dtype=jnp.float32)
    gll_weights = jnp.asarray(weights_np, dtype=jnp.float32)
    weight_x = jnp.tile(gll_weights, NX // 8)
    weight_y = jnp.tile(gll_weights, NY // 8)
    weight_z = jnp.tile(gll_weights, NZ // 8)
    quad_weights = weight_x[:, None, None] * weight_y[None, :, None] * weight_z[None, None, :]
    coefficient = quad_weights * conductivity.astype(jnp.float32)
    reaction = quad_weights * node_kappa(region, kappa_table)
    keep_mask = (1 - flags).astype(jnp.float32)
    mult_weights = share_weights(NX, 0, NX)[:, None, None] * share_weights(NY, 0, NY)[None, :, None] * share_weights(NZ, 0, NZ)[None, None, :]

    def operator(vector):
        local_out = apply_local(keep_mask * vector, coefficient, reaction, derivative, derivative)
        return keep_mask * assemble_global(local_out) + (1.0 - keep_mask) * vector

    diagonal = keep_mask * assemble_global(diag_local(coefficient, reaction, derivative, derivative)) + (1.0 - keep_mask)
    first_res = keep_mask * assemble_global(load)
    first_z = precondition(first_res, diagonal, operator)
    image_vec = operator(first_z)
    first_dot = jnp.sum(first_res * first_z * mult_weights)
    curv_dot = jnp.sum(first_z * image_vec * mult_weights)
    step_length = first_dot / curv_dot
    solution = step_length * first_z
    residual = first_res - step_length * image_vec
    next_z = precondition(residual, diagonal, operator)
    next_dot = jnp.sum(residual * next_z * mult_weights)
    direction = next_z + (next_dot / first_dot) * first_z
    return solution, residual, direction
```

```python
import jax
import jax.numpy as jnp
import ml_dtypes
import numpy as np
from jax import lax
from jax.experimental import pallas as pl
from jax.experimental.pallas import tpu as pltpu
from jax.sharding import PartitionSpec as P

NREG = 3
CENTER = 24.0
HALF = 23.0
RHO0 = HALF / CENTER
RHO1 = 1.0 / (2.0 * CENTER / HALF - RHO0)
RHO2 = 1.0 / (2.0 * CENTER / HALF - RHO1)
MIX1, GAIN1 = RHO1 * RHO0, 2.0 * RHO1 / HALF
MIX2, GAIN2 = RHO2 * RHO1, 2.0 * RHO2 / HALF

F32 = jnp.float32
BF16 = jnp.bfloat16
ROWS, COLS = 256, 512


def gll_tables():
    nodes = np.array(
        [
            -1.0,
            -0.8717401485096066,
            -0.5917001814331423,
            -0.2092992179024789,
            0.2092992179024789,
            0.5917001814331423,
            0.8717401485096066,
            1.0,
        ]
    )
    prev = np.ones(8)
    now = nodes.copy()
    for degree in range(1, 7):
        prev, now = now, ((2 * degree + 1) * nodes * now - degree * prev) / (degree + 1)
    weights = 2.0 / (56.0 * now**2)
    table = np.zeros((8, 8))
    for a in range(8):
        for b in range(8):
            if a != b:
                table[a, b] = now[a] / (now[b] * (nodes[a] - nodes[b]))
    table[0, 0] = -14.0
    table[7, 7] = 14.0
    return table, weights


def split_np(mat):
    high = mat.astype(ml_dtypes.bfloat16)
    low = (mat - high.astype(np.float64)).astype(ml_dtypes.bfloat16)
    return high, low


def left_pair(mat):
    high, low = split_np(mat)
    return np.stack([np.concatenate([high, high], 1), np.concatenate([low, low], 1)])


def right_pair(mat):
    high, low = split_np(mat)
    both = np.concatenate([high, low], 1)
    return np.concatenate([both, both], 0)


def constants():
    table, weights = gll_tables()
    table = table.astype(np.float32).astype(np.float64)
    weights = weights.astype(np.float32)
    eye8, eye2, eye16 = np.eye(8), np.eye(2), np.eye(16)
    d_x = np.kron(table, eye16)
    d_y = np.kron(eye8, np.kron(eye2, table))
    square = (table * table).astype(np.float32).astype(np.float64)
    q_x = np.kron(square, eye16)
    q_y = np.kron(eye8, np.kron(eye2, square))
    d_z = np.kron(eye16, table)
    q_z = np.kron(eye16, square)
    grad = left_pair(np.concatenate([d_x, d_y], 0))
    back_h, back_l = split_np(np.concatenate([d_x.T, d_y.T], 1))
    back = np.stack([back_h, back_l])
    sq = left_pair(q_x.T + q_y.T)
    grad_z = right_pair(d_z.T)
    back_z = right_pair(d_z)
    sq_z = right_pair(q_z)
    w_xy = (weights[:, None] * weights[None, :]).astype(np.float32)
    w_xy = np.tile(w_xy, (2, 2)).reshape(ROWS, 1)
    w_rows = np.ascontiguousarray(np.broadcast_to(w_xy, (ROWS, 128)))
    w_z = np.tile(weights, COLS // 8).reshape(1, COLS).astype(np.float32)
    return dict(grad=grad, back=back, sq=sq, grad_z=grad_z, back_z=back_z, sq_z=sq_z, w_rows=w_rows, w_z=w_z)


def dot(a, b):
    return lax.dot_general(a, b, (((1,), (0,)), ((), ())), preferred_element_type=F32)


def halves(v):
    high = v.astype(BF16)
    low = (v - high.astype(F32)).astype(BF16)
    return high, low


def mul_z(high, low, mat):
    outs = []
    for k in range(COLS // 128):
        part = slice(128 * k, 128 * (k + 1))
        both = dot(jnp.concatenate([high[:, part], low[:, part]], 1), mat)
        outs.append(both[:, :128] + both[:, 128:])
    return jnp.concatenate(outs, 1)


def local_op(v, coef, react, grad, back, grad_z, back_z):
    high, low = halves(v)
    rows = []
    for e in range(2):
        part = slice(128 * e, 128 * (e + 1))
        pair = jnp.concatenate([high[part], low[part]], 0)
        flux = dot(grad[0], pair) + dot(grad[1], pair)
        c = coef[part]
        f_h, f_l = halves(flux * jnp.concatenate([c, c], 0))
        rows.append(dot(back[0], f_h) + (dot(back[0], f_l) + dot(back[1], f_h)))
    out = jnp.concatenate(rows, 0)
    flux_z = mul_z(high, low, grad_z) * coef
    return out + mul_z(*halves(flux_z), back_z) + react * v


def join_z(f):
    lane = lax.broadcasted_iota(jnp.int32, (1, COLS), 1)
    upper = ((lane % 8) == 7) & (lane != COLS - 1)
    lower = ((lane % 8) == 0) & (lane != 0)
    nxt = pltpu.roll(f, COLS - 1, 1)
    prv = pltpu.roll(f, 1, 1)
    return f + jnp.where(upper, nxt, jnp.where(lower, prv, 0.0))


def emit_partial(f, p_ref, x_ref, y_ref):
    p_ref[...] = join_z(f)
    p_ref[112:128, :] = p_ref[112:128, :] + p_ref[128:144, :]
    p_ref[128:144, :] = p_ref[112:128, :]
    for x in range(16):
        r = 16 * x
        mid = p_ref[r + 7:r + 8, :] + p_ref[r + 8:r + 9, :]
        p_ref[r + 7:r + 8, :] = mid
        p_ref[r + 8:r + 9, :] = mid
        y_ref[0, x:x + 1, :] = p_ref[r:r + 1, :]
        y_ref[1, x:x + 1, :] = p_ref[r + 15:r + 16, :]
    x_ref[0] = p_ref[0:16, :]
    x_ref[1] = p_ref[240:256, :]


def take_sum(p_ref, recv, s_ref):
    left, right, below, above = recv
    s_ref[...] = p_ref[...]
    s_ref[0:16, :] = s_ref[0:16, :] + left
    s_ref[240:256, :] = s_ref[240:256, :] + right
    for x in range(16):
        r = 16 * x
        s_ref[r:r + 1, :] = s_ref[r:r + 1, :] + below[x:x + 1, :]
        s_ref[r + 15:r + 16, :] = s_ref[r + 15:r + 16, :] + above[x:x + 1, :]
    return s_ref[...]


def fold(prod):
    part = prod.reshape(ROWS // 8, 8, COLS).sum(axis=0)
    return part[:, 0:128] + part[:, 128:256] + part[:, 256:384] + part[:, 384:512]


def first_kernel(table_ref, load_ref, cond_ref, region_ref, sq_ref, sqz_ref, wr_ref, wz_ref,
                 coef_ref, react_ref, pl_ref, pd_ref, x_ref, y_ref):
    w_row = wr_ref[...]
    w_row = jnp.concatenate([w_row] * 4, axis=1)
    quad_z = wz_ref[...]
    coef = (w_row * quad_z) * cond_ref[...].reshape(ROWS, COLS).astype(F32)
    coef_ref[...] = coef
    elem = lax.broadcasted_iota(jnp.int32, (COLS // 8, COLS), 0)
    lane = lax.broadcasted_iota(jnp.int32, (COLS // 8, COLS), 1)
    spread = (lane // 8 == elem).astype(F32)
    for ex in range(2):
        ids = region_ref[ex]
        kappa = jnp.zeros(ids.shape, F32)
        for k in range(NREG):
            kappa = kappa + jnp.where(ids == k, table_ref[k], 0.0)
        kappa = lax.dot_general(kappa, spread, (((1,), (0,)), ((), ())),
                                precision=lax.Precision.HIGHEST, preferred_element_type=F32)
        for x in range(8):
            for ey in range(2):
                r = (ex * 8 + x) * 16 + ey * 8
                react_ref[r:r + 8, :] = (w_row[r:r + 8] * quad_z) * kappa[ey:ey + 1, :]
    high, low = halves(coef)
    rows = []
    for e in range(2):
        part = slice(128 * e, 128 * (e + 1))
        pair = jnp.concatenate([high[part], low[part]], 0)
        rows.append(dot(sq_ref[0], pair) + dot(sq_ref[1], pair))
    diag = jnp.concatenate(rows, 0) + mul_z(high, low, sqz_ref[...]) + react_ref[...]
    emit_partial(diag, pd_ref, x_ref.at[1], y_ref.at[1])
    emit_partial(load_ref[...].reshape(ROWS, COLS), pl_ref, x_ref.at[0], y_ref.at[0])


def second_kernel(pl_ref, pd_ref, xl_ref, xr_ref, yb_ref, ya_ref, flags_ref, coef_ref, react_ref,
                  grad_ref, back_ref, gz_ref, bz_ref,
                  r_ref, dinv_ref, p_ref, x_ref, y_ref, s_ref):
    diag = take_sum(pd_ref, (xl_ref[1], xr_ref[1], yb_ref[1], ya_ref[1]), s_ref)
    dinv_ref[...] = 1.0 / diag
    keep = (1 - flags_ref[...].reshape(ROWS, 128)).astype(F32)
    dinv_ref[:, 0:128] = keep * dinv_ref[:, 0:128]
    r = take_sum(pl_ref, (xl_ref[0], xr_ref[0], yb_ref[0], ya_ref[0]), s_ref)
    r_ref[...] = r
    r_ref[:, 0:128] = keep * r_ref[:, 0:128]
    a0 = dinv_ref[...] * r_ref[...] * (1.0 / CENTER)
    f = local_op(a0, coef_ref[...], react_ref[...], grad_ref, back_ref, gz_ref[...], bz_ref[...])
    emit_partial(f, p_ref, x_ref, y_ref)


def sweep1_kernel(pin_ref, xl_ref, xr_ref, yb_ref, ya_ref, r_ref, dinv_ref, coef_ref, react_ref,
                  grad_ref, back_ref, gz_ref, bz_ref,
                  a1_ref, p_ref, x_ref, y_ref, s_ref):
    image = take_sum(pin_ref, (xl_ref[0], xr_ref[0], yb_ref[0], ya_ref[0]), s_ref)
    dinv, r = dinv_ref[...], r_ref[...]
    a0 = dinv * r * (1.0 / CENTER)
    a1 = (1.0 + MIX1) * a0 + GAIN1 * (dinv * (r - image))
    a1_ref[...] = a1
    f = local_op(a1, coef_ref[...], react_ref[...], grad_ref, back_ref, gz_ref[...], bz_ref[...])
    emit_partial(f, p_ref, x_ref, y_ref)


def sweep2(image, a1, r, dinv):
    a0 = dinv * r * (1.0 / CENTER)
    return a1 + (MIX2 * (a1 - a0) + GAIN2 * (dinv * (r - image)))


def third_kernel(pin_ref, xl_ref, xr_ref, yb_ref, ya_ref, r_ref, dinv_ref, a1_ref, load_ref, coef_ref, react_ref,
                 grad_ref, back_ref, gz_ref, bz_ref,
                 z_ref, p_ref, x_ref, y_ref, dots_ref, s_ref):
    image = take_sum(pin_ref, (xl_ref[0], xr_ref[0], yb_ref[0], ya_ref[0]), s_ref)
    z = sweep2(image, a1_ref[...], r_ref[...], dinv_ref[...])
    z_ref[...] = z
    dots_ref[0] = fold(load_ref[...].reshape(ROWS, COLS) * z)
    f = local_op(z, coef_ref[...], react_ref[...], grad_ref, back_ref, gz_ref[...], bz_ref[...])
    dots_ref[1] = fold(f * z)
    emit_partial(f, p_ref, x_ref, y_ref)


def fourth_kernel(pin_ref, xl_ref, xr_ref, yb_ref, ya_ref, dinv_ref, z_ref, coef_ref, react_ref,
                  grad_ref, back_ref, gz_ref, bz_ref,
                  im_ref, p_ref, x_ref, y_ref, dots_ref, s_ref):
    image = take_sum(pin_ref, (xl_ref[0], xr_ref[0], yb_ref[0], ya_ref[0]), s_ref)
    dinv = dinv_ref[...]
    im = jnp.where(dinv != 0.0, image, 0.0)
    im_ref[...] = im
    b0 = dinv * im * (1.0 / CENTER)
    f = local_op(b0, coef_ref[...], react_ref[...], grad_ref, back_ref, gz_ref[...], bz_ref[...])
    dots_ref[...] = fold(f * z_ref[...])
    emit_partial(f, p_ref, x_ref, y_ref)


def fifth_kernel(pin_ref, xl_ref, xr_ref, yb_ref, ya_ref, im_ref, dinv_ref, z_ref, d34_ref, d5_ref, coef_ref, react_ref,
                 grad_ref, back_ref, gz_ref, bz_ref,
                 b1_ref, p_ref, x_ref, y_ref, dots_ref, s_ref):
    image = take_sum(pin_ref, (xl_ref[0], xr_ref[0], yb_ref[0], ya_ref[0]), s_ref)
    dinv, im = dinv_ref[...], im_ref[...]
    b0 = dinv * im * (1.0 / CENTER)
    b1 = (1.0 + MIX1) * b0 + GAIN1 * (dinv * (im - image))
    b1_ref[...] = b1
    f = local_op(b1, coef_ref[...], react_ref[...], grad_ref, back_ref, gz_ref[...], bz_ref[...])
    emit_partial(f, p_ref, x_ref, y_ref)
    last = fold(f * ((1.0 + MIX2) * z_ref[...] - (CENTER * GAIN2) * b0))
    both = last + (CENTER * GAIN2 - MIX2) * d5_ref[...]
    lane = lax.broadcasted_iota(jnp.int32, (1, 128), 1)
    dots_ref[...] = jnp.where(
        lane == 0, jnp.sum(d34_ref[0]), jnp.where(lane == 1, jnp.sum(d34_ref[1]), jnp.sum(both)))


def last_kernel(dots_ref, pin_ref, xl_ref, xr_ref, yb_ref, ya_ref, im_ref, dinv_ref, b1_ref, z_ref, r_ref,
                sol_ref, res_ref, dir_ref, s_ref):
    first, curv, quad = dots_ref[0], dots_ref[1], dots_ref[2]
    step = first / curv
    ratio = (first - 2.0 * step * curv + step * step * quad) / first
    image = take_sum(pin_ref, (xl_ref[0], xr_ref[0], yb_ref[0], ya_ref[0]), s_ref)
    im = im_ref[...]
    b2 = sweep2(image, b1_ref[...], im, dinv_ref[...])
    z = z_ref[...]
    shape = (16, 16, COLS)
    sol_ref[...] = (step * z).reshape(shape)
    res_ref[...] = (r_ref[...] - step * im).reshape(shape)
    dir_ref[...] = ((z - step * b2) + ratio * z).reshape(shape)


VM = pl.BlockSpec(memory_space=pltpu.VMEM)
SM = pl.BlockSpec(memory_space=pltpu.SMEM)
BIG = jax.ShapeDtypeStruct((ROWS, COLS), F32)
FACES = jax.ShapeDtypeStruct((2, 16, COLS), F32)
SCRATCH = [pltpu.VMEM((ROWS, COLS), F32)]
PARAMS = pltpu.CompilerParams(vmem_limit_bytes=24 << 20)


def call(kernel, outs, n_in, smem_first=False, scratch=True):
    specs = [VM] * n_in
    if smem_first:
        specs[0] = SM
    return pl.pallas_call(
        kernel, out_shape=outs, in_specs=specs, out_specs=jax.tree.map(lambda _: VM, outs),
        scratch_shapes=SCRATCH if scratch else [], compiler_params=PARAMS)


def per_device(load, conductivity, flags, region, kappa_table):
    k = {name: jnp.asarray(value) for name, value in constants().items()}
    mats = (k["grad"], k["back"], k["grad_z"], k["back_z"])
    n_x, n_y = lax.axis_size("gx"), lax.axis_size("gy")
    up_x = [(i, i + 1) for i in range(n_x - 1)]
    up_y = [(i, i + 1) for i in range(n_y - 1)]
    down_x = [(j, i) for i, j in up_x]
    down_y = [(j, i) for i, j in up_y]

    def exchange(faces_x, faces_y):
        left = lax.ppermute(faces_x[:, 1], "gx", up_x)
        right = lax.ppermute(faces_x[:, 0], "gx", down_x)

        def with_corners(side, row):
            face = faces_y[:, side]
            fields = face.shape[0]
            inner = jnp.zeros((fields, 14, COLS), F32)
            return face + jnp.concatenate([left[:, row:row + 1], inner, right[:, row:row + 1]], axis=1)

        below = lax.ppermute(with_corners(1, 15), "gy", up_y)
        above = lax.ppermute(with_corners(0, 0), "gy", down_y)
        return left, right, below, above

    two = jax.ShapeDtypeStruct((2, 2, 16, COLS), F32)
    coef, react, part_l, part_d, fx, fy = call(first_kernel, (BIG, BIG, BIG, BIG, two, two), 8, True, False)(
        kappa_table, load, conductivity, region, k["sq"], k["sq_z"], k["w_rows"], k["w_z"])
    recv = exchange(fx, fy)
    flags0 = lax.slice_in_dim(flags, 0, 128, axis=2)
    r, dinv, part, fx, fy = call(second_kernel, (BIG, BIG, BIG, FACES, FACES), 13)(
        part_l, part_d, *recv, flags0, coef, react, *mats)
    recv = exchange(fx[None], fy[None])
    a1, part, fx, fy = call(sweep1_kernel, (BIG, BIG, FACES, FACES), 13)(part, *recv, r, dinv, coef, react, *mats)
    recv = exchange(fx[None], fy[None])
    z, part, fx, fy, d34 = call(
        third_kernel, (BIG, BIG, FACES, FACES, jax.ShapeDtypeStruct((2, 8, 128), F32)), 15)(
        part, *recv, r, dinv, a1, load, coef, react, *mats)
    recv = exchange(fx[None], fy[None])
    im, part, fx, fy, d5 = call(fourth_kernel, (BIG, BIG, FACES, FACES, jax.ShapeDtypeStruct((8, 128), F32)), 13)(
        part, *recv, dinv, z, coef, react, *mats)
    recv = exchange(fx[None], fy[None])
    b1, part, fx, fy, dots = call(fifth_kernel, (BIG, BIG, FACES, FACES, jax.ShapeDtypeStruct((1, 128), F32)), 16)(
        part, *recv, im, dinv, z, d34, d5, coef, react, *mats)
    total = lax.all_to_all(jnp.broadcast_to(dots, (n_y, 128)), "gy", 0, 0, tiled=True).sum(0)
    total = lax.all_to_all(jnp.broadcast_to(total, (n_x, 128)), "gx", 0, 0, tiled=True).sum(0)
    recv = exchange(fx[None], fy[None])
    shape = jax.ShapeDtypeStruct((16, 16, COLS), F32)
    return call(last_kernel, (shape, shape, shape), 11, True)(
        total, part, *recv, im, dinv, b1, z, r)


def solution(mesh):
    placed = P("gx", "gy", None)
    return jax.shard_map(
        per_device,
        mesh=mesh,
        in_specs=(placed, placed, placed, placed, P()),
        out_specs=(placed, placed, placed),
        check_vma=False,
    )
```

```python
import jax
import jax.numpy as jnp
import ml_dtypes
import numpy as np
from jax import lax
from jax.experimental import pallas as pl
from jax.experimental.pallas import tpu as pltpu
from jax.sharding import PartitionSpec as P

NREG = 3
CENTER = 24.0
HALF = 23.0
RHO0 = HALF / CENTER
RHO1 = 1.0 / (2.0 * CENTER / HALF - RHO0)
RHO2 = 1.0 / (2.0 * CENTER / HALF - RHO1)
MIX1, GAIN1 = RHO1 * RHO0, 2.0 * RHO1 / HALF
MIX2, GAIN2 = RHO2 * RHO1, 2.0 * RHO2 / HALF

F32 = jnp.float32
BF16 = jnp.bfloat16
ROWS, COLS = 256, 512


def gll_tables():
    nodes = np.array(
        [
            -1.0,
            -0.8717401485096066,
            -0.5917001814331423,
            -0.2092992179024789,
            0.2092992179024789,
            0.5917001814331423,
            0.8717401485096066,
            1.0,
        ]
    )
    prev = np.ones(8)
    now = nodes.copy()
    for degree in range(1, 7):
        prev, now = now, ((2 * degree + 1) * nodes * now - degree * prev) / (degree + 1)
    weights = 2.0 / (56.0 * now**2)
    table = np.zeros((8, 8))
    for a in range(8):
        for b in range(8):
            if a != b:
                table[a, b] = now[a] / (now[b] * (nodes[a] - nodes[b]))
    table[0, 0] = -14.0
    table[7, 7] = 14.0
    return table, weights


def split_np(mat):
    high = mat.astype(ml_dtypes.bfloat16)
    low = (mat - high.astype(np.float64)).astype(ml_dtypes.bfloat16)
    return high, low


def left_pair(mat):
    high, low = split_np(mat)
    return np.stack([np.concatenate([high, high], 1), np.concatenate([low, low], 1)])


def right_pair(mat):
    high, low = split_np(mat)
    both = np.concatenate([high, low], 1)
    return np.concatenate([both, both], 0)


def constants():
    table, weights = gll_tables()
    table = table.astype(np.float32).astype(np.float64)
    weights = weights.astype(np.float32)
    eye8, eye2, eye16 = np.eye(8), np.eye(2), np.eye(16)
    d_x = np.kron(table, eye16)
    d_y = np.kron(eye8, np.kron(eye2, table))
    square = (table * table).astype(np.float32).astype(np.float64)
    q_x = np.kron(square, eye16)
    q_y = np.kron(eye8, np.kron(eye2, square))
    d_z = np.kron(eye16, table)
    q_z = np.kron(eye16, square)
    grad = left_pair(np.concatenate([d_x, d_y], 0))
    back_h, back_l = split_np(np.concatenate([d_x.T, d_y.T], 1))
    back = np.stack([back_h, back_l])
    sq = left_pair(q_x.T + q_y.T)
    grad_z = right_pair(d_z.T)
    back_z = right_pair(d_z)
    sq_z = right_pair(q_z)
    w_xy = (weights[:, None] * weights[None, :]).astype(np.float32)
    w_xy = np.tile(w_xy, (2, 2)).reshape(ROWS, 1)
    w_rows = np.ascontiguousarray(np.broadcast_to(w_xy, (ROWS, 128)))
    w_z = np.tile(weights, COLS // 8).reshape(1, COLS).astype(np.float32)
    return dict(grad=grad, back=back, sq=sq, grad_z=grad_z, back_z=back_z, sq_z=sq_z, w_rows=w_rows, w_z=w_z)


def dot(a, b):
    return lax.dot_general(a, b, (((1,), (0,)), ((), ())), preferred_element_type=F32)


def halves(v):
    high = v.astype(BF16)
    low = (v - high.astype(F32)).astype(BF16)
    return high, low


def mul_z(high, low, mat):
    outs = []
    for k in range(COLS // 128):
        part = slice(128 * k, 128 * (k + 1))
        both = dot(jnp.concatenate([high[:, part], low[:, part]], 1), mat)
        outs.append(both[:, :128] + both[:, 128:])
    return jnp.concatenate(outs, 1)


def local_op(v, coef, react, grad, back, grad_z, back_z):
    high, low = halves(v)
    rows = []
    for e in range(2):
        part = slice(128 * e, 128 * (e + 1))
        pair = jnp.concatenate([high[part], low[part]], 0)
        flux = dot(grad[0], pair) + dot(grad[1], pair)
        c = coef[part]
        f_h, f_l = halves(flux * jnp.concatenate([c, c], 0))
        rows.append(dot(back[0], f_h) + (dot(back[0], f_l) + dot(back[1], f_h)))
    out = jnp.concatenate(rows, 0)
    flux_z = mul_z(high, low, grad_z) * coef
    return out + mul_z(*halves(flux_z), back_z) + react * v


def join_z(f):
    lane = lax.broadcasted_iota(jnp.int32, (1, COLS), 1)
    upper = ((lane % 8) == 7) & (lane != COLS - 1)
    lower = ((lane % 8) == 0) & (lane != 0)
    nxt = pltpu.roll(f, COLS - 1, 1)
    prv = pltpu.roll(f, 1, 1)
    return f + jnp.where(upper, nxt, jnp.where(lower, prv, 0.0))


def emit_partial(f, edge_ref, p_ref, faces):
    p_ref[...] = join_z(f)
    p_ref[112:128, :] = p_ref[112:128, :] + p_ref[128:144, :]
    p_ref[128:144, :] = p_ref[112:128, :]
    x_low, x_high, y_low, y_high = faces
    for x in range(16):
        r = 16 * x
        mid = p_ref[r + 7:r + 8, :] + p_ref[r + 8:r + 9, :]
        p_ref[r + 7:r + 8, :] = mid
        p_ref[r + 8:r + 9, :] = mid
        y_low[x:x + 1, :] = p_ref[r:r + 1, :]
        y_high[x:x + 1, :] = p_ref[r + 15:r + 16, :]
    x_low[...] = jnp.where(edge_ref[0] == 1, 0.0, p_ref[0:16, :])
    x_high[...] = jnp.where(edge_ref[1] == 1, 0.0, p_ref[240:256, :])


def take_sum(p_ref, recv, s_ref):
    left, right, below, above = recv
    s_ref[...] = p_ref[...]
    s_ref[0:16, :] = s_ref[0:16, :] + left
    s_ref[240:256, :] = s_ref[240:256, :] + right
    for x in range(16):
        r = 16 * x
        s_ref[r:r + 1, :] = s_ref[r:r + 1, :] + below[x:x + 1, :]
        s_ref[r + 15:r + 16, :] = s_ref[r + 15:r + 16, :] + above[x:x + 1, :]
    return s_ref[...]


def fold(prod):
    part = prod.reshape(ROWS // 8, 8, COLS).sum(axis=0)
    return part[:, 0:128] + part[:, 128:256] + part[:, 256:384] + part[:, 384:512]


def first_kernel(edge_ref, table_hbm, load_hbm, cond_hbm, flags_hbm, region_hbm, sq_hbm, sqz_hbm, wr_hbm, wz_hbm,
                 coef_ref, react_ref, keep_ref, pl_ref, pd_ref, xl_ref, xh_ref, yl_ref, yh_ref,
                 table_ref, load_ref, cond_ref, flags_ref, region_ref, sq_ref, sqz_ref, wr_ref, wz_ref, sems):
    flags_tile = flags_hbm.at[:, :, pl.ds(0, 128)]
    pairs = ((cond_hbm, cond_ref), (wr_hbm, wr_ref), (wz_hbm, wz_ref), (region_hbm, region_ref), (table_hbm, table_ref),
             (sq_hbm, sq_ref), (sqz_hbm, sqz_ref), (load_hbm, load_ref), (flags_tile, flags_ref))
    copies = [pltpu.make_async_copy(src, dst, sems.at[i]) for i, (src, dst) in enumerate(pairs)]
    for copy in copies:
        copy.start()
    for copy in copies[:5]:
        copy.wait()
    w_row = wr_ref[...]
    w_row = jnp.concatenate([w_row] * 4, axis=1)
    quad_z = wz_ref[...]
    coef = (w_row * quad_z) * cond_ref[...].reshape(ROWS, COLS).astype(F32)
    coef_ref[...] = coef
    elem = lax.broadcasted_iota(jnp.int32, (COLS // 8, COLS), 0)
    lane = lax.broadcasted_iota(jnp.int32, (COLS // 8, COLS), 1)
    spread = (lane // 8 == elem).astype(F32)
    for ex in range(2):
        ids = region_ref[ex]
        kappa = jnp.zeros(ids.shape, F32)
        for k in range(NREG):
            kappa = kappa + jnp.where(ids == k, table_ref[k], 0.0)
        kappa = lax.dot_general(kappa, spread, (((1,), (0,)), ((), ())),
                                precision=lax.Precision.HIGHEST, preferred_element_type=F32)
        for x in range(8):
            for ey in range(2):
                r = (ex * 8 + x) * 16 + ey * 8
                react_ref[r:r + 8, :] = (w_row[r:r + 8] * quad_z) * kappa[ey:ey + 1, :]
    for copy in copies[5:]:
        copy.wait()
    keep_ref[...] = (1 - flags_ref[...].reshape(ROWS, 128)).astype(F32)
    high, low = halves(coef)
    rows = []
    for e in range(2):
        part = slice(128 * e, 128 * (e + 1))
        pair = jnp.concatenate([high[part], low[part]], 0)
        rows.append(dot(sq_ref[0], pair) + dot(sq_ref[1], pair))
    diag = jnp.concatenate(rows, 0) + mul_z(high, low, sqz_ref[...]) + react_ref[...]
    faces = (xl_ref, xh_ref, yl_ref, yh_ref)
    emit_partial(diag, edge_ref, pd_ref, [face.at[1] for face in faces])
    emit_partial(load_ref[...].reshape(ROWS, COLS), edge_ref, pl_ref, [face.at[0] for face in faces])


def second_kernel(edge_ref, pl_ref, pd_ref, xl_ref, xr_ref, yb_ref, ya_ref, keep_ref, coef_ref, react_ref,
                  grad_ref, back_ref, gz_ref, bz_ref,
                  r_ref, dinv_ref, p_ref, lo_x, hi_x, lo_y, hi_y, s_ref):
    diag = take_sum(pd_ref, (xl_ref[1], xr_ref[1], yb_ref[1], ya_ref[1]), s_ref)
    dinv_ref[...] = 1.0 / diag
    keep = keep_ref[...]
    dinv_ref[:, 0:128] = keep * dinv_ref[:, 0:128]
    r = take_sum(pl_ref, (xl_ref[0], xr_ref[0], yb_ref[0], ya_ref[0]), s_ref)
    r_ref[...] = r
    r_ref[:, 0:128] = keep * r_ref[:, 0:128]
    a0 = dinv_ref[...] * r_ref[...] * (1.0 / CENTER)
    f = local_op(a0, coef_ref[...], react_ref[...], grad_ref, back_ref, gz_ref[...], bz_ref[...])
    emit_partial(f, edge_ref, p_ref, (lo_x, hi_x, lo_y, hi_y))


def sweep1_kernel(edge_ref, pin_ref, xl_ref, xr_ref, yb_ref, ya_ref, r_ref, dinv_ref, coef_ref, react_ref,
                  grad_ref, back_ref, gz_ref, bz_ref,
                  a1_ref, p_ref, lo_x, hi_x, lo_y, hi_y, s_ref):
    image = take_sum(pin_ref, (xl_ref[...], xr_ref[...], yb_ref[...], ya_ref[...]), s_ref)
    dinv, r = dinv_ref[...], r_ref[...]
    a0 = dinv * r * (1.0 / CENTER)
    a1 = (1.0 + MIX1) * a0 + GAIN1 * (dinv * (r - image))
    a1_ref[...] = a1
    f = local_op(a1, coef_ref[...], react_ref[...], grad_ref, back_ref, gz_ref[...], bz_ref[...])
    emit_partial(f, edge_ref, p_ref, (lo_x, hi_x, lo_y, hi_y))


def sweep2(image, a1, r, dinv):
    a0 = dinv * r * (1.0 / CENTER)
    return a1 + (MIX2 * (a1 - a0) + GAIN2 * (dinv * (r - image)))


def third_kernel(edge_ref, pin_ref, xl_ref, xr_ref, yb_ref, ya_ref, r_ref, dinv_ref, a1_ref, load_ref, coef_ref, react_ref,
                 grad_ref, back_ref, gz_ref, bz_ref,
                 z_ref, p_ref, lo_x, hi_x, lo_y, hi_y, dots_ref, s_ref):
    image = take_sum(pin_ref, (xl_ref[...], xr_ref[...], yb_ref[...], ya_ref[...]), s_ref)
    z = sweep2(image, a1_ref[...], r_ref[...], dinv_ref[...])
    z_ref[...] = z
    dots_ref[0] = fold(load_ref[...].reshape(ROWS, COLS) * z)
    f = local_op(z, coef_ref[...], react_ref[...], grad_ref, back_ref, gz_ref[...], bz_ref[...])
    dots_ref[1] = fold(f * z)
    emit_partial(f, edge_ref, p_ref, (lo_x, hi_x, lo_y, hi_y))


def fourth_kernel(edge_ref, pin_ref, xl_ref, xr_ref, yb_ref, ya_ref, dinv_ref, z_ref, coef_ref, react_ref,
                  grad_ref, back_ref, gz_ref, bz_ref,
                  im_ref, p_ref, lo_x, hi_x, lo_y, hi_y, dots_ref, s_ref):
    image = take_sum(pin_ref, (xl_ref[...], xr_ref[...], yb_ref[...], ya_ref[...]), s_ref)
    dinv = dinv_ref[...]
    im = jnp.where(dinv != 0.0, image, 0.0)
    im_ref[...] = im
    b0 = dinv * im * (1.0 / CENTER)
    f = local_op(b0, coef_ref[...], react_ref[...], grad_ref, back_ref, gz_ref[...], bz_ref[...])
    dots_ref[...] = fold(f * z_ref[...])
    emit_partial(f, edge_ref, p_ref, (lo_x, hi_x, lo_y, hi_y))


def fifth_kernel(edge_ref, pin_ref, xl_ref, xr_ref, yb_ref, ya_ref, im_ref, dinv_ref, z_ref, d34_ref, d5_ref, coef_ref, react_ref,
                 grad_ref, back_ref, gz_ref, bz_ref,
                 b1_ref, p_ref, lo_x, hi_x, lo_y, hi_y, dots_ref, s_ref):
    image = take_sum(pin_ref, (xl_ref[...], xr_ref[...], yb_ref[...], ya_ref[...]), s_ref)
    dinv, im = dinv_ref[...], im_ref[...]
    b0 = dinv * im * (1.0 / CENTER)
    b1 = (1.0 + MIX1) * b0 + GAIN1 * (dinv * (im - image))
    b1_ref[...] = b1
    f = local_op(b1, coef_ref[...], react_ref[...], grad_ref, back_ref, gz_ref[...], bz_ref[...])
    emit_partial(f, edge_ref, p_ref, (lo_x, hi_x, lo_y, hi_y))
    last = fold(f * ((1.0 + MIX2) * z_ref[...] - (CENTER * GAIN2) * b0))
    both = last + (CENTER * GAIN2 - MIX2) * d5_ref[...]
    lane = lax.broadcasted_iota(jnp.int32, (1, 128), 1)
    sums = jnp.where(
        lane == 0, jnp.sum(d34_ref[0]), jnp.where(lane == 1, jnp.sum(d34_ref[1]), jnp.sum(both)))
    dots_ref[...] = jnp.broadcast_to(sums, dots_ref.shape)


def last_kernel(dots_ref, pin_ref, xl_ref, xr_ref, yb_ref, ya_ref, im_ref, dinv_ref, b1_ref, z_ref, r_ref,
                sol_ref, res_ref, dir_ref, s_ref):
    first, curv, quad = dots_ref[0], dots_ref[1], dots_ref[2]
    step = first / curv
    ratio = (first - 2.0 * step * curv + step * step * quad) / first
    image = take_sum(pin_ref, (xl_ref[...], xr_ref[...], yb_ref[...], ya_ref[...]), s_ref)
    im = im_ref[...]
    b2 = sweep2(image, b1_ref[...], im, dinv_ref[...])
    z = z_ref[...]
    shape = (16, 16, COLS)
    sol_ref[...] = (step * z).reshape(shape)
    res_ref[...] = (r_ref[...] - step * im).reshape(shape)
    dir_ref[...] = ((z - step * b2) + ratio * z).reshape(shape)


VM = pl.BlockSpec(memory_space=pltpu.VMEM)
SM = pl.BlockSpec(memory_space=pltpu.SMEM)
HB = pl.BlockSpec(memory_space=pl.ANY)
BIG = jax.ShapeDtypeStruct((ROWS, COLS), F32)
FACE = jax.ShapeDtypeStruct((16, COLS), F32)
PART = (BIG, FACE, FACE, FACE, FACE)
PARAMS = pltpu.CompilerParams(vmem_limit_bytes=24 << 20)


def call(kernel, outs, specs, scratch):
    return pl.pallas_call(
        kernel, out_shape=outs, in_specs=specs, out_specs=jax.tree.map(lambda _: VM, outs),
        scratch_shapes=scratch, compiler_params=PARAMS)


def step_call(kernel, outs, n_in):
    return call(kernel, outs, [SM] + [VM] * n_in, [pltpu.VMEM((ROWS, COLS), F32)])


def per_device(load, conductivity, flags, region, kappa_table):
    k = {name: jnp.asarray(value) for name, value in constants().items()}
    mats = (k["grad"], k["back"], k["grad_z"], k["back_z"])
    n_x, n_y = lax.axis_size("gx"), lax.axis_size("gy")
    at_x, at_y = lax.axis_index("gx"), lax.axis_index("gy")
    edge = jnp.stack([at_x == 0, at_x == n_x - 1, at_y == 0, at_y == n_y - 1]).astype(jnp.int32)
    up_x = [(i, (i + 1) % n_x) for i in range(n_x)]
    up_y = [(i, (i + 1) % n_y) for i in range(n_y)]
    down_x = [(j, i) for i, j in up_x]
    down_y = [(j, i) for i, j in up_y]

    def exchange(faces):
        x_low, x_high, y_low, y_high = faces
        left = lax.ppermute(x_high, "gx", up_x)
        right = lax.ppermute(x_low, "gx", down_x)

        def with_corners(face, row, last):
            inner = jnp.zeros(face.shape[:-2] + (14, COLS), F32)
            ends = [left[..., row:row + 1, :], inner, right[..., row:row + 1, :]]
            return jnp.where(last, 0.0, face + jnp.concatenate(ends, axis=-2))

        below = lax.ppermute(with_corners(y_high, 15, at_y == n_y - 1), "gy", up_y)
        above = lax.ppermute(with_corners(y_low, 0, at_y == 0), "gy", down_y)
        return left, right, below, above

    two = jax.ShapeDtypeStruct((2, 16, COLS), F32)
    keep_shape = jax.ShapeDtypeStruct((ROWS, 128), F32)
    inputs = (kappa_table, load, conductivity, flags, region, k["sq"], k["sq_z"], k["w_rows"], k["w_z"])
    buffers = [pltpu.VMEM(v.shape, v.dtype) for v in inputs]
    buffers[0] = pltpu.SMEM(kappa_table.shape, F32)
    buffers[3] = pltpu.VMEM((16, 16, 128), jnp.int32)
    coef, react, keep, part_l, part_d, *faces = call(
        first_kernel, (BIG, BIG, keep_shape, BIG, BIG, two, two, two, two), [SM] + [HB] * len(inputs),
        buffers + [pltpu.SemaphoreType.DMA((len(inputs),))])(edge, *inputs)
    recv = exchange(faces)
    r, dinv, part, *faces = step_call(second_kernel, (BIG, BIG) + PART, 13)(
        edge, part_l, part_d, *recv, keep, coef, react, *mats)
    recv = exchange(faces)
    a1, part, *faces = step_call(sweep1_kernel, (BIG,) + PART, 13)(
        edge, part, *recv, r, dinv, coef, react, *mats)
    recv = exchange(faces)
    d34_shape = jax.ShapeDtypeStruct((2, 8, 128), F32)
    z, part, *faces, d34 = step_call(third_kernel, (BIG,) + PART + (d34_shape,), 15)(
        edge, part, *recv, r, dinv, a1, load, coef, react, *mats)
    recv = exchange(faces)
    d5_shape = jax.ShapeDtypeStruct((8, 128), F32)
    im, part, *faces, d5 = step_call(fourth_kernel, (BIG,) + PART + (d5_shape,), 13)(
        edge, part, *recv, dinv, z, coef, react, *mats)
    recv = exchange(faces)
    dots_shape = jax.ShapeDtypeStruct((n_y, 128), F32)
    b1, part, *faces, dots = step_call(fifth_kernel, (BIG,) + PART + (dots_shape,), 16)(
        edge, part, *recv, im, dinv, z, d34, d5, coef, react, *mats)
    total = lax.all_to_all(dots, "gy", 0, 0, tiled=True).sum(0)
    recv = exchange(faces)
    total = lax.all_to_all(jnp.broadcast_to(total, (n_x, 128)), "gx", 0, 0, tiled=True).sum(0)
    shape = jax.ShapeDtypeStruct((16, 16, COLS), F32)
    return step_call(last_kernel, (shape, shape, shape), 10)(
        total, part, *recv, im, dinv, b1, z, r)


def solution(mesh):
    placed = P("gx", "gy", None)
    return jax.shard_map(
        per_device,
        mesh=mesh,
        in_specs=(placed, placed, placed, placed, P()),
        out_specs=(placed, placed, placed),
        check_vma=False,
    )
```

```python
import jax
import jax.numpy as jnp
import ml_dtypes
import numpy as np
from jax import lax
from jax.experimental import pallas as pl
from jax.experimental.pallas import tpu as pltpu
from jax.sharding import PartitionSpec as P

NREG = 3
CENTER = 24.0
HALF = 23.0
RHO0 = HALF / CENTER
RHO1 = 1.0 / (2.0 * CENTER / HALF - RHO0)
RHO2 = 1.0 / (2.0 * CENTER / HALF - RHO1)
MIX1, GAIN1 = RHO1 * RHO0, 2.0 * RHO1 / HALF
MIX2, GAIN2 = RHO2 * RHO1, 2.0 * RHO2 / HALF

F32 = jnp.float32
BF16 = jnp.bfloat16
ROWS, COLS = 256, 512


def gll_tables():
    nodes = np.array(
        [
            -1.0,
            -0.8717401485096066,
            -0.5917001814331423,
            -0.2092992179024789,
            0.2092992179024789,
            0.5917001814331423,
            0.8717401485096066,
            1.0,
        ]
    )
    prev = np.ones(8)
    now = nodes.copy()
    for degree in range(1, 7):
        prev, now = now, ((2 * degree + 1) * nodes * now - degree * prev) / (degree + 1)
    weights = 2.0 / (56.0 * now**2)
    table = np.zeros((8, 8))
    for a in range(8):
        for b in range(8):
            if a != b:
                table[a, b] = now[a] / (now[b] * (nodes[a] - nodes[b]))
    table[0, 0] = -14.0
    table[7, 7] = 14.0
    return table, weights


def split_np(mat):
    high = mat.astype(ml_dtypes.bfloat16)
    low = (mat - high.astype(np.float64)).astype(ml_dtypes.bfloat16)
    return high, low


def left_pair(mat):
    high, low = split_np(mat)
    return np.stack([np.concatenate([high, high], 1), np.concatenate([low, low], 1)])


def right_pair(mat):
    high, low = split_np(mat)
    both = np.concatenate([high, low], 1)
    return np.concatenate([both, both], 0)


def constants():
    table, weights = gll_tables()
    table = table.astype(np.float32).astype(np.float64)
    weights = weights.astype(np.float32)
    eye8, eye2, eye16 = np.eye(8), np.eye(2), np.eye(16)
    d_x = np.kron(table, eye16)
    d_y = np.kron(eye8, np.kron(eye2, table))
    square = (table * table).astype(np.float32).astype(np.float64)
    q_x = np.kron(square, eye16)
    q_y = np.kron(eye8, np.kron(eye2, square))
    d_z = np.kron(eye16, table)
    q_z = np.kron(eye16, square)
    grad = left_pair(np.concatenate([d_x, d_y], 0))
    back_h, back_l = split_np(np.concatenate([d_x.T, d_y.T], 1))
    back = np.stack([back_h, back_l])
    sq = left_pair(q_x.T + q_y.T)
    grad_z = right_pair(d_z.T)
    back_z = right_pair(d_z)
    sq_z = right_pair(q_z)
    w_xy = (weights[:, None] * weights[None, :]).astype(np.float32)
    w_xy = np.tile(w_xy, (2, 2)).reshape(ROWS, 1)
    w_rows = np.ascontiguousarray(np.broadcast_to(w_xy, (ROWS, 128)))
    w_z = np.tile(weights, COLS // 8).reshape(1, COLS).astype(np.float32)
    return dict(grad=grad, back=back, sq=sq, grad_z=grad_z, back_z=back_z, sq_z=sq_z, w_rows=w_rows, w_z=w_z)


def dot(a, b):
    return lax.dot_general(a, b, (((1,), (0,)), ((), ())), preferred_element_type=F32)


def halves(v):
    high = v.astype(BF16)
    low = (v - high.astype(F32)).astype(BF16)
    return high, low


def mul_z(high, low, mat):
    outs = []
    for k in range(COLS // 128):
        part = slice(128 * k, 128 * (k + 1))
        both = dot(jnp.concatenate([high[:, part], low[:, part]], 1), mat)
        outs.append(both[:, :128] + both[:, 128:])
    return jnp.concatenate(outs, 1)


def local_op(v, coef, react, grad, back, grad_z, back_z):
    high, low = halves(v)
    rows = []
    for e in range(2):
        part = slice(128 * e, 128 * (e + 1))
        pair = jnp.concatenate([high[part], low[part]], 0)
        flux = dot(grad[0], pair) + dot(grad[1], pair)
        c = coef[part]
        f_h, f_l = halves(flux * jnp.concatenate([c, c], 0))
        rows.append(dot(back[0], f_h) + (dot(back[0], f_l) + dot(back[1], f_h)))
    out = jnp.concatenate(rows, 0)
    flux_z = mul_z(high, low, grad_z) * coef
    return out + mul_z(*halves(flux_z), back_z) + react * v


def join_z(f):
    lane = lax.broadcasted_iota(jnp.int32, (1, COLS), 1)
    upper = ((lane % 8) == 7) & (lane != COLS - 1)
    lower = ((lane % 8) == 0) & (lane != 0)
    nxt = pltpu.roll(f, COLS - 1, 1)
    prv = pltpu.roll(f, 1, 1)
    return f + jnp.where(upper, nxt, jnp.where(lower, prv, 0.0))


def emit_partial(f, inside_ref, p_ref, faces):
    p_ref[...] = join_z(f)
    p_ref[112:128, :] = p_ref[112:128, :] + p_ref[128:144, :]
    p_ref[128:144, :] = p_ref[112:128, :]
    x_low, x_high, y_low, y_high = faces
    for x in range(16):
        r = 16 * x
        mid = p_ref[r + 7:r + 8, :] + p_ref[r + 8:r + 9, :]
        p_ref[r + 7:r + 8, :] = mid
        p_ref[r + 8:r + 9, :] = mid
        y_low[x:x + 1, :] = p_ref[r:r + 1, :]
        y_high[x:x + 1, :] = p_ref[r + 15:r + 16, :]
    x_low[...] = inside_ref[0:1, :] * p_ref[0:16, :]
    x_high[...] = inside_ref[1:2, :] * p_ref[240:256, :]


def take_sum(p_ref, recv, s_ref):
    left, right, below, above = recv
    s_ref[...] = p_ref[...]
    s_ref[0:16, :] = s_ref[0:16, :] + left
    s_ref[240:256, :] = s_ref[240:256, :] + right
    for x in range(16):
        r = 16 * x
        s_ref[r:r + 1, :] = s_ref[r:r + 1, :] + below[x:x + 1, :]
        s_ref[r + 15:r + 16, :] = s_ref[r + 15:r + 16, :] + above[x:x + 1, :]
    return s_ref[...]


def fold(prod):
    part = prod.reshape(ROWS // 8, 8, COLS).sum(axis=0)
    return part[:, 0:128] + part[:, 128:256] + part[:, 256:384] + part[:, 384:512]


def first_kernel(inside_ref, table_hbm, load_hbm, cond_hbm, flags_hbm, region_hbm, sq_hbm, sqz_hbm, wr_hbm, wz_hbm,
                 coef_ref, react_ref, keep_ref, pl_ref, pd_ref, xl_ref, xh_ref, yl_ref, yh_ref,
                 table_ref, load_ref, cond_ref, flags_ref, region_ref, sq_ref, sqz_ref, wr_ref, wz_ref, sems):
    flags_tile = flags_hbm.at[:, :, pl.ds(0, 128)]
    pairs = ((cond_hbm, cond_ref), (wr_hbm, wr_ref), (wz_hbm, wz_ref), (region_hbm, region_ref), (table_hbm, table_ref),
             (sq_hbm, sq_ref), (sqz_hbm, sqz_ref), (load_hbm, load_ref), (flags_tile, flags_ref))
    copies = [pltpu.make_async_copy(src, dst, sems.at[i]) for i, (src, dst) in enumerate(pairs)]
    for copy in copies:
        copy.start()
    for copy in copies[:5]:
        copy.wait()
    w_row = wr_ref[...]
    w_row = jnp.concatenate([w_row] * 4, axis=1)
    quad_z = wz_ref[...]
    coef = (w_row * quad_z) * cond_ref[...].reshape(ROWS, COLS).astype(F32)
    coef_ref[...] = coef
    elem = lax.broadcasted_iota(jnp.int32, (COLS // 8, COLS), 0)
    lane = lax.broadcasted_iota(jnp.int32, (COLS // 8, COLS), 1)
    spread = (lane // 8 == elem).astype(F32)
    for ex in range(2):
        ids = region_ref[ex]
        kappa = jnp.zeros(ids.shape, F32)
        for k in range(NREG):
            kappa = kappa + jnp.where(ids == k, table_ref[k], 0.0)
        kappa = lax.dot_general(kappa, spread, (((1,), (0,)), ((), ())),
                                precision=lax.Precision.HIGHEST, preferred_element_type=F32)
        for x in range(8):
            for ey in range(2):
                r = (ex * 8 + x) * 16 + ey * 8
                react_ref[r:r + 8, :] = (w_row[r:r + 8] * quad_z) * kappa[ey:ey + 1, :]
    for copy in copies[5:]:
        copy.wait()
    keep_ref[...] = (1 - flags_ref[...].reshape(ROWS, 128)).astype(F32)
    high, low = halves(coef)
    rows = []
    for e in range(2):
        part = slice(128 * e, 128 * (e + 1))
        pair = jnp.concatenate([high[part], low[part]], 0)
        rows.append(dot(sq_ref[0], pair) + dot(sq_ref[1], pair))
    diag = jnp.concatenate(rows, 0) + mul_z(high, low, sqz_ref[...]) + react_ref[...]
    faces = (xl_ref, xh_ref, yl_ref, yh_ref)
    emit_partial(diag, inside_ref, pd_ref, [face.at[1] for face in faces])
    emit_partial(load_ref[...].reshape(ROWS, COLS), inside_ref, pl_ref, [face.at[0] for face in faces])


def second_kernel(inside_ref, pl_ref, pd_ref, xl_ref, xr_ref, yb_ref, ya_ref, keep_ref, coef_ref, react_ref,
                  grad_ref, back_ref, gz_ref, bz_ref,
                  r_ref, dinv_ref, p_ref, lo_x, hi_x, lo_y, hi_y, s_ref):
    diag = take_sum(pd_ref, (xl_ref[1], xr_ref[1], yb_ref[1], ya_ref[1]), s_ref)
    dinv_ref[...] = 1.0 / diag
    keep = keep_ref[...]
    dinv_ref[:, 0:128] = keep * dinv_ref[:, 0:128]
    r = take_sum(pl_ref, (xl_ref[0], xr_ref[0], yb_ref[0], ya_ref[0]), s_ref)
    r_ref[...] = r
    r_ref[:, 0:128] = keep * r_ref[:, 0:128]
    a0 = dinv_ref[...] * r_ref[...] * (1.0 / CENTER)
    f = local_op(a0, coef_ref[...], react_ref[...], grad_ref, back_ref, gz_ref[...], bz_ref[...])
    emit_partial(f, inside_ref, p_ref, (lo_x, hi_x, lo_y, hi_y))


def sweep1_kernel(inside_ref, pin_ref, xl_ref, xr_ref, yb_ref, ya_ref, r_ref, dinv_ref, coef_ref, react_ref,
                  grad_ref, back_ref, gz_ref, bz_ref,
                  a1_ref, p_ref, lo_x, hi_x, lo_y, hi_y, s_ref):
    image = take_sum(pin_ref, (xl_ref[...], xr_ref[...], yb_ref[...], ya_ref[...]), s_ref)
    dinv, r = dinv_ref[...], r_ref[...]
    a0 = dinv * r * (1.0 / CENTER)
    a1 = (1.0 + MIX1) * a0 + GAIN1 * (dinv * (r - image))
    a1_ref[...] = a1
    f = local_op(a1, coef_ref[...], react_ref[...], grad_ref, back_ref, gz_ref[...], bz_ref[...])
    emit_partial(f, inside_ref, p_ref, (lo_x, hi_x, lo_y, hi_y))


def sweep2(image, a1, r, dinv):
    a0 = dinv * r * (1.0 / CENTER)
    return a1 + (MIX2 * (a1 - a0) + GAIN2 * (dinv * (r - image)))


def third_kernel(inside_ref, pin_ref, xl_ref, xr_ref, yb_ref, ya_ref, r_ref, dinv_ref, a1_ref, load_ref, coef_ref, react_ref,
                 grad_ref, back_ref, gz_ref, bz_ref,
                 z_ref, p_ref, lo_x, hi_x, lo_y, hi_y, dots_ref, s_ref):
    image = take_sum(pin_ref, (xl_ref[...], xr_ref[...], yb_ref[...], ya_ref[...]), s_ref)
    z = sweep2(image, a1_ref[...], r_ref[...], dinv_ref[...])
    z_ref[...] = z
    dots_ref[0] = fold(load_ref[...].reshape(ROWS, COLS) * z)
    f = local_op(z, coef_ref[...], react_ref[...], grad_ref, back_ref, gz_ref[...], bz_ref[...])
    dots_ref[1] = fold(f * z)
    emit_partial(f, inside_ref, p_ref, (lo_x, hi_x, lo_y, hi_y))


def fourth_kernel(inside_ref, pin_ref, xl_ref, xr_ref, yb_ref, ya_ref, dinv_ref, z_ref, coef_ref, react_ref,
                  grad_ref, back_ref, gz_ref, bz_ref,
                  im_ref, p_ref, lo_x, hi_x, lo_y, hi_y, dots_ref, s_ref):
    image = take_sum(pin_ref, (xl_ref[...], xr_ref[...], yb_ref[...], ya_ref[...]), s_ref)
    dinv = dinv_ref[...]
    im = jnp.where(dinv != 0.0, image, 0.0)
    im_ref[...] = im
    b0 = dinv * im * (1.0 / CENTER)
    f = local_op(b0, coef_ref[...], react_ref[...], grad_ref, back_ref, gz_ref[...], bz_ref[...])
    dots_ref[...] = fold(f * z_ref[...])
    emit_partial(f, inside_ref, p_ref, (lo_x, hi_x, lo_y, hi_y))


def fifth_kernel(inside_ref, pin_ref, xl_ref, xr_ref, yb_ref, ya_ref, im_ref, dinv_ref, z_ref, d34_ref, d5_ref, coef_ref, react_ref,
                 grad_ref, back_ref, gz_ref, bz_ref,
                 b1_ref, p_ref, lo_x, hi_x, lo_y, hi_y, dots_ref, s_ref):
    image = take_sum(pin_ref, (xl_ref[...], xr_ref[...], yb_ref[...], ya_ref[...]), s_ref)
    dinv, im = dinv_ref[...], im_ref[...]
    b0 = dinv * im * (1.0 / CENTER)
    b1 = (1.0 + MIX1) * b0 + GAIN1 * (dinv * (im - image))
    b1_ref[...] = b1
    f = local_op(b1, coef_ref[...], react_ref[...], grad_ref, back_ref, gz_ref[...], bz_ref[...])
    emit_partial(f, inside_ref, p_ref, (lo_x, hi_x, lo_y, hi_y))
    last = fold(f * ((1.0 + MIX2) * z_ref[...] - (CENTER * GAIN2) * b0))
    both = last + (CENTER * GAIN2 - MIX2) * d5_ref[...]
    lane = lax.broadcasted_iota(jnp.int32, (1, 128), 1)
    sums = jnp.where(
        lane == 0, jnp.sum(d34_ref[0]), jnp.where(lane == 1, jnp.sum(d34_ref[1]), jnp.sum(both)))
    dots_ref[...] = jnp.broadcast_to(sums, dots_ref.shape)


def last_kernel(dots_ref, pin_ref, xl_ref, xr_ref, yb_ref, ya_ref, im_ref, dinv_ref, b1_ref, z_ref, r_ref,
                sol_ref, res_ref, dir_ref, s_ref):
    first, curv, quad = dots_ref[0], dots_ref[1], dots_ref[2]
    step = first / curv
    ratio = (first - 2.0 * step * curv + step * step * quad) / first
    image = take_sum(pin_ref, (xl_ref[...], xr_ref[...], yb_ref[...], ya_ref[...]), s_ref)
    im = im_ref[...]
    b2 = sweep2(image, b1_ref[...], im, dinv_ref[...])
    z = z_ref[...]
    shape = (16, 16, COLS)
    sol_ref[...] = (step * z).reshape(shape)
    res_ref[...] = (r_ref[...] - step * im).reshape(shape)
    dir_ref[...] = ((z - step * b2) + ratio * z).reshape(shape)


VM = pl.BlockSpec(memory_space=pltpu.VMEM)
SM = pl.BlockSpec(memory_space=pltpu.SMEM)
HB = pl.BlockSpec(memory_space=pl.ANY)
BIG = jax.ShapeDtypeStruct((ROWS, COLS), F32)
FACE = jax.ShapeDtypeStruct((16, COLS), F32)
PART = (BIG, FACE, FACE, FACE, FACE)
PARAMS = pltpu.CompilerParams(vmem_limit_bytes=24 << 20)


def call(kernel, outs, specs, scratch):
    return pl.pallas_call(
        kernel, out_shape=outs, in_specs=specs, out_specs=jax.tree.map(lambda _: VM, outs),
        scratch_shapes=scratch, compiler_params=PARAMS)


def step_call(kernel, outs, n_in, first=VM):
    return call(kernel, outs, [first] + [VM] * n_in, [pltpu.VMEM((ROWS, COLS), F32)])


def per_device(load, conductivity, flags, region, kappa_table):
    k = {name: jnp.asarray(value) for name, value in constants().items()}
    mats = (k["grad"], k["back"], k["grad_z"], k["back_z"])
    n_x, n_y = lax.axis_size("gx"), lax.axis_size("gy")
    at_x, at_y = lax.axis_index("gx"), lax.axis_index("gy")
    inside = jnp.stack([at_x != 0, at_x != n_x - 1]).astype(F32)
    inside = jnp.broadcast_to(inside[:, None], (2, COLS))
    up_x = [(i, (i + 1) % n_x) for i in range(n_x)]
    up_y = [(i, (i + 1) % n_y) for i in range(n_y)]
    down_x = [(j, i) for i, j in up_x]
    down_y = [(j, i) for i, j in up_y]

    def exchange(faces):
        x_low, x_high, y_low, y_high = faces
        left = lax.ppermute(x_high, "gx", up_x)
        right = lax.ppermute(x_low, "gx", down_x)

        def with_corners(face, row, last):
            inner = jnp.zeros(face.shape[:-2] + (14, COLS), F32)
            ends = [left[..., row:row + 1, :], inner, right[..., row:row + 1, :]]
            return jnp.where(last, 0.0, face + jnp.concatenate(ends, axis=-2))

        below = lax.ppermute(with_corners(y_high, 15, at_y == n_y - 1), "gy", up_y)
        above = lax.ppermute(with_corners(y_low, 0, at_y == 0), "gy", down_y)
        return left, right, below, above

    two = jax.ShapeDtypeStruct((2, 16, COLS), F32)
    keep_shape = jax.ShapeDtypeStruct((ROWS, 128), F32)
    inputs = (kappa_table, load, conductivity, flags, region, k["sq"], k["sq_z"], k["w_rows"], k["w_z"])
    inputs = tuple(pltpu.with_memory_space_constraint(v, pltpu.HBM) for v in inputs)
    buffers = [pltpu.VMEM(v.shape, v.dtype) for v in inputs]
    buffers[0] = pltpu.SMEM(kappa_table.shape, F32)
    buffers[3] = pltpu.VMEM((16, 16, 128), jnp.int32)
    coef, react, keep, part_l, part_d, *faces = call(
        first_kernel, (BIG, BIG, keep_shape, BIG, BIG, two, two, two, two), [VM] + [HB] * len(inputs),
        buffers + [pltpu.SemaphoreType.DMA((len(inputs),))])(inside, *inputs)
    recv = exchange(faces)
    r, dinv, part, *faces = step_call(second_kernel, (BIG, BIG) + PART, 13)(
        inside, part_l, part_d, *recv, keep, coef, react, *mats)
    recv = exchange(faces)
    a1, part, *faces = step_call(sweep1_kernel, (BIG,) + PART, 13)(
        inside, part, *recv, r, dinv, coef, react, *mats)
    recv = exchange(faces)
    d34_shape = jax.ShapeDtypeStruct((2, 8, 128), F32)
    z, part, *faces, d34 = step_call(third_kernel, (BIG,) + PART + (d34_shape,), 15)(
        inside, part, *recv, r, dinv, a1, load, coef, react, *mats)
    recv = exchange(faces)
    d5_shape = jax.ShapeDtypeStruct((8, 128), F32)
    im, part, *faces, d5 = step_call(fourth_kernel, (BIG,) + PART + (d5_shape,), 13)(
        inside, part, *recv, dinv, z, coef, react, *mats)
    recv = exchange(faces)
    dots_shape = jax.ShapeDtypeStruct((n_y, 128), F32)
    b1, part, *faces, dots = step_call(fifth_kernel, (BIG,) + PART + (dots_shape,), 16)(
        inside, part, *recv, im, dinv, z, d34, d5, coef, react, *mats)
    total = lax.all_to_all(dots, "gy", 0, 0, tiled=True).sum(0)
    recv = exchange(faces)
    total = lax.all_to_all(jnp.broadcast_to(total, (n_x, 128)), "gx", 0, 0, tiled=True).sum(0)
    shape = jax.ShapeDtypeStruct((16, 16, COLS), F32)
    return step_call(last_kernel, (shape, shape, shape), 10, SM)(
        total, part, *recv, im, dinv, b1, z, r)


def solution(mesh):
    placed = P("gx", "gy", None)
    return jax.shard_map(
        per_device,
        mesh=mesh,
        in_specs=(placed, placed, placed, placed, P()),
        out_specs=(placed, placed, placed),
        check_vma=False,
    )
```

```python
import jax
import jax.numpy as jnp
import ml_dtypes
import numpy as np
from jax import lax
from jax.experimental import pallas as pl
from jax.experimental.pallas import tpu as pltpu
from jax.sharding import PartitionSpec as P

NREG = 3
CENTER = 24.0
HALF = 23.0
RHO0 = HALF / CENTER
RHO1 = 1.0 / (2.0 * CENTER / HALF - RHO0)
RHO2 = 1.0 / (2.0 * CENTER / HALF - RHO1)
MIX1, GAIN1 = RHO1 * RHO0, 2.0 * RHO1 / HALF
MIX2, GAIN2 = RHO2 * RHO1, 2.0 * RHO2 / HALF

F32 = jnp.float32
BF16 = jnp.bfloat16
ROWS, COLS = 256, 512


def gll_tables():
    nodes = np.array(
        [
            -1.0,
            -0.8717401485096066,
            -0.5917001814331423,
            -0.2092992179024789,
            0.2092992179024789,
            0.5917001814331423,
            0.8717401485096066,
            1.0,
        ]
    )
    prev = np.ones(8)
    now = nodes.copy()
    for degree in range(1, 7):
        prev, now = now, ((2 * degree + 1) * nodes * now - degree * prev) / (degree + 1)
    weights = 2.0 / (56.0 * now**2)
    table = np.zeros((8, 8))
    for a in range(8):
        for b in range(8):
            if a != b:
                table[a, b] = now[a] / (now[b] * (nodes[a] - nodes[b]))
    table[0, 0] = -14.0
    table[7, 7] = 14.0
    return table, weights


def split_np(mat):
    high = mat.astype(ml_dtypes.bfloat16)
    low = (mat - high.astype(np.float64)).astype(ml_dtypes.bfloat16)
    return high, low


def left_pair(mat):
    high, low = split_np(mat)
    return np.stack([np.concatenate([high, high], 1), np.concatenate([low, low], 1)])


def right_pair(mat):
    high, low = split_np(mat)
    both = np.concatenate([high, low], 1)
    return np.concatenate([both, both], 0)


def constants():
    table, weights = gll_tables()
    table = table.astype(np.float32).astype(np.float64)
    weights = weights.astype(np.float32)
    eye8, eye2, eye16 = np.eye(8), np.eye(2), np.eye(16)
    d_x = np.kron(table, eye16)
    d_y = np.kron(eye8, np.kron(eye2, table))
    square = (table * table).astype(np.float32).astype(np.float64)
    q_x = np.kron(square, eye16)
    q_y = np.kron(eye8, np.kron(eye2, square))
    d_z = np.kron(eye16, table)
    q_z = np.kron(eye16, square)
    grad = left_pair(np.concatenate([d_x, d_y], 0))
    back_h, back_l = split_np(np.concatenate([d_x.T, d_y.T], 1))
    back = np.stack([back_h, back_l])
    sq = left_pair(q_x.T + q_y.T)
    grad_z = right_pair(d_z.T)
    back_z = right_pair(d_z)
    sq_z = right_pair(q_z)
    lines = np.zeros((8, 64))
    for face in range(4):
        lines[2 * face, 16 * face:16 * face + 8] = table[:, 0]
        lines[2 * face + 1, 16 * face + 8:16 * face + 16] = table[:, 7]
    grad_f = left_pair(np.kron(np.eye(8), table))
    back_f = left_pair(lines)
    w_xy = (weights[:, None] * weights[None, :]).astype(np.float32)
    w_xy = np.tile(w_xy, (2, 2)).reshape(ROWS, 1)
    w_rows = np.ascontiguousarray(np.broadcast_to(w_xy, (ROWS, 128)))
    w_z = np.tile(weights, COLS // 8).reshape(1, COLS).astype(np.float32)
    return dict(grad=grad, back=back, sq=sq, grad_z=grad_z, back_z=back_z, grad_f=grad_f, back_f=back_f, sq_z=sq_z, w_rows=w_rows, w_z=w_z)


def dot(a, b):
    return lax.dot_general(a, b, (((1,), (0,)), ((), ())), preferred_element_type=F32)


def halves(v):
    high = v.astype(BF16)
    low = (v - high.astype(F32)).astype(BF16)
    return high, low


def mul_z(high, low, mat):
    outs = []
    for k in range(COLS // 128):
        part = slice(128 * k, 128 * (k + 1))
        both = dot(jnp.concatenate([high[:, part], low[:, part]], 1), mat)
        outs.append(both[:, :128] + both[:, 128:])
    return jnp.concatenate(outs, 1)


def local_op(v, coef, react, grad, back, grad_z, back_z):
    high, low = halves(v)
    rows = []
    for e in range(2):
        part = slice(128 * e, 128 * (e + 1))
        pair = jnp.concatenate([high[part], low[part]], 0)
        flux = dot(grad[0], pair) + dot(grad[1], pair)
        c = coef[part]
        f_h, f_l = halves(flux * jnp.concatenate([c, c], 0))
        rows.append(dot(back[0], f_h) + (dot(back[0], f_l) + dot(back[1], f_h)))
    out = jnp.concatenate(rows, 0)
    flux_z = mul_z(high, low, grad_z) * coef
    return out + mul_z(*halves(flux_z), back_z) + react * v


def join_z(f):
    lane = lax.broadcasted_iota(jnp.int32, (1, COLS), 1)
    upper = ((lane % 8) == 7) & (lane != COLS - 1)
    lower = ((lane % 8) == 0) & (lane != 0)
    nxt = pltpu.roll(f, COLS - 1, 1)
    prv = pltpu.roll(f, 1, 1)
    return f + jnp.where(upper, nxt, jnp.where(lower, prv, 0.0))


def corner_lines(v_ref, cf, cz, rz, fv_ref, grad_f, back_f, grad_z, back_z):
    for x in range(16):
        r = 16 * x
        fv_ref[x:x + 1, :] = v_ref[r + 15:r + 16, :]
        fv_ref[16 + x:17 + x, :] = v_ref[r:r + 1, :]
    fv_ref[32:48, :] = v_ref[240:256, :]
    fv_ref[48:64, :] = v_ref[0:16, :]
    pair = jnp.concatenate(halves(fv_ref[...]), 0)
    flux = (dot(grad_f[0], pair) + dot(grad_f[1], pair)) * cf
    pair = jnp.concatenate(halves(flux), 0)
    ends = dot(back_f[0], pair) + dot(back_f[1], pair)
    for row, r in enumerate((255, 15, 240, 0, 255, 15, 240, 0)):
        fv_ref[row:row + 1, :] = v_ref[r:r + 1, :]
    at = fv_ref[0:8, :]
    flux_z = mul_z(*halves(at), grad_z) * cz
    return join_z(jnp.concatenate([ends, mul_z(*halves(flux_z), back_z) + rz * at], 0))


def join_rows(f, p_ref):
    p_ref[...] = join_z(f)
    p_ref[112:128, :] = p_ref[112:128, :] + p_ref[128:144, :]
    p_ref[128:144, :] = p_ref[112:128, :]
    for x in range(16):
        r = 16 * x
        mid = p_ref[r + 7:r + 8, :] + p_ref[r + 8:r + 9, :]
        p_ref[r + 7:r + 8, :] = mid
        p_ref[r + 8:r + 9, :] = mid


def put_y(p_ref, low, high, base):
    for x in range(16):
        r = 16 * x
        low[base + x:base + x + 1, :] = p_ref[r:r + 1, :]
        high[base + x:base + x + 1, :] = p_ref[r + 15:r + 16, :]


def add_row(ref, row, line):
    ref[row:row + 1, :] = ref[row:row + 1, :] + line


def emit_partial(f, lines, ctl_ref, p_ref, faces, st_ref):
    even, odd, low_y, high_y = faces
    join_rows(f, p_ref)
    st_ref[0:16, :] = p_ref[0:16, :]
    st_ref[16:32, :] = p_ref[240:256, :]
    put_y(p_ref, low_y, high_y, 0)
    ln = [lines[i:i + 1] for i in range(12)]
    add_row(st_ref, 15, ln[0])
    add_row(st_ref, 31, ln[1])
    add_row(st_ref, 0, ln[2])
    add_row(st_ref, 16, ln[3])
    add_row(low_y, 15, ln[4])
    add_row(high_y, 15, ln[5])
    add_row(low_y, 0, ln[6])
    add_row(high_y, 0, ln[7])
    for i, r in enumerate((255, 15, 240, 0)):
        add_row(p_ref, r, ln[8 + i])
    is_odd = ctl_ref[0:1, :] > 0.5
    low, high = st_ref[0:16, :], st_ref[16:32, :]
    even[...] = jnp.where(is_odd, low, high)
    odd[...] = jnp.where(is_odd, high, low)
    low_y[...] = ctl_ref[1:2, :] * low_y[...]
    high_y[...] = ctl_ref[2:3, :] * high_y[...]


def pick(ctl_ref, even, odd):
    is_odd = ctl_ref[0:1, :] > 0.5
    return jnp.where(is_odd, even, odd), jnp.where(is_odd, odd, even)


def take_sum(p_ref, recv, s_ref):
    left, right, below, above = recv
    s_ref[...] = p_ref[...]
    s_ref[0:16, :] = s_ref[0:16, :] + left
    s_ref[240:256, :] = s_ref[240:256, :] + right
    for x in range(16):
        r = 16 * x
        s_ref[r:r + 1, :] = s_ref[r:r + 1, :] + below[x:x + 1, :]
        s_ref[r + 15:r + 16, :] = s_ref[r + 15:r + 16, :] + above[x:x + 1, :]
    return s_ref[...]


def fold(prod):
    part = prod.reshape(ROWS // 8, 8, COLS).sum(axis=0)
    return part[:, 0:128] + part[:, 128:256] + part[:, 256:384] + part[:, 384:512]


def first_kernel(ctl_ref, table_hbm, load_hbm, cond_hbm, flags_hbm, region_hbm, sq_hbm, sqz_hbm, wr_hbm, wz_hbm,
                 coef_ref, react_ref, keep_ref, pl_ref, pd_ref, even_ref, odd_ref, yl_ref, yh_ref,
                 table_ref, load_ref, cond_ref, flags_ref, region_ref, sq_ref, sqz_ref, wr_ref, wz_ref, sems, st_ref):
    flags_tile = flags_hbm.at[:, :, pl.ds(0, 128)]
    pairs = ((cond_hbm, cond_ref), (wr_hbm, wr_ref), (wz_hbm, wz_ref), (region_hbm, region_ref), (table_hbm, table_ref),
             (sq_hbm, sq_ref), (sqz_hbm, sqz_ref), (load_hbm, load_ref), (flags_tile, flags_ref))
    copies = [pltpu.make_async_copy(src, dst, sems.at[i]) for i, (src, dst) in enumerate(pairs)]
    for copy in copies:
        copy.start()
    for copy in copies[:5]:
        copy.wait()
    w_row = wr_ref[...]
    w_row = jnp.concatenate([w_row] * 4, axis=1)
    quad_z = wz_ref[...]
    coef = (w_row * quad_z) * cond_ref[...].reshape(ROWS, COLS).astype(F32)
    coef_ref[...] = coef
    elem = lax.broadcasted_iota(jnp.int32, (COLS // 8, COLS), 0)
    lane = lax.broadcasted_iota(jnp.int32, (COLS // 8, COLS), 1)
    spread = (lane // 8 == elem).astype(F32)
    for ex in range(2):
        ids = region_ref[ex]
        kappa = jnp.zeros(ids.shape, F32)
        for k in range(NREG):
            kappa = kappa + jnp.where(ids == k, table_ref[k], 0.0)
        kappa = lax.dot_general(kappa, spread, (((1,), (0,)), ((), ())),
                                precision=lax.Precision.HIGHEST, preferred_element_type=F32)
        for x in range(8):
            for ey in range(2):
                r = (ex * 8 + x) * 16 + ey * 8
                react_ref[r:r + 8, :] = (w_row[r:r + 8] * quad_z) * kappa[ey:ey + 1, :]
    for copy in copies[5:]:
        copy.wait()
    keep_ref[...] = (1 - flags_ref[...].reshape(ROWS, 128)).astype(F32)
    high, low = halves(coef)
    rows = []
    for e in range(2):
        part = slice(128 * e, 128 * (e + 1))
        pair = jnp.concatenate([high[part], low[part]], 0)
        rows.append(dot(sq_ref[0], pair) + dot(sq_ref[1], pair))
    diag = jnp.concatenate(rows, 0) + mul_z(high, low, sqz_ref[...]) + react_ref[...]
    join_rows(load_ref[...].reshape(ROWS, COLS), pl_ref)
    join_rows(diag, pd_ref)
    for i, src in enumerate((pl_ref, pd_ref, coef_ref)):
        st_ref[0, 16 * i:16 * i + 16, :] = src[0:16, :]
        st_ref[1, 16 * i:16 * i + 16, :] = src[240:256, :]
        put_y(src, yl_ref, yh_ref, 16 * i)
    zeros = jnp.zeros((8, COLS), F32)
    for side, r in enumerate((0, 240)):
        st_ref[side, 48:56, :] = zeros
        st_ref[side, 48:49, :] = react_ref[r:r + 1, :]
        st_ref[side, 49:50, :] = react_ref[r + 15:r + 16, :]
    yl_ref[48:56, :] = zeros
    yh_ref[48:56, :] = zeros
    is_odd = ctl_ref[0:1, :] > 0.5
    even_ref[...] = jnp.where(is_odd, st_ref[0], st_ref[1])
    odd_ref[...] = jnp.where(is_odd, st_ref[1], st_ref[0])


def corner_kernel(ctl_ref, even_ref, odd_ref, lin_ref, hin_ref, low_ref, high_ref, x_ref):
    x_ref[0], x_ref[1] = pick(ctl_ref, even_ref[...], odd_ref[...])
    for src, out, row in ((lin_ref, low_ref, 0), (hin_ref, high_ref, 15)):
        out[...] = src[...]
        for base in (0, 16):
            add_row(out, base, x_ref[0, base + row:base + row + 1, :])
            add_row(out, base + 15, x_ref[1, base + row:base + row + 1, :])
        line = 48 if row == 0 else 49
        out[48:49, :] = x_ref[0, 32 + row:33 + row, :]
        out[49:50, :] = x_ref[1, 32 + row:33 + row, :]
        out[50:51, :] = x_ref[0, line:line + 1, :]
        out[51:52, :] = x_ref[1, line:line + 1, :]
    low_ref[...] = ctl_ref[1:2, :] * low_ref[...]
    high_ref[...] = ctl_ref[2:3, :] * high_ref[...]


def second_kernel(ctl_ref, pl_ref, pd_ref, xe_ref, xo_ref, yb_ref, ya_ref, keep_ref, coef_ref, react_ref,
                  grad_ref, back_ref, gz_ref, bz_ref, gf_ref, bf_ref,
                  r_ref, dinv_ref, cf_ref, cz_ref, rz_ref, p_ref, even, odd, low_y, high_y, s_ref, fv_ref, st_ref):
    left, right = pick(ctl_ref, xe_ref[...], xo_ref[...])
    below, above = yb_ref[...], ya_ref[...]
    diag = take_sum(pd_ref, (left[16:32], right[16:32], below[16:32], above[16:32]), s_ref)
    dinv_ref[...] = 1.0 / diag
    keep = keep_ref[...]
    dinv_ref[:, 0:128] = keep * dinv_ref[:, 0:128]
    r = take_sum(pl_ref, (left[0:16], right[0:16], below[0:16], above[0:16]), s_ref)
    r_ref[...] = r
    r_ref[:, 0:128] = keep * r_ref[:, 0:128]
    cf_ref[0:16, :] = above[32:48]
    cf_ref[16:32, :] = below[32:48]
    cf_ref[32:48, :] = right[32:48]
    cf_ref[48:64, :] = left[32:48]
    for out, base in ((cz_ref, 48), (rz_ref, 50)):
        out[0:1, :] = above[base + 1:base + 2]
        out[1:2, :] = above[base:base + 1]
        out[2:3, :] = below[base + 1:base + 2]
        out[3:4, :] = below[base:base + 1]
        out[4:8, :] = jnp.zeros((4, COLS), F32)
    a0 = dinv_ref[...] * r_ref[...] * (1.0 / CENTER)
    s_ref[...] = a0
    lines = corner_lines(s_ref, cf_ref[...], cz_ref[...], rz_ref[...], fv_ref, gf_ref, bf_ref, gz_ref[...], bz_ref[...])
    f = local_op(a0, coef_ref[...], react_ref[...], grad_ref, back_ref, gz_ref[...], bz_ref[...])
    emit_partial(f, lines, ctl_ref, p_ref, (even, odd, low_y, high_y), st_ref)


def sweep1_kernel(ctl_ref, pin_ref, xe_ref, xo_ref, yb_ref, ya_ref, r_ref, dinv_ref, coef_ref, react_ref,
                  cf_ref, cz_ref, rz_ref, grad_ref, back_ref, gz_ref, bz_ref, gf_ref, bf_ref,
                  a1_ref, p_ref, even, odd, low_y, high_y, s_ref, fv_ref, st_ref):
    image = take_sum(pin_ref, (*pick(ctl_ref, xe_ref[...], xo_ref[...]), yb_ref[...], ya_ref[...]), s_ref)
    dinv, r = dinv_ref[...], r_ref[...]
    a0 = dinv * r * (1.0 / CENTER)
    a1 = (1.0 + MIX1) * a0 + GAIN1 * (dinv * (r - image))
    a1_ref[...] = a1
    lines = corner_lines(a1_ref, cf_ref[...], cz_ref[...], rz_ref[...], fv_ref, gf_ref, bf_ref, gz_ref[...], bz_ref[...])
    f = local_op(a1, coef_ref[...], react_ref[...], grad_ref, back_ref, gz_ref[...], bz_ref[...])
    emit_partial(f, lines, ctl_ref, p_ref, (even, odd, low_y, high_y), st_ref)


def sweep2(image, a1, r, dinv):
    a0 = dinv * r * (1.0 / CENTER)
    return a1 + (MIX2 * (a1 - a0) + GAIN2 * (dinv * (r - image)))


def third_kernel(ctl_ref, pin_ref, xe_ref, xo_ref, yb_ref, ya_ref, r_ref, dinv_ref, a1_ref, load_ref, coef_ref, react_ref,
                 cf_ref, cz_ref, rz_ref, grad_ref, back_ref, gz_ref, bz_ref, gf_ref, bf_ref,
                 z_ref, p_ref, even, odd, low_y, high_y, dots_ref, s_ref, fv_ref, st_ref):
    image = take_sum(pin_ref, (*pick(ctl_ref, xe_ref[...], xo_ref[...]), yb_ref[...], ya_ref[...]), s_ref)
    z = sweep2(image, a1_ref[...], r_ref[...], dinv_ref[...])
    z_ref[...] = z
    dots_ref[0] = fold(load_ref[...].reshape(ROWS, COLS) * z)
    lines = corner_lines(z_ref, cf_ref[...], cz_ref[...], rz_ref[...], fv_ref, gf_ref, bf_ref, gz_ref[...], bz_ref[...])
    f = local_op(z, coef_ref[...], react_ref[...], grad_ref, back_ref, gz_ref[...], bz_ref[...])
    dots_ref[1] = fold(f * z)
    emit_partial(f, lines, ctl_ref, p_ref, (even, odd, low_y, high_y), st_ref)


def fourth_kernel(ctl_ref, pin_ref, xe_ref, xo_ref, yb_ref, ya_ref, dinv_ref, z_ref, coef_ref, react_ref,
                  cf_ref, cz_ref, rz_ref, grad_ref, back_ref, gz_ref, bz_ref, gf_ref, bf_ref,
                  im_ref, p_ref, even, odd, low_y, high_y, dots_ref, s_ref, fv_ref, st_ref):
    image = take_sum(pin_ref, (*pick(ctl_ref, xe_ref[...], xo_ref[...]), yb_ref[...], ya_ref[...]), s_ref)
    dinv = dinv_ref[...]
    im = jnp.where(dinv != 0.0, image, 0.0)
    im_ref[...] = im
    b0 = dinv * im * (1.0 / CENTER)
    s_ref[...] = b0
    lines = corner_lines(s_ref, cf_ref[...], cz_ref[...], rz_ref[...], fv_ref, gf_ref, bf_ref, gz_ref[...], bz_ref[...])
    f = local_op(b0, coef_ref[...], react_ref[...], grad_ref, back_ref, gz_ref[...], bz_ref[...])
    dots_ref[...] = fold(f * z_ref[...])
    emit_partial(f, lines, ctl_ref, p_ref, (even, odd, low_y, high_y), st_ref)


def fifth_kernel(ctl_ref, pin_ref, xe_ref, xo_ref, yb_ref, ya_ref, im_ref, dinv_ref, z_ref, d34_ref, d5_ref, coef_ref, react_ref,
                 cf_ref, cz_ref, rz_ref, grad_ref, back_ref, gz_ref, bz_ref, gf_ref, bf_ref,
                 b1_ref, p_ref, even, odd, low_y, high_y, dots_ref, s_ref, fv_ref, st_ref):
    image = take_sum(pin_ref, (*pick(ctl_ref, xe_ref[...], xo_ref[...]), yb_ref[...], ya_ref[...]), s_ref)
    dinv, im = dinv_ref[...], im_ref[...]
    b0 = dinv * im * (1.0 / CENTER)
    b1 = (1.0 + MIX1) * b0 + GAIN1 * (dinv * (im - image))
    b1_ref[...] = b1
    lines = corner_lines(b1_ref, cf_ref[...], cz_ref[...], rz_ref[...], fv_ref, gf_ref, bf_ref, gz_ref[...], bz_ref[...])
    f = local_op(b1, coef_ref[...], react_ref[...], grad_ref, back_ref, gz_ref[...], bz_ref[...])
    emit_partial(f, lines, ctl_ref, p_ref, (even, odd, low_y, high_y), st_ref)
    last = fold(f * ((1.0 + MIX2) * z_ref[...] - (CENTER * GAIN2) * b0))
    both = last + (CENTER * GAIN2 - MIX2) * d5_ref[...]
    lane = lax.broadcasted_iota(jnp.int32, (1, 128), 1)
    sums = jnp.where(
        lane == 0, jnp.sum(d34_ref[0]), jnp.where(lane == 1, jnp.sum(d34_ref[1]), jnp.sum(both)))
    dots_ref[...] = jnp.broadcast_to(sums, dots_ref.shape)


def last_kernel(dots_ref, ctl_ref, pin_ref, xe_ref, xo_ref, yb_ref, ya_ref, im_ref, dinv_ref, b1_ref, z_ref, r_ref,
                sol_ref, res_ref, dir_ref, s_ref):
    first, curv, quad = dots_ref[0], dots_ref[1], dots_ref[2]
    step = first / curv
    ratio = (first - 2.0 * step * curv + step * step * quad) / first
    image = take_sum(pin_ref, (*pick(ctl_ref, xe_ref[...], xo_ref[...]), yb_ref[...], ya_ref[...]), s_ref)
    im = im_ref[...]
    b2 = sweep2(image, b1_ref[...], im, dinv_ref[...])
    z = z_ref[...]
    shape = (16, 16, COLS)
    sol_ref[...] = (step * z).reshape(shape)
    res_ref[...] = (r_ref[...] - step * im).reshape(shape)
    dir_ref[...] = ((z - step * b2) + ratio * z).reshape(shape)


VM = pl.BlockSpec(memory_space=pltpu.VMEM)
SM = pl.BlockSpec(memory_space=pltpu.SMEM)
HB = pl.BlockSpec(memory_space=pl.ANY)
BIG = jax.ShapeDtypeStruct((ROWS, COLS), F32)
FACE = jax.ShapeDtypeStruct((16, COLS), F32)
PART = (BIG, FACE, FACE, FACE, FACE)
MESSAGE = jax.ShapeDtypeStruct((56, COLS), F32)
PARAMS = pltpu.CompilerParams(vmem_limit_bytes=24 << 20)


def call(kernel, outs, specs, scratch):
    return pl.pallas_call(
        kernel, out_shape=outs, in_specs=specs, out_specs=jax.tree.map(lambda _: VM, outs),
        scratch_shapes=scratch, compiler_params=PARAMS)


def step_call(kernel, outs, n_in):
    scratch = [pltpu.VMEM((rows, COLS), F32) for rows in (ROWS, 64, 32)]
    return call(kernel, outs, [VM] * (n_in + 1), scratch)


def swaps(first, count):
    pairs = [(i, i + 1) for i in range(first, count - 1, 2)]
    return pairs + [(j, i) for i, j in pairs]


def per_device(load, conductivity, flags, region, kappa_table):
    k = {name: jnp.asarray(value) for name, value in constants().items()}
    mats = (k["grad"], k["back"], k["grad_z"], k["back_z"], k["grad_f"], k["back_f"])
    n_x, n_y = lax.axis_size("gx"), lax.axis_size("gy")
    at_x, at_y = lax.axis_index("gx"), lax.axis_index("gy")
    ctl = jnp.stack([at_x % 2 == 1, at_y != 0, at_y != n_y - 1, at_y < 0]).astype(F32)
    ctl = jnp.broadcast_to(ctl[:, None], (4, COLS))
    up_y = [(i, (i + 1) % n_y) for i in range(n_y)]
    down_y = [(j, i) for i, j in up_y]

    def along_x(even, odd):
        return lax.ppermute(even, "gx", swaps(0, n_x)), lax.ppermute(odd, "gx", swaps(1, n_x))

    def along_y(low, high):
        return lax.ppermute(high, "gy", up_y), lax.ppermute(low, "gy", down_y)

    def exchange(faces):
        even, odd, low_y, high_y = faces
        return (*along_x(even, odd), *along_y(low_y, high_y))

    keep_shape = jax.ShapeDtypeStruct((ROWS, 128), F32)
    inputs = (kappa_table, load, conductivity, flags, region, k["sq"], k["sq_z"], k["w_rows"], k["w_z"])
    inputs = tuple(pltpu.with_memory_space_constraint(v, pltpu.HBM) for v in inputs)
    buffers = [pltpu.VMEM(v.shape, v.dtype) for v in inputs]
    buffers[0] = pltpu.SMEM(kappa_table.shape, F32)
    buffers[3] = pltpu.VMEM((16, 16, 128), jnp.int32)
    buffers += [pltpu.SemaphoreType.DMA((len(inputs),)), pltpu.VMEM((2, 56, COLS), F32)]
    coef, react, keep, part_l, part_d, even, odd, low_y, high_y = call(
        first_kernel, (BIG, BIG, keep_shape, BIG, BIG) + (MESSAGE,) * 4, [VM] + [HB] * len(inputs), buffers)(ctl, *inputs)
    even, odd = along_x(even, odd)
    low_y, high_y = call(corner_kernel, (MESSAGE, MESSAGE), [VM] * 5, [pltpu.VMEM((2, 56, COLS), F32)])(
        ctl, even, odd, low_y, high_y)
    recv = (even, odd, *along_y(low_y, high_y))
    line = jax.ShapeDtypeStruct((8, COLS), F32)
    r, dinv, cf, cz, rz, part, *faces = step_call(
        second_kernel, (BIG, BIG, jax.ShapeDtypeStruct((64, COLS), F32), line, line) + PART, 15)(
        ctl, part_l, part_d, *recv, keep, coef, react, *mats)
    tail = (coef, react, cf, cz, rz, *mats)
    recv = exchange(faces)
    a1, part, *faces = step_call(sweep1_kernel, (BIG,) + PART, 18)(ctl, part, *recv, r, dinv, *tail)
    recv = exchange(faces)
    d34_shape = jax.ShapeDtypeStruct((2, 8, 128), F32)
    z, part, *faces, d34 = step_call(third_kernel, (BIG,) + PART + (d34_shape,), 20)(
        ctl, part, *recv, r, dinv, a1, load, *tail)
    recv = exchange(faces)
    d5_shape = jax.ShapeDtypeStruct((8, 128), F32)
    im, part, *faces, d5 = step_call(fourth_kernel, (BIG,) + PART + (d5_shape,), 18)(
        ctl, part, *recv, dinv, z, *tail)
    recv = exchange(faces)
    dots_shape = jax.ShapeDtypeStruct((n_y, 128), F32)
    b1, part, *faces, dots = step_call(fifth_kernel, (BIG,) + PART + (dots_shape,), 21)(
        ctl, part, *recv, im, dinv, z, d34, d5, *tail)
    total = lax.all_to_all(dots, "gy", 0, 0, tiled=True).sum(0)
    recv = exchange(faces)
    total = lax.all_to_all(jnp.broadcast_to(total, (n_x, 128)), "gx", 0, 0, tiled=True).sum(0)
    shape = jax.ShapeDtypeStruct((16, 16, COLS), F32)
    return call(last_kernel, (shape, shape, shape), [SM] + [VM] * 11, [pltpu.VMEM((ROWS, COLS), F32)])(
        total, ctl, part, *recv, im, dinv, b1, z, r)


def solution(mesh):
    placed = P("gx", "gy", None)
    return jax.shard_map(
        per_device,
        mesh=mesh,
        in_specs=(placed, placed, placed, placed, P()),
        out_specs=(placed, placed, placed),
        check_vma=False,
    )
```

```python
import jax
import jax.numpy as jnp
import ml_dtypes
import numpy as np
from jax import lax
from jax.experimental import pallas as pl
from jax.experimental.pallas import tpu as pltpu
from jax.sharding import PartitionSpec as P

NREG = 3
CENTER = 24.0
HALF = 23.0
RHO0 = HALF / CENTER
RHO1 = 1.0 / (2.0 * CENTER / HALF - RHO0)
RHO2 = 1.0 / (2.0 * CENTER / HALF - RHO1)
MIX1, GAIN1 = RHO1 * RHO0, 2.0 * RHO1 / HALF
MIX2, GAIN2 = RHO2 * RHO1, 2.0 * RHO2 / HALF

F32 = jnp.float32
BF16 = jnp.bfloat16
ROWS, COLS = 256, 512


def gll_tables():
    nodes = np.array(
        [
            -1.0,
            -0.8717401485096066,
            -0.5917001814331423,
            -0.2092992179024789,
            0.2092992179024789,
            0.5917001814331423,
            0.8717401485096066,
            1.0,
        ]
    )
    prev = np.ones(8)
    now = nodes.copy()
    for degree in range(1, 7):
        prev, now = now, ((2 * degree + 1) * nodes * now - degree * prev) / (degree + 1)
    weights = 2.0 / (56.0 * now**2)
    table = np.zeros((8, 8))
    for a in range(8):
        for b in range(8):
            if a != b:
                table[a, b] = now[a] / (now[b] * (nodes[a] - nodes[b]))
    table[0, 0] = -14.0
    table[7, 7] = 14.0
    return table, weights


def split_np(mat):
    high = mat.astype(ml_dtypes.bfloat16)
    low = (mat - high.astype(np.float64)).astype(ml_dtypes.bfloat16)
    return high, low


def left_pair(mat):
    high, low = split_np(mat)
    return np.stack([np.concatenate([high, high], 1), np.concatenate([low, low], 1)])


def right_pair(mat):
    high, low = split_np(mat)
    both = np.concatenate([high, low], 1)
    return np.concatenate([both, both], 0)


def constants():
    table, weights = gll_tables()
    table = table.astype(np.float32).astype(np.float64)
    weights = weights.astype(np.float32)
    eye8, eye2, eye16 = np.eye(8), np.eye(2), np.eye(16)
    d_x = np.kron(table, eye16)
    d_y = np.kron(eye8, np.kron(eye2, table))
    square = (table * table).astype(np.float32).astype(np.float64)
    q_x = np.kron(square, eye16)
    q_y = np.kron(eye8, np.kron(eye2, square))
    d_z = np.kron(eye16, table)
    q_z = np.kron(eye16, square)
    grad = left_pair(np.concatenate([d_x, d_y], 0))
    back_h, back_l = split_np(np.concatenate([d_x.T, d_y.T], 1))
    back = np.stack([back_h, back_l])
    sq = left_pair(q_x.T + q_y.T)
    grad_z = right_pair(d_z.T)
    back_z = right_pair(d_z)
    sq_z = right_pair(q_z)
    lines = np.zeros((8, 64))
    for face in range(4):
        lines[2 * face, 16 * face:16 * face + 8] = table[:, 0]
        lines[2 * face + 1, 16 * face + 8:16 * face + 16] = table[:, 7]
    grad_f = left_pair(np.kron(np.eye(8), table))
    back_f = left_pair(lines)
    w_xy = (weights[:, None] * weights[None, :]).astype(np.float32)
    w_xy = np.tile(w_xy, (2, 2)).reshape(ROWS, 1)
    w_rows = np.ascontiguousarray(np.broadcast_to(w_xy, (ROWS, 128)))
    w_z = np.tile(weights, COLS // 8).reshape(1, COLS).astype(np.float32)
    return dict(grad=grad, back=back, sq=sq, grad_z=grad_z, back_z=back_z, grad_f=grad_f, back_f=back_f, sq_z=sq_z, w_rows=w_rows, w_z=w_z)


def dot(a, b):
    return lax.dot_general(a, b, (((1,), (0,)), ((), ())), preferred_element_type=F32)


def halves(v):
    high = v.astype(BF16)
    low = (v - high.astype(F32)).astype(BF16)
    return high, low


def mul_z(high, low, mat):
    outs = []
    for k in range(COLS // 128):
        part = slice(128 * k, 128 * (k + 1))
        both = dot(jnp.concatenate([high[:, part], low[:, part]], 1), mat)
        outs.append(both[:, :128] + both[:, 128:])
    return jnp.concatenate(outs, 1)


def local_op(v, coef, react, grad, back, grad_z, back_z):
    high, low = halves(v)
    rows = []
    for e in range(2):
        part = slice(128 * e, 128 * (e + 1))
        pair = jnp.concatenate([high[part], low[part]], 0)
        flux = dot(grad[0], pair) + dot(grad[1], pair)
        c = coef[part]
        f_h, f_l = halves(flux * jnp.concatenate([c, c], 0))
        rows.append(dot(back[0], f_h) + (dot(back[0], f_l) + dot(back[1], f_h)))
    out = jnp.concatenate(rows, 0)
    flux_z = mul_z(high, low, grad_z) * coef
    return out + mul_z(*halves(flux_z), back_z) + react * v


def join_z(f):
    lane = lax.broadcasted_iota(jnp.int32, (1, COLS), 1)
    upper = ((lane % 8) == 7) & (lane != COLS - 1)
    lower = ((lane % 8) == 0) & (lane != 0)
    nxt = pltpu.roll(f, COLS - 1, 1)
    prv = pltpu.roll(f, 1, 1)
    return f + jnp.where(upper, nxt, jnp.where(lower, prv, 0.0))


def corner_lines(v_ref, cf, cz, rz, fv_ref, grad_f, back_f, grad_z, back_z):
    for x in range(16):
        r = 16 * x
        fv_ref[x:x + 1, :] = v_ref[r + 15:r + 16, :]
        fv_ref[16 + x:17 + x, :] = v_ref[r:r + 1, :]
    fv_ref[32:48, :] = v_ref[240:256, :]
    fv_ref[48:64, :] = v_ref[0:16, :]
    pair = jnp.concatenate(halves(fv_ref[...]), 0)
    flux = (dot(grad_f[0], pair) + dot(grad_f[1], pair)) * cf
    pair = jnp.concatenate(halves(flux), 0)
    ends = dot(back_f[0], pair) + dot(back_f[1], pair)
    for row, r in enumerate((255, 15, 240, 0, 255, 15, 240, 0)):
        fv_ref[row:row + 1, :] = v_ref[r:r + 1, :]
    at = fv_ref[0:8, :]
    flux_z = mul_z(*halves(at), grad_z) * cz
    return join_z(jnp.concatenate([ends, mul_z(*halves(flux_z), back_z) + rz * at], 0))


def join_rows(f, p_ref):
    p_ref[...] = join_z(f)
    p_ref[112:128, :] = p_ref[112:128, :] + p_ref[128:144, :]
    p_ref[128:144, :] = p_ref[112:128, :]
    for x in range(16):
        r = 16 * x
        mid = p_ref[r + 7:r + 8, :] + p_ref[r + 8:r + 9, :]
        p_ref[r + 7:r + 8, :] = mid
        p_ref[r + 8:r + 9, :] = mid


def put_y(p_ref, low, high, base):
    for x in range(16):
        r = 16 * x
        low[base + x:base + x + 1, :] = p_ref[r:r + 1, :]
        high[base + x:base + x + 1, :] = p_ref[r + 15:r + 16, :]


def add_row(ref, row, line):
    ref[row:row + 1, :] = ref[row:row + 1, :] + line


def emit_partial(f, lines, ctl_ref, p_ref, faces, st_ref):
    even, odd, low_y, high_y = faces
    join_rows(f, p_ref)
    st_ref[0:16, :] = p_ref[0:16, :]
    st_ref[16:32, :] = p_ref[240:256, :]
    put_y(p_ref, low_y, high_y, 0)
    ln = [lines[i:i + 1] for i in range(12)]
    add_row(st_ref, 15, ln[0])
    add_row(st_ref, 31, ln[1])
    add_row(st_ref, 0, ln[2])
    add_row(st_ref, 16, ln[3])
    add_row(low_y, 15, ln[4])
    add_row(high_y, 15, ln[5])
    add_row(low_y, 0, ln[6])
    add_row(high_y, 0, ln[7])
    for i, r in enumerate((255, 15, 240, 0)):
        add_row(p_ref, r, ln[8 + i])
    is_odd = ctl_ref[0:1, :] > 0.5
    low, high = st_ref[0:16, :], st_ref[16:32, :]
    even[...] = jnp.where(is_odd, low, high)
    odd[...] = jnp.where(is_odd, high, low)
    low_y[...] = ctl_ref[1:2, :] * low_y[...]
    high_y[...] = ctl_ref[2:3, :] * high_y[...]


def pick(ctl_ref, even, odd):
    is_odd = ctl_ref[0:1, :] > 0.5
    return jnp.where(is_odd, even, odd), jnp.where(is_odd, odd, even)


def take_sum(p_ref, recv, s_ref):
    left, right, below, above = recv
    s_ref[...] = p_ref[...]
    s_ref[0:16, :] = s_ref[0:16, :] + left
    s_ref[240:256, :] = s_ref[240:256, :] + right
    for x in range(16):
        r = 16 * x
        s_ref[r:r + 1, :] = s_ref[r:r + 1, :] + below[x:x + 1, :]
        s_ref[r + 15:r + 16, :] = s_ref[r + 15:r + 16, :] + above[x:x + 1, :]
    return s_ref[...]


def fold(prod):
    part = prod.reshape(ROWS // 8, 8, COLS).sum(axis=0)
    return part[:, 0:128] + part[:, 128:256] + part[:, 256:384] + part[:, 384:512]


def first_kernel(ctl_ref, table_hbm, load_hbm, cond_hbm, flags_hbm, region_hbm, sq_hbm, sqz_hbm, wr_hbm, wz_hbm,
                 gf_hbm, bf_hbm,
                 coef_ref, react_ref, keep_ref, pl_ref, pd_ref, even_ref, odd_ref, yl_ref, yh_ref, gf_ref, bf_ref,
                 table_ref, load_ref, cond_ref, flags_ref, region_ref, sq_ref, sqz_ref, wr_ref, wz_ref, sems, st_ref):
    flags_tile = flags_hbm.at[:, :, pl.ds(0, 128)]
    pairs = ((cond_hbm, cond_ref), (wr_hbm, wr_ref), (wz_hbm, wz_ref), (region_hbm, region_ref), (table_hbm, table_ref),
             (sq_hbm, sq_ref), (sqz_hbm, sqz_ref), (load_hbm, load_ref), (flags_tile, flags_ref),
             (gf_hbm, gf_ref), (bf_hbm, bf_ref))
    copies = [pltpu.make_async_copy(src, dst, sems.at[i]) for i, (src, dst) in enumerate(pairs)]
    for copy in copies:
        copy.start()
    for copy in copies[:5]:
        copy.wait()
    w_row = wr_ref[...]
    w_row = jnp.concatenate([w_row] * 4, axis=1)
    quad_z = wz_ref[...]
    coef = (w_row * quad_z) * cond_ref[...].reshape(ROWS, COLS).astype(F32)
    coef_ref[...] = coef
    elem = lax.broadcasted_iota(jnp.int32, (COLS // 8, COLS), 0)
    lane = lax.broadcasted_iota(jnp.int32, (COLS // 8, COLS), 1)
    spread = (lane // 8 == elem).astype(F32)
    for ex in range(2):
        ids = region_ref[ex]
        kappa = jnp.zeros(ids.shape, F32)
        for k in range(NREG):
            kappa = kappa + jnp.where(ids == k, table_ref[k], 0.0)
        kappa = lax.dot_general(kappa, spread, (((1,), (0,)), ((), ())),
                                precision=lax.Precision.HIGHEST, preferred_element_type=F32)
        for x in range(8):
            for ey in range(2):
                r = (ex * 8 + x) * 16 + ey * 8
                react_ref[r:r + 8, :] = (w_row[r:r + 8] * quad_z) * kappa[ey:ey + 1, :]
    for copy in copies[5:]:
        copy.wait()
    keep_ref[...] = (1 - flags_ref[...].reshape(ROWS, 128)).astype(F32)
    high, low = halves(coef)
    rows = []
    for e in range(2):
        part = slice(128 * e, 128 * (e + 1))
        pair = jnp.concatenate([high[part], low[part]], 0)
        rows.append(dot(sq_ref[0], pair) + dot(sq_ref[1], pair))
    diag = jnp.concatenate(rows, 0) + mul_z(high, low, sqz_ref[...]) + react_ref[...]
    join_rows(load_ref[...].reshape(ROWS, COLS), pl_ref)
    join_rows(diag, pd_ref)
    for i, src in enumerate((pl_ref, pd_ref, coef_ref)):
        st_ref[0, 16 * i:16 * i + 16, :] = src[0:16, :]
        st_ref[1, 16 * i:16 * i + 16, :] = src[240:256, :]
        put_y(src, yl_ref, yh_ref, 16 * i)
    zeros = jnp.zeros((8, COLS), F32)
    for side, r in enumerate((0, 240)):
        st_ref[side, 48:56, :] = zeros
        st_ref[side, 48:49, :] = react_ref[r:r + 1, :]
        st_ref[side, 49:50, :] = react_ref[r + 15:r + 16, :]
    yl_ref[48:56, :] = zeros
    yh_ref[48:56, :] = zeros
    is_odd = ctl_ref[0:1, :] > 0.5
    even_ref[...] = jnp.where(is_odd, st_ref[0], st_ref[1])
    odd_ref[...] = jnp.where(is_odd, st_ref[1], st_ref[0])


def corner_kernel(ctl_ref, even_ref, odd_ref, lin_ref, hin_ref, low_ref, high_ref, x_ref):
    x_ref[0], x_ref[1] = pick(ctl_ref, even_ref[...], odd_ref[...])
    for src, out, row in ((lin_ref, low_ref, 0), (hin_ref, high_ref, 15)):
        out[...] = src[...]
        for base in (0, 16):
            add_row(out, base, x_ref[0, base + row:base + row + 1, :])
            add_row(out, base + 15, x_ref[1, base + row:base + row + 1, :])
        line = 48 if row == 0 else 49
        out[48:49, :] = x_ref[0, 32 + row:33 + row, :]
        out[49:50, :] = x_ref[1, 32 + row:33 + row, :]
        out[50:51, :] = x_ref[0, line:line + 1, :]
        out[51:52, :] = x_ref[1, line:line + 1, :]
    low_ref[...] = ctl_ref[1:2, :] * low_ref[...]
    high_ref[...] = ctl_ref[2:3, :] * high_ref[...]


def second_kernel(ctl_ref, pl_ref, pd_ref, xe_ref, xo_ref, yb_ref, ya_ref, keep_ref, coef_ref, react_ref,
                  grad_ref, back_ref, gz_ref, bz_ref, gf_ref, bf_ref,
                  r_ref, dinv_ref, cf_ref, cz_ref, rz_ref, p_ref, even, odd, low_y, high_y, s_ref, fv_ref, st_ref):
    left, right = pick(ctl_ref, xe_ref[...], xo_ref[...])
    below, above = yb_ref[...], ya_ref[...]
    diag = take_sum(pd_ref, (left[16:32], right[16:32], below[16:32], above[16:32]), s_ref)
    dinv_ref[...] = 1.0 / diag
    keep = keep_ref[...]
    dinv_ref[:, 0:128] = keep * dinv_ref[:, 0:128]
    r = take_sum(pl_ref, (left[0:16], right[0:16], below[0:16], above[0:16]), s_ref)
    r_ref[...] = r
    r_ref[:, 0:128] = keep * r_ref[:, 0:128]
    cf_ref[0:16, :] = above[32:48]
    cf_ref[16:32, :] = below[32:48]
    cf_ref[32:48, :] = right[32:48]
    cf_ref[48:64, :] = left[32:48]
    for out, base in ((cz_ref, 48), (rz_ref, 50)):
        out[0:1, :] = above[base + 1:base + 2]
        out[1:2, :] = above[base:base + 1]
        out[2:3, :] = below[base + 1:base + 2]
        out[3:4, :] = below[base:base + 1]
        out[4:8, :] = jnp.zeros((4, COLS), F32)
    a0 = dinv_ref[...] * r_ref[...] * (1.0 / CENTER)
    s_ref[...] = a0
    lines = corner_lines(s_ref, cf_ref[...], cz_ref[...], rz_ref[...], fv_ref, gf_ref, bf_ref, gz_ref[...], bz_ref[...])
    f = local_op(a0, coef_ref[...], react_ref[...], grad_ref, back_ref, gz_ref[...], bz_ref[...])
    emit_partial(f, lines, ctl_ref, p_ref, (even, odd, low_y, high_y), st_ref)


def sweep1_kernel(ctl_ref, pin_ref, xe_ref, xo_ref, yb_ref, ya_ref, r_ref, dinv_ref, coef_ref, react_ref,
                  cf_ref, cz_ref, rz_ref, grad_ref, back_ref, gz_ref, bz_ref, gf_ref, bf_ref,
                  a1_ref, p_ref, even, odd, low_y, high_y, s_ref, fv_ref, st_ref):
    image = take_sum(pin_ref, (*pick(ctl_ref, xe_ref[...], xo_ref[...]), yb_ref[...], ya_ref[...]), s_ref)
    dinv, r = dinv_ref[...], r_ref[...]
    a0 = dinv * r * (1.0 / CENTER)
    a1 = (1.0 + MIX1) * a0 + GAIN1 * (dinv * (r - image))
    a1_ref[...] = a1
    lines = corner_lines(a1_ref, cf_ref[...], cz_ref[...], rz_ref[...], fv_ref, gf_ref, bf_ref, gz_ref[...], bz_ref[...])
    f = local_op(a1, coef_ref[...], react_ref[...], grad_ref, back_ref, gz_ref[...], bz_ref[...])
    emit_partial(f, lines, ctl_ref, p_ref, (even, odd, low_y, high_y), st_ref)


def sweep2(image, a1, r, dinv):
    a0 = dinv * r * (1.0 / CENTER)
    return a1 + (MIX2 * (a1 - a0) + GAIN2 * (dinv * (r - image)))


def third_kernel(ctl_ref, pin_ref, xe_ref, xo_ref, yb_ref, ya_ref, r_ref, dinv_ref, a1_ref, load_ref, coef_ref, react_ref,
                 cf_ref, cz_ref, rz_ref, grad_ref, back_ref, gz_ref, bz_ref, gf_ref, bf_ref,
                 z_ref, p_ref, even, odd, low_y, high_y, dots_ref, s_ref, fv_ref, st_ref):
    image = take_sum(pin_ref, (*pick(ctl_ref, xe_ref[...], xo_ref[...]), yb_ref[...], ya_ref[...]), s_ref)
    z = sweep2(image, a1_ref[...], r_ref[...], dinv_ref[...])
    z_ref[...] = z
    dots_ref[0] = fold(load_ref[...].reshape(ROWS, COLS) * z)
    lines = corner_lines(z_ref, cf_ref[...], cz_ref[...], rz_ref[...], fv_ref, gf_ref, bf_ref, gz_ref[...], bz_ref[...])
    f = local_op(z, coef_ref[...], react_ref[...], grad_ref, back_ref, gz_ref[...], bz_ref[...])
    dots_ref[1] = fold(f * z)
    emit_partial(f, lines, ctl_ref, p_ref, (even, odd, low_y, high_y), st_ref)


def fourth_kernel(ctl_ref, pin_ref, xe_ref, xo_ref, yb_ref, ya_ref, dinv_ref, z_ref, coef_ref, react_ref,
                  cf_ref, cz_ref, rz_ref, grad_ref, back_ref, gz_ref, bz_ref, gf_ref, bf_ref,
                  im_ref, p_ref, even, odd, low_y, high_y, dots_ref, s_ref, fv_ref, st_ref):
    image = take_sum(pin_ref, (*pick(ctl_ref, xe_ref[...], xo_ref[...]), yb_ref[...], ya_ref[...]), s_ref)
    dinv = dinv_ref[...]
    im = jnp.where(dinv != 0.0, image, 0.0)
    im_ref[...] = im
    b0 = dinv * im * (1.0 / CENTER)
    s_ref[...] = b0
    lines = corner_lines(s_ref, cf_ref[...], cz_ref[...], rz_ref[...], fv_ref, gf_ref, bf_ref, gz_ref[...], bz_ref[...])
    f = local_op(b0, coef_ref[...], react_ref[...], grad_ref, back_ref, gz_ref[...], bz_ref[...])
    dots_ref[...] = fold(f * z_ref[...])
    emit_partial(f, lines, ctl_ref, p_ref, (even, odd, low_y, high_y), st_ref)


def fifth_kernel(ctl_ref, pin_ref, xe_ref, xo_ref, yb_ref, ya_ref, im_ref, dinv_ref, z_ref, d34_ref, d5_ref, coef_ref, react_ref,
                 cf_ref, cz_ref, rz_ref, grad_ref, back_ref, gz_ref, bz_ref, gf_ref, bf_ref,
                 b1_ref, p_ref, even, odd, low_y, high_y, dots_ref, s_ref, fv_ref, st_ref):
    image = take_sum(pin_ref, (*pick(ctl_ref, xe_ref[...], xo_ref[...]), yb_ref[...], ya_ref[...]), s_ref)
    dinv, im = dinv_ref[...], im_ref[...]
    b0 = dinv * im * (1.0 / CENTER)
    b1 = (1.0 + MIX1) * b0 + GAIN1 * (dinv * (im - image))
    b1_ref[...] = b1
    lines = corner_lines(b1_ref, cf_ref[...], cz_ref[...], rz_ref[...], fv_ref, gf_ref, bf_ref, gz_ref[...], bz_ref[...])
    f = local_op(b1, coef_ref[...], react_ref[...], grad_ref, back_ref, gz_ref[...], bz_ref[...])
    emit_partial(f, lines, ctl_ref, p_ref, (even, odd, low_y, high_y), st_ref)
    last = fold(f * ((1.0 + MIX2) * z_ref[...] - (CENTER * GAIN2) * b0))
    both = last + (CENTER * GAIN2 - MIX2) * d5_ref[...]
    rows = [part.sum(axis=0, keepdims=True) for part in (d34_ref[0], d34_ref[1], both)]
    lane = lax.broadcasted_iota(jnp.int32, (1, 128), 1)
    packed = jnp.zeros((1, 128), F32)
    for i, row in enumerate(rows):
        row = row + pltpu.roll(row, 64, 1)
        row = row + pltpu.roll(row, 32, 1)
        packed = jnp.where(lane // 32 == i, row, packed)
    dots_ref[...] = jnp.broadcast_to(packed, dots_ref.shape)


def last_kernel(dots_ref, ctl_ref, pin_ref, xe_ref, xo_ref, yb_ref, ya_ref, im_ref, dinv_ref, b1_ref, z_ref, r_ref,
                sol_hbm, res_hbm, dir_hbm, s_ref, sol_ref, res_ref, dir_ref, sems):
    lane = lax.broadcasted_iota(jnp.int32, (8, 128), 1)
    row = lax.broadcasted_iota(jnp.int32, (8, 128), 0)
    sums = jnp.sum(dots_ref[...], axis=0, keepdims=True)
    sums = jnp.sum(jnp.where(lane // 32 == row, sums, 0.0), axis=1, keepdims=True)
    first, curv, quad = sums[0:1], sums[1:2], sums[2:3]
    step = first / curv
    ratio = (first - 2.0 * step * curv + step * step * quad) / first
    shape = (16, 16, COLS)
    copies = [pltpu.make_async_copy(src, dst, sems.at[i])
              for i, (src, dst) in enumerate(((sol_ref, sol_hbm), (res_ref, res_hbm), (dir_ref, dir_hbm)))]
    z, im = z_ref[...], im_ref[...]
    sol_ref[...] = (step * z).reshape(shape)
    copies[0].start()
    res_ref[...] = (r_ref[...] - step * im).reshape(shape)
    copies[1].start()
    image = take_sum(pin_ref, (*pick(ctl_ref, xe_ref[...], xo_ref[...]), yb_ref[...], ya_ref[...]), s_ref)
    b2 = sweep2(image, b1_ref[...], im, dinv_ref[...])
    dir_ref[...] = ((z - step * b2) + ratio * z).reshape(shape)
    copies[2].start()
    for copy in copies:
        copy.wait()


VM = pl.BlockSpec(memory_space=pltpu.VMEM)
HB = pl.BlockSpec(memory_space=pl.ANY)
BIG = jax.ShapeDtypeStruct((ROWS, COLS), F32)
FACE = jax.ShapeDtypeStruct((16, COLS), F32)
PART = (BIG, FACE, FACE, FACE, FACE)
MESSAGE = jax.ShapeDtypeStruct((56, COLS), F32)
PARAMS = pltpu.CompilerParams(vmem_limit_bytes=24 << 20)


def call(kernel, outs, specs, scratch):
    return pl.pallas_call(
        kernel, out_shape=outs, in_specs=specs, out_specs=jax.tree.map(lambda _: VM, outs),
        scratch_shapes=scratch, compiler_params=PARAMS)


def step_call(kernel, outs, n_in):
    scratch = [pltpu.VMEM((rows, COLS), F32) for rows in (ROWS, 64, 32)]
    return call(kernel, outs, [VM] * (n_in + 1), scratch)


def swaps(first, count):
    pairs = [(i, i + 1) for i in range(first, count - 1, 2)]
    return pairs + [(j, i) for i, j in pairs]


def per_device(load, conductivity, flags, region, kappa_table):
    k = {name: jnp.asarray(value) for name, value in constants().items()}
    n_x, n_y = lax.axis_size("gx"), lax.axis_size("gy")
    at_x, at_y = lax.axis_index("gx"), lax.axis_index("gy")
    ctl = jnp.stack([at_x % 2 == 1, at_y != 0, at_y != n_y - 1, at_y < 0]).astype(F32)
    ctl = jnp.broadcast_to(ctl[:, None], (4, COLS))
    up_y = [(i, (i + 1) % n_y) for i in range(n_y)]
    down_y = [(j, i) for i, j in up_y]

    def along_x(even, odd):
        return lax.ppermute(even, "gx", swaps(0, n_x)), lax.ppermute(odd, "gx", swaps(1, n_x))

    def along_y(low, high):
        return lax.ppermute(high, "gy", up_y), lax.ppermute(low, "gy", down_y)

    def exchange(faces):
        even, odd, low_y, high_y = faces
        return (*along_x(even, odd), *along_y(low_y, high_y))

    keep_shape = jax.ShapeDtypeStruct((ROWS, 128), F32)
    inputs = (kappa_table, load, conductivity, flags, region, k["sq"], k["sq_z"], k["w_rows"], k["w_z"],
              k["grad_f"], k["back_f"])
    inputs = tuple(pltpu.with_memory_space_constraint(v, pltpu.HBM) for v in inputs)
    buffers = [pltpu.VMEM(v.shape, v.dtype) for v in inputs[:9]]
    buffers[0] = pltpu.SMEM(kappa_table.shape, F32)
    buffers[3] = pltpu.VMEM((16, 16, 128), jnp.int32)
    buffers += [pltpu.SemaphoreType.DMA((len(inputs),)), pltpu.VMEM((2, 56, COLS), F32)]
    small = tuple(jax.ShapeDtypeStruct(v.shape, v.dtype) for v in inputs[9:])
    coef, react, keep, part_l, part_d, even, odd, low_y, high_y, grad_f, back_f = call(
        first_kernel, (BIG, BIG, keep_shape, BIG, BIG) + (MESSAGE,) * 4 + small, [VM] + [HB] * len(inputs),
        buffers)(ctl, *inputs)
    mats = (k["grad"], k["back"], k["grad_z"], k["back_z"], grad_f, back_f)
    even, odd = along_x(even, odd)
    low_y, high_y = call(corner_kernel, (MESSAGE, MESSAGE), [VM] * 5, [pltpu.VMEM((2, 56, COLS), F32)])(
        ctl, even, odd, low_y, high_y)
    recv = (even, odd, *along_y(low_y, high_y))
    line = jax.ShapeDtypeStruct((8, COLS), F32)
    r, dinv, cf, cz, rz, part, *faces = step_call(
        second_kernel, (BIG, BIG, jax.ShapeDtypeStruct((64, COLS), F32), line, line) + PART, 15)(
        ctl, part_l, part_d, *recv, keep, coef, react, *mats)
    tail = (coef, react, cf, cz, rz, *mats)
    recv = exchange(faces)
    a1, part, *faces = step_call(sweep1_kernel, (BIG,) + PART, 18)(ctl, part, *recv, r, dinv, *tail)
    recv = exchange(faces)
    d34_shape = jax.ShapeDtypeStruct((2, 8, 128), F32)
    z, part, *faces, d34 = step_call(third_kernel, (BIG,) + PART + (d34_shape,), 20)(
        ctl, part, *recv, r, dinv, a1, load, *tail)
    recv = exchange(faces)
    d5_shape = jax.ShapeDtypeStruct((8, 128), F32)
    im, part, *faces, d5 = step_call(fourth_kernel, (BIG,) + PART + (d5_shape,), 18)(
        ctl, part, *recv, dinv, z, *tail)
    recv = exchange(faces)
    dots_shape = jax.ShapeDtypeStruct((n_y, 128), F32)
    b1, part, *faces, dots = step_call(fifth_kernel, (BIG,) + PART + (dots_shape,), 21)(
        ctl, part, *recv, im, dinv, z, d34, d5, *tail)
    total = lax.all_to_all(dots, "gy", 0, 0, tiled=True).sum(0)
    recv = exchange(faces)
    total = lax.all_to_all(jnp.broadcast_to(total, (n_x, 128)), "gx", 0, 0, tiled=True)
    shape = jax.ShapeDtypeStruct((16, 16, COLS), F32)
    scratch = [pltpu.VMEM((ROWS, COLS), F32)] + [pltpu.VMEM((16, 16, COLS), F32)] * 3 + [pltpu.SemaphoreType.DMA((3,))]
    return pl.pallas_call(
        last_kernel, out_shape=(shape, shape, shape), in_specs=[VM] * 12, out_specs=(HB, HB, HB),
        scratch_shapes=scratch, compiler_params=PARAMS)(total, ctl, part, *recv, im, dinv, b1, z, r)


def solution(mesh):
    placed = P("gx", "gy", None)
    return jax.shard_map(
        per_device,
        mesh=mesh,
        in_specs=(placed, placed, placed, placed, P()),
        out_specs=(placed, placed, placed),
        check_vma=False,
    )
```

```python
import jax
import jax.numpy as jnp
import ml_dtypes
import numpy as np
from jax import lax
from jax.experimental import pallas as pl
from jax.experimental.pallas import tpu as pltpu
from jax.sharding import PartitionSpec as P

NREG = 3
CENTER = 24.0
HALF = 23.0
RHO0 = HALF / CENTER
RHO1 = 1.0 / (2.0 * CENTER / HALF - RHO0)
RHO2 = 1.0 / (2.0 * CENTER / HALF - RHO1)
MIX1, GAIN1 = RHO1 * RHO0, 2.0 * RHO1 / HALF
MIX2, GAIN2 = RHO2 * RHO1, 2.0 * RHO2 / HALF

F32 = jnp.float32
BF16 = jnp.bfloat16
ROWS, COLS = 256, 512


def gll_tables():
    nodes = np.array(
        [
            -1.0,
            -0.8717401485096066,
            -0.5917001814331423,
            -0.2092992179024789,
            0.2092992179024789,
            0.5917001814331423,
            0.8717401485096066,
            1.0,
        ]
    )
    prev = np.ones(8)
    now = nodes.copy()
    for degree in range(1, 7):
        prev, now = now, ((2 * degree + 1) * nodes * now - degree * prev) / (degree + 1)
    weights = 2.0 / (56.0 * now**2)
    table = np.zeros((8, 8))
    for a in range(8):
        for b in range(8):
            if a != b:
                table[a, b] = now[a] / (now[b] * (nodes[a] - nodes[b]))
    table[0, 0] = -14.0
    table[7, 7] = 14.0
    return table, weights


def split_np(mat):
    high = mat.astype(ml_dtypes.bfloat16)
    low = (mat - high.astype(np.float64)).astype(ml_dtypes.bfloat16)
    return high, low


def left_pair(mat):
    high, low = split_np(mat)
    return np.stack([np.concatenate([high, high], 1), np.concatenate([low, low], 1)])


def right_pair(mat):
    high, low = split_np(mat)
    both = np.concatenate([high, low], 1)
    return np.concatenate([both, both], 0)


def constants():
    table, weights = gll_tables()
    table = table.astype(np.float32).astype(np.float64)
    weights = weights.astype(np.float32)
    eye8, eye2, eye16 = np.eye(8), np.eye(2), np.eye(16)
    d_x = np.kron(table, eye16)
    d_y = np.kron(eye8, np.kron(eye2, table))
    square = (table * table).astype(np.float32).astype(np.float64)
    q_x = np.kron(square, eye16)
    q_y = np.kron(eye8, np.kron(eye2, square))
    d_z = np.kron(eye16, table)
    q_z = np.kron(eye16, square)
    grad = left_pair(np.concatenate([d_x, d_y], 0))
    back_h, back_l = split_np(np.concatenate([d_x.T, d_y.T], 1))
    back = np.stack([back_h, back_l])
    sq = left_pair(q_x.T + q_y.T)
    grad_z = right_pair(d_z.T)
    back_z = right_pair(d_z)
    sq_z = right_pair(q_z)
    lines = np.zeros((8, 64))
    for face in range(4):
        lines[2 * face, 16 * face:16 * face + 8] = table[:, 0]
        lines[2 * face + 1, 16 * face + 8:16 * face + 16] = table[:, 7]
    grad_f = left_pair(np.kron(np.eye(8), table))
    back_f = left_pair(lines)
    w_xy = (weights[:, None] * weights[None, :]).astype(np.float32)
    w_xy = np.tile(w_xy, (2, 2)).reshape(ROWS, 1)
    w_rows = np.ascontiguousarray(np.broadcast_to(w_xy, (ROWS, 128)))
    w_z = np.tile(weights, COLS // 8).reshape(1, COLS).astype(np.float32)
    return dict(grad=grad, back=back, sq=sq, grad_z=grad_z, back_z=back_z, grad_f=grad_f, back_f=back_f, sq_z=sq_z, w_rows=w_rows, w_z=w_z)


def dot(a, b):
    return lax.dot_general(a, b, (((1,), (0,)), ((), ())), preferred_element_type=F32)


def halves(v):
    high = v.astype(BF16)
    low = (v - high.astype(F32)).astype(BF16)
    return high, low


def mul_z(high, low, mat):
    outs = []
    for k in range(COLS // 128):
        part = slice(128 * k, 128 * (k + 1))
        both = dot(jnp.concatenate([high[:, part], low[:, part]], 1), mat)
        outs.append(both[:, :128] + both[:, 128:])
    return jnp.concatenate(outs, 1)


def local_op(v, coef, react, grad, back, grad_z, back_z):
    high, low = halves(v)
    rows = []
    for e in range(2):
        part = slice(128 * e, 128 * (e + 1))
        pair = jnp.concatenate([high[part], low[part]], 0)
        flux = dot(grad[0], pair) + dot(grad[1], pair)
        c = coef[part]
        f_h, f_l = halves(flux * jnp.concatenate([c, c], 0))
        rows.append(dot(back[0], f_h) + (dot(back[0], f_l) + dot(back[1], f_h)))
    out = jnp.concatenate(rows, 0)
    flux_z = mul_z(high, low, grad_z) * coef
    return out + mul_z(*halves(flux_z), back_z) + react * v


def join_z(f):
    lane = lax.broadcasted_iota(jnp.int32, (1, COLS), 1)
    upper = ((lane % 8) == 7) & (lane != COLS - 1)
    lower = ((lane % 8) == 0) & (lane != 0)
    nxt = pltpu.roll(f, COLS - 1, 1)
    prv = pltpu.roll(f, 1, 1)
    return f + jnp.where(upper, nxt, jnp.where(lower, prv, 0.0))


def corner_lines(v_ref, cf, cz, rz, fv_ref, grad_f, back_f, grad_z, back_z):
    for x in range(16):
        r = 16 * x
        fv_ref[x:x + 1, :] = v_ref[r + 15:r + 16, :]
        fv_ref[16 + x:17 + x, :] = v_ref[r:r + 1, :]
    fv_ref[32:48, :] = v_ref[240:256, :]
    fv_ref[48:64, :] = v_ref[0:16, :]
    pair = jnp.concatenate(halves(fv_ref[...]), 0)
    flux = (dot(grad_f[0], pair) + dot(grad_f[1], pair)) * cf
    pair = jnp.concatenate(halves(flux), 0)
    ends = dot(back_f[0], pair) + dot(back_f[1], pair)
    for row, r in enumerate((255, 15, 240, 0, 255, 15, 240, 0)):
        fv_ref[row:row + 1, :] = v_ref[r:r + 1, :]
    at = fv_ref[0:8, :]
    flux_z = mul_z(*halves(at), grad_z) * cz
    return join_z(jnp.concatenate([ends, mul_z(*halves(flux_z), back_z) + rz * at], 0))


def join_rows(f, p_ref):
    p_ref[...] = join_z(f)
    p_ref[112:128, :] = p_ref[112:128, :] + p_ref[128:144, :]
    p_ref[128:144, :] = p_ref[112:128, :]
    for x in range(16):
        r = 16 * x
        mid = p_ref[r + 7:r + 8, :] + p_ref[r + 8:r + 9, :]
        p_ref[r + 7:r + 8, :] = mid
        p_ref[r + 8:r + 9, :] = mid


def put_y(p_ref, low, high, base):
    for x in range(16):
        r = 16 * x
        low[base + x:base + x + 1, :] = p_ref[r:r + 1, :]
        high[base + x:base + x + 1, :] = p_ref[r + 15:r + 16, :]


def add_row(ref, row, line):
    ref[row:row + 1, :] = ref[row:row + 1, :] + line


def emit_partial(f, lines, ctl_ref, p_ref, faces, st_ref):
    even, odd, low_y, high_y = faces
    join_rows(f, p_ref)
    st_ref[0:16, :] = p_ref[0:16, :]
    st_ref[16:32, :] = p_ref[240:256, :]
    put_y(p_ref, low_y, high_y, 0)
    ln = [lines[i:i + 1] for i in range(12)]
    add_row(st_ref, 15, ln[0])
    add_row(st_ref, 31, ln[1])
    add_row(st_ref, 0, ln[2])
    add_row(st_ref, 16, ln[3])
    add_row(low_y, 15, ln[4])
    add_row(high_y, 15, ln[5])
    add_row(low_y, 0, ln[6])
    add_row(high_y, 0, ln[7])
    for i, r in enumerate((255, 15, 240, 0)):
        add_row(p_ref, r, ln[8 + i])
    is_odd = ctl_ref[0:1, :] > 0.5
    low, high = st_ref[0:16, :], st_ref[16:32, :]
    even[...] = jnp.where(is_odd, low, high)
    odd[...] = jnp.where(is_odd, high, low)
    low_y[...] = ctl_ref[1:2, :] * low_y[...]
    high_y[...] = ctl_ref[2:3, :] * high_y[...]


def pick(ctl_ref, even, odd):
    is_odd = ctl_ref[0:1, :] > 0.5
    return jnp.where(is_odd, even, odd), jnp.where(is_odd, odd, even)


def take_sum(p_ref, recv, s_ref):
    left, right, below, above = recv
    s_ref[...] = p_ref[...]
    s_ref[0:16, :] = s_ref[0:16, :] + left
    s_ref[240:256, :] = s_ref[240:256, :] + right
    for x in range(16):
        r = 16 * x
        s_ref[r:r + 1, :] = s_ref[r:r + 1, :] + below[x:x + 1, :]
        s_ref[r + 15:r + 16, :] = s_ref[r + 15:r + 16, :] + above[x:x + 1, :]
    return s_ref[...]


def fold(prod):
    part = prod.reshape(ROWS // 8, 8, COLS).sum(axis=0)
    return part[:, 0:128] + part[:, 128:256] + part[:, 256:384] + part[:, 384:512]


def first_kernel(ctl_ref, table_hbm, load_hbm, cond_hbm, flags_hbm, region_hbm, sq_hbm, sqz_hbm, wr_hbm, wz_hbm,
                 gf_hbm, bf_hbm,
                 coef_ref, react_ref, keep_ref, pl_ref, pd_ref, even_ref, odd_ref, yl_ref, yh_ref, gf_ref, bf_ref,
                 table_ref, load_ref, cond_ref, flags_ref, region_ref, sq_ref, sqz_ref, wr_ref, wz_ref, sems, st_ref):
    flags_tile = flags_hbm.at[:, :, pl.ds(0, 128)]
    pairs = ((cond_hbm, cond_ref), (wr_hbm, wr_ref), (wz_hbm, wz_ref), (region_hbm, region_ref), (table_hbm, table_ref),
             (sq_hbm, sq_ref), (sqz_hbm, sqz_ref), (load_hbm, load_ref), (flags_tile, flags_ref),
             (gf_hbm, gf_ref), (bf_hbm, bf_ref))
    copies = [pltpu.make_async_copy(src, dst, sems.at[i]) for i, (src, dst) in enumerate(pairs)]
    for copy in copies:
        copy.start()
    for copy in copies[:5]:
        copy.wait()
    w_row = wr_ref[...]
    w_row = jnp.concatenate([w_row] * 4, axis=1)
    quad_z = wz_ref[...]
    coef = (w_row * quad_z) * cond_ref[...].reshape(ROWS, COLS).astype(F32)
    coef_ref[...] = coef
    elem = lax.broadcasted_iota(jnp.int32, (COLS // 8, COLS), 0)
    lane = lax.broadcasted_iota(jnp.int32, (COLS // 8, COLS), 1)
    spread = (lane // 8 == elem).astype(F32)
    for ex in range(2):
        ids = region_ref[ex]
        kappa = jnp.zeros(ids.shape, F32)
        for k in range(NREG):
            kappa = kappa + jnp.where(ids == k, table_ref[k], 0.0)
        kappa = lax.dot_general(kappa, spread, (((1,), (0,)), ((), ())),
                                precision=lax.Precision.HIGHEST, preferred_element_type=F32)
        for x in range(8):
            for ey in range(2):
                r = (ex * 8 + x) * 16 + ey * 8
                react_ref[r:r + 8, :] = (w_row[r:r + 8] * quad_z) * kappa[ey:ey + 1, :]
    for copy in copies[5:]:
        copy.wait()
    keep_ref[...] = (1 - flags_ref[...].reshape(ROWS, 128)).astype(F32)
    high, low = halves(coef)
    rows = []
    for e in range(2):
        part = slice(128 * e, 128 * (e + 1))
        pair = jnp.concatenate([high[part], low[part]], 0)
        rows.append(dot(sq_ref[0], pair) + dot(sq_ref[1], pair))
    diag = jnp.concatenate(rows, 0) + mul_z(high, low, sqz_ref[...]) + react_ref[...]
    join_rows(load_ref[...].reshape(ROWS, COLS), pl_ref)
    join_rows(diag, pd_ref)
    for i, src in enumerate((pl_ref, pd_ref, coef_ref)):
        st_ref[0, 16 * i:16 * i + 16, :] = src[0:16, :]
        st_ref[1, 16 * i:16 * i + 16, :] = src[240:256, :]
        put_y(src, yl_ref, yh_ref, 16 * i)
    zeros = jnp.zeros((8, COLS), F32)
    for side, r in enumerate((0, 240)):
        st_ref[side, 48:56, :] = zeros
        st_ref[side, 48:49, :] = react_ref[r:r + 1, :]
        st_ref[side, 49:50, :] = react_ref[r + 15:r + 16, :]
    yl_ref[48:56, :] = zeros
    yh_ref[48:56, :] = zeros
    is_odd = ctl_ref[0:1, :] > 0.5
    even_ref[...] = jnp.where(is_odd, st_ref[0], st_ref[1])
    odd_ref[...] = jnp.where(is_odd, st_ref[1], st_ref[0])


def corner_kernel(ctl_ref, even_ref, odd_ref, lin_ref, hin_ref, low_ref, high_ref, x_ref):
    x_ref[0], x_ref[1] = pick(ctl_ref, even_ref[...], odd_ref[...])
    for src, out, row in ((lin_ref, low_ref, 0), (hin_ref, high_ref, 15)):
        out[...] = src[...]
        for base in (0, 16):
            add_row(out, base, x_ref[0, base + row:base + row + 1, :])
            add_row(out, base + 15, x_ref[1, base + row:base + row + 1, :])
        line = 48 if row == 0 else 49
        out[48:49, :] = x_ref[0, 32 + row:33 + row, :]
        out[49:50, :] = x_ref[1, 32 + row:33 + row, :]
        out[50:51, :] = x_ref[0, line:line + 1, :]
        out[51:52, :] = x_ref[1, line:line + 1, :]
    low_ref[...] = ctl_ref[1:2, :] * low_ref[...]
    high_ref[...] = ctl_ref[2:3, :] * high_ref[...]


def second_kernel(ctl_ref, pl_ref, pd_ref, xe_ref, xo_ref, yb_ref, ya_ref, keep_ref, coef_ref, react_ref,
                  grad_ref, back_ref, gz_ref, bz_ref, gf_ref, bf_ref,
                  r_ref, dinv_ref, cf_ref, cz_ref, rz_ref, p_ref, even, odd, low_y, high_y, s_ref, fv_ref, st_ref):
    left, right = pick(ctl_ref, xe_ref[...], xo_ref[...])
    below, above = yb_ref[...], ya_ref[...]
    diag = take_sum(pd_ref, (left[16:32], right[16:32], below[16:32], above[16:32]), s_ref)
    dinv_ref[...] = 1.0 / diag
    keep = keep_ref[...]
    dinv_ref[:, 0:128] = keep * dinv_ref[:, 0:128]
    r = take_sum(pl_ref, (left[0:16], right[0:16], below[0:16], above[0:16]), s_ref)
    r_ref[...] = r
    r_ref[:, 0:128] = keep * r_ref[:, 0:128]
    cf_ref[0:16, :] = above[32:48]
    cf_ref[16:32, :] = below[32:48]
    cf_ref[32:48, :] = right[32:48]
    cf_ref[48:64, :] = left[32:48]
    for out, base in ((cz_ref, 48), (rz_ref, 50)):
        out[0:1, :] = above[base + 1:base + 2]
        out[1:2, :] = above[base:base + 1]
        out[2:3, :] = below[base + 1:base + 2]
        out[3:4, :] = below[base:base + 1]
        out[4:8, :] = jnp.zeros((4, COLS), F32)
    a0 = dinv_ref[...] * r_ref[...] * (1.0 / CENTER)
    s_ref[...] = a0
    lines = corner_lines(s_ref, cf_ref[...], cz_ref[...], rz_ref[...], fv_ref, gf_ref, bf_ref, gz_ref[...], bz_ref[...])
    f = local_op(a0, coef_ref[...], react_ref[...], grad_ref, back_ref, gz_ref[...], bz_ref[...])
    emit_partial(f, lines, ctl_ref, p_ref, (even, odd, low_y, high_y), st_ref)


def sweep1_kernel(ctl_ref, pin_ref, xe_ref, xo_ref, yb_ref, ya_ref, r_ref, dinv_ref, coef_ref, react_ref,
                  cf_ref, cz_ref, rz_ref, grad_ref, back_ref, gz_ref, bz_ref, gf_ref, bf_ref,
                  a1_ref, p_ref, even, odd, low_y, high_y, s_ref, fv_ref, st_ref):
    image = take_sum(pin_ref, (*pick(ctl_ref, xe_ref[...], xo_ref[...]), yb_ref[...], ya_ref[...]), s_ref)
    dinv, r = dinv_ref[...], r_ref[...]
    a0 = dinv * r * (1.0 / CENTER)
    a1 = (1.0 + MIX1) * a0 + GAIN1 * (dinv * (r - image))
    a1_ref[...] = a1
    lines = corner_lines(a1_ref, cf_ref[...], cz_ref[...], rz_ref[...], fv_ref, gf_ref, bf_ref, gz_ref[...], bz_ref[...])
    f = local_op(a1, coef_ref[...], react_ref[...], grad_ref, back_ref, gz_ref[...], bz_ref[...])
    emit_partial(f, lines, ctl_ref, p_ref, (even, odd, low_y, high_y), st_ref)


def sweep2(image, a1, r, dinv):
    a0 = dinv * r * (1.0 / CENTER)
    return a1 + (MIX2 * (a1 - a0) + GAIN2 * (dinv * (r - image)))


def third_kernel(ctl_ref, pin_ref, xe_ref, xo_ref, yb_ref, ya_ref, r_ref, dinv_ref, a1_ref, load_ref, coef_ref, react_ref,
                 cf_ref, cz_ref, rz_ref, grad_ref, back_ref, gz_ref, bz_ref, gf_ref, bf_ref,
                 z_ref, p_ref, even, odd, low_y, high_y, dots_ref, s_ref, fv_ref, st_ref):
    image = take_sum(pin_ref, (*pick(ctl_ref, xe_ref[...], xo_ref[...]), yb_ref[...], ya_ref[...]), s_ref)
    z = sweep2(image, a1_ref[...], r_ref[...], dinv_ref[...])
    z_ref[...] = z
    dots_ref[0] = fold(load_ref[...].reshape(ROWS, COLS) * z)
    lines = corner_lines(z_ref, cf_ref[...], cz_ref[...], rz_ref[...], fv_ref, gf_ref, bf_ref, gz_ref[...], bz_ref[...])
    f = local_op(z, coef_ref[...], react_ref[...], grad_ref, back_ref, gz_ref[...], bz_ref[...])
    dots_ref[1] = fold(f * z)
    emit_partial(f, lines, ctl_ref, p_ref, (even, odd, low_y, high_y), st_ref)


def fourth_kernel(ctl_ref, pin_ref, xe_ref, xo_ref, yb_ref, ya_ref, dinv_ref, z_ref, coef_ref, react_ref,
                  cf_ref, cz_ref, rz_ref, grad_ref, back_ref, gz_ref, bz_ref, gf_ref, bf_ref,
                  im_ref, p_ref, even, odd, low_y, high_y, dots_ref, s_ref, fv_ref, st_ref):
    image = take_sum(pin_ref, (*pick(ctl_ref, xe_ref[...], xo_ref[...]), yb_ref[...], ya_ref[...]), s_ref)
    dinv = dinv_ref[...]
    im = jnp.where(dinv != 0.0, image, 0.0)
    im_ref[...] = im
    b0 = dinv * im * (1.0 / CENTER)
    s_ref[...] = b0
    lines = corner_lines(s_ref, cf_ref[...], cz_ref[...], rz_ref[...], fv_ref, gf_ref, bf_ref, gz_ref[...], bz_ref[...])
    f = local_op(b0, coef_ref[...], react_ref[...], grad_ref, back_ref, gz_ref[...], bz_ref[...])
    dots_ref[...] = fold(f * z_ref[...])
    emit_partial(f, lines, ctl_ref, p_ref, (even, odd, low_y, high_y), st_ref)


def fifth_kernel(ctl_ref, pin_ref, xe_ref, xo_ref, yb_ref, ya_ref, im_ref, dinv_ref, z_ref, d34_ref, d5_ref, coef_ref, react_ref,
                 cf_ref, cz_ref, rz_ref, grad_ref, back_ref, gz_ref, bz_ref, gf_ref, bf_ref,
                 b1_ref, p_ref, even, odd, low_y, high_y, dots_ref, s_ref, fv_ref, st_ref):
    image = take_sum(pin_ref, (*pick(ctl_ref, xe_ref[...], xo_ref[...]), yb_ref[...], ya_ref[...]), s_ref)
    dinv, im = dinv_ref[...], im_ref[...]
    b0 = dinv * im * (1.0 / CENTER)
    b1 = (1.0 + MIX1) * b0 + GAIN1 * (dinv * (im - image))
    b1_ref[...] = b1
    lines = corner_lines(b1_ref, cf_ref[...], cz_ref[...], rz_ref[...], fv_ref, gf_ref, bf_ref, gz_ref[...], bz_ref[...])
    f = local_op(b1, coef_ref[...], react_ref[...], grad_ref, back_ref, gz_ref[...], bz_ref[...])
    emit_partial(f, lines, ctl_ref, p_ref, (even, odd, low_y, high_y), st_ref)
    last = fold(f * ((1.0 + MIX2) * z_ref[...] - (CENTER * GAIN2) * b0))
    both = last + (CENTER * GAIN2 - MIX2) * d5_ref[...]
    rows = [part.sum(axis=0, keepdims=True) for part in (d34_ref[0], d34_ref[1], both)]
    dots_ref[0] = jnp.concatenate(rows + [jnp.zeros((5, 128), F32)], 0)
    for i in range(1, dots_ref.shape[0]):
        dots_ref[i] = dots_ref[0]


def last_kernel(dots_ref, ctl_ref, pin_ref, xe_ref, xo_ref, yb_ref, ya_ref, im_ref, dinv_ref, b1_ref, z_ref, r_ref,
                sol_hbm, res_hbm, dir_hbm, s_ref, sol_ref, res_ref, dir_ref, sems):
    sums = dots_ref[0]
    for i in range(1, dots_ref.shape[0]):
        sums = sums + dots_ref[i]
    sums = jnp.sum(sums, axis=1, keepdims=True)
    first, curv, quad = sums[0:1], sums[1:2], sums[2:3]
    step = first / curv
    ratio = (first - 2.0 * step * curv + step * step * quad) / first
    shape = (16, 16, COLS)
    copies = [pltpu.make_async_copy(src, dst, sems.at[i])
              for i, (src, dst) in enumerate(((sol_ref, sol_hbm), (res_ref, res_hbm), (dir_ref, dir_hbm)))]
    z, im = z_ref[...], im_ref[...]
    sol_ref[...] = (step * z).reshape(shape)
    copies[0].start()
    res_ref[...] = (r_ref[...] - step * im).reshape(shape)
    copies[1].start()
    image = take_sum(pin_ref, (*pick(ctl_ref, xe_ref[...], xo_ref[...]), yb_ref[...], ya_ref[...]), s_ref)
    b2 = sweep2(image, b1_ref[...], im, dinv_ref[...])
    dir_ref[...] = ((z - step * b2) + ratio * z).reshape(shape)
    copies[2].start()
    for copy in copies:
        copy.wait()


VM = pl.BlockSpec(memory_space=pltpu.VMEM)
HB = pl.BlockSpec(memory_space=pl.ANY)
BIG = jax.ShapeDtypeStruct((ROWS, COLS), F32)
FACE = jax.ShapeDtypeStruct((16, COLS), F32)
PART = (BIG, FACE, FACE, FACE, FACE)
MESSAGE = jax.ShapeDtypeStruct((56, COLS), F32)
PARAMS = pltpu.CompilerParams(vmem_limit_bytes=24 << 20)


def call(kernel, outs, specs, scratch):
    return pl.pallas_call(
        kernel, out_shape=outs, in_specs=specs, out_specs=jax.tree.map(lambda _: VM, outs),
        scratch_shapes=scratch, compiler_params=PARAMS)


def step_call(kernel, outs, n_in):
    scratch = [pltpu.VMEM((rows, COLS), F32) for rows in (ROWS, 64, 32)]
    return call(kernel, outs, [VM] * (n_in + 1), scratch)


def swaps(first, count):
    pairs = [(i, i + 1) for i in range(first, count - 1, 2)]
    return pairs + [(j, i) for i, j in pairs]


def per_device(load, conductivity, flags, region, kappa_table):
    k = {name: jnp.asarray(value) for name, value in constants().items()}
    n_x, n_y = lax.axis_size("gx"), lax.axis_size("gy")
    at_x, at_y = lax.axis_index("gx"), lax.axis_index("gy")
    ctl = jnp.stack([at_x % 2 == 1, at_y != 0, at_y != n_y - 1, at_y < 0]).astype(F32)
    ctl = jnp.broadcast_to(ctl[:, None], (4, COLS))
    up_y = [(i, (i + 1) % n_y) for i in range(n_y)]
    down_y = [(j, i) for i, j in up_y]

    def along_x(even, odd):
        return lax.ppermute(even, "gx", swaps(0, n_x)), lax.ppermute(odd, "gx", swaps(1, n_x))

    def along_y(low, high):
        return lax.ppermute(high, "gy", up_y), lax.ppermute(low, "gy", down_y)

    def exchange(faces):
        even, odd, low_y, high_y = faces
        return (*along_x(even, odd), *along_y(low_y, high_y))

    keep_shape = jax.ShapeDtypeStruct((ROWS, 128), F32)
    inputs = (kappa_table, load, conductivity, flags, region, k["sq"], k["sq_z"], k["w_rows"], k["w_z"],
              k["grad_f"], k["back_f"])
    inputs = tuple(pltpu.with_memory_space_constraint(v, pltpu.HBM) for v in inputs)
    buffers = [pltpu.VMEM(v.shape, v.dtype) for v in inputs[:9]]
    buffers[0] = pltpu.SMEM(kappa_table.shape, F32)
    buffers[3] = pltpu.VMEM((16, 16, 128), jnp.int32)
    buffers += [pltpu.SemaphoreType.DMA((len(inputs),)), pltpu.VMEM((2, 56, COLS), F32)]
    small = tuple(jax.ShapeDtypeStruct(v.shape, v.dtype) for v in inputs[9:])
    coef, react, keep, part_l, part_d, even, odd, low_y, high_y, grad_f, back_f = call(
        first_kernel, (BIG, BIG, keep_shape, BIG, BIG) + (MESSAGE,) * 4 + small, [VM] + [HB] * len(inputs),
        buffers)(ctl, *inputs)
    mats = (k["grad"], k["back"], k["grad_z"], k["back_z"], grad_f, back_f)
    even, odd = along_x(even, odd)
    low_y, high_y = call(corner_kernel, (MESSAGE, MESSAGE), [VM] * 5, [pltpu.VMEM((2, 56, COLS), F32)])(
        ctl, even, odd, low_y, high_y)
    recv = (even, odd, *along_y(low_y, high_y))
    line = jax.ShapeDtypeStruct((8, COLS), F32)
    r, dinv, cf, cz, rz, part, *faces = step_call(
        second_kernel, (BIG, BIG, jax.ShapeDtypeStruct((64, COLS), F32), line, line) + PART, 15)(
        ctl, part_l, part_d, *recv, keep, coef, react, *mats)
    tail = (coef, react, cf, cz, rz, *mats)
    recv = exchange(faces)
    a1, part, *faces = step_call(sweep1_kernel, (BIG,) + PART, 18)(ctl, part, *recv, r, dinv, *tail)
    recv = exchange(faces)
    d34_shape = jax.ShapeDtypeStruct((2, 8, 128), F32)
    z, part, *faces, d34 = step_call(third_kernel, (BIG,) + PART + (d34_shape,), 20)(
        ctl, part, *recv, r, dinv, a1, load, *tail)
    recv = exchange(faces)
    d5_shape = jax.ShapeDtypeStruct((8, 128), F32)
    im, part, *faces, d5 = step_call(fourth_kernel, (BIG,) + PART + (d5_shape,), 18)(
        ctl, part, *recv, dinv, z, *tail)
    recv = exchange(faces)
    dots_shape = jax.ShapeDtypeStruct((n_y, 8, 128), F32)
    b1, part, *faces, dots = step_call(fifth_kernel, (BIG,) + PART + (dots_shape,), 21)(
        ctl, part, *recv, im, dinv, z, d34, d5, *tail)
    total = lax.all_to_all(dots, "gy", 0, 0, tiled=True).sum(0)
    recv = exchange(faces)
    total, recv = lax.optimization_barrier((total, recv))
    total = lax.all_to_all(jnp.broadcast_to(total, (n_x, 8, 128)), "gx", 0, 0, tiled=True)
    shape = jax.ShapeDtypeStruct((16, 16, COLS), F32)
    scratch = [pltpu.VMEM((ROWS, COLS), F32)] + [pltpu.VMEM((16, 16, COLS), F32)] * 3 + [pltpu.SemaphoreType.DMA((3,))]
    return pl.pallas_call(
        last_kernel, out_shape=(shape, shape, shape), in_specs=[VM] * 12, out_specs=(HB, HB, HB),
        scratch_shapes=scratch, compiler_params=PARAMS)(total, ctl, part, *recv, im, dinv, b1, z, r)


def solution(mesh):
    placed = P("gx", "gy", None)
    return jax.shard_map(
        per_device,
        mesh=mesh,
        in_specs=(placed, placed, placed, placed, P()),
        out_specs=(placed, placed, placed),
        check_vma=False,
    )
```

```python
import jax
import jax.numpy as jnp
import ml_dtypes
import numpy as np
from jax import lax
from jax.experimental import pallas as pl
from jax.experimental.pallas import tpu as pltpu
from jax.sharding import PartitionSpec as P

NREG = 3
CENTER = 24.0
HALF = 23.0
RHO0 = HALF / CENTER
RHO1 = 1.0 / (2.0 * CENTER / HALF - RHO0)
RHO2 = 1.0 / (2.0 * CENTER / HALF - RHO1)
MIX1, GAIN1 = RHO1 * RHO0, 2.0 * RHO1 / HALF
MIX2, GAIN2 = RHO2 * RHO1, 2.0 * RHO2 / HALF

F32 = jnp.float32
BF16 = jnp.bfloat16
ROWS, COLS = 256, 512


def gll_tables():
    nodes = np.array(
        [
            -1.0,
            -0.8717401485096066,
            -0.5917001814331423,
            -0.2092992179024789,
            0.2092992179024789,
            0.5917001814331423,
            0.8717401485096066,
            1.0,
        ]
    )
    prev = np.ones(8)
    now = nodes.copy()
    for degree in range(1, 7):
        prev, now = now, ((2 * degree + 1) * nodes * now - degree * prev) / (degree + 1)
    weights = 2.0 / (56.0 * now**2)
    table = np.zeros((8, 8))
    for a in range(8):
        for b in range(8):
            if a != b:
                table[a, b] = now[a] / (now[b] * (nodes[a] - nodes[b]))
    table[0, 0] = -14.0
    table[7, 7] = 14.0
    return table, weights


def split_np(mat):
    high = mat.astype(ml_dtypes.bfloat16)
    low = (mat - high.astype(np.float64)).astype(ml_dtypes.bfloat16)
    return high, low


def left_pair(mat):
    high, low = split_np(mat)
    return np.stack([np.concatenate([high, high], 1), np.concatenate([low, low], 1)])


def right_pair(mat):
    high, low = split_np(mat)
    both = np.concatenate([high, low], 1)
    return np.concatenate([both, both], 0)


def constants():
    table, weights = gll_tables()
    table = table.astype(np.float32).astype(np.float64)
    weights = weights.astype(np.float32)
    eye8, eye2, eye16 = np.eye(8), np.eye(2), np.eye(16)
    d_x = np.kron(table, eye16)
    d_y = np.kron(eye8, np.kron(eye2, table))
    square = (table * table).astype(np.float32).astype(np.float64)
    q_x = np.kron(square, eye16)
    q_y = np.kron(eye8, np.kron(eye2, square))
    d_z = np.kron(eye16, table)
    q_z = np.kron(eye16, square)
    grad = left_pair(np.concatenate([d_x, d_y], 0))
    back_h, back_l = split_np(np.concatenate([d_x.T, d_y.T], 1))
    back = np.stack([back_h, back_l])
    sq = left_pair(q_x.T + q_y.T)
    grad_z = right_pair(d_z.T)
    back_z = right_pair(d_z)
    sq_z = right_pair(q_z)
    lines = np.zeros((8, 64))
    for face in range(4):
        lines[2 * face, 16 * face:16 * face + 8] = table[:, 0]
        lines[2 * face + 1, 16 * face + 8:16 * face + 16] = table[:, 7]
    grad_f = left_pair(np.kron(np.eye(8), table))
    back_f = left_pair(lines)
    w_xy = (weights[:, None] * weights[None, :]).astype(np.float32)
    w_xy = np.tile(w_xy, (2, 2)).reshape(ROWS, 1)
    w_rows = np.ascontiguousarray(np.broadcast_to(w_xy, (ROWS, 128)))
    w_z = np.tile(weights, COLS // 8).reshape(1, COLS).astype(np.float32)
    return dict(grad=grad, back=back, sq=sq, grad_z=grad_z, back_z=back_z, grad_f=grad_f, back_f=back_f, sq_z=sq_z, w_rows=w_rows, w_z=w_z)


def dot(a, b):
    return lax.dot_general(a, b, (((1,), (0,)), ((), ())), preferred_element_type=F32)


def halves(v):
    high = v.astype(BF16)
    low = (v - high.astype(F32)).astype(BF16)
    return high, low


def mul_z(high, low, mat):
    outs = []
    for k in range(COLS // 128):
        part = slice(128 * k, 128 * (k + 1))
        both = dot(jnp.concatenate([high[:, part], low[:, part]], 1), mat)
        outs.append(both[:, :128] + both[:, 128:])
    return jnp.concatenate(outs, 1)


def local_op(v, coef, react, grad, back, grad_z, back_z):
    high, low = halves(v)
    rows = []
    for e in range(2):
        part = slice(128 * e, 128 * (e + 1))
        pair = jnp.concatenate([high[part], low[part]], 0)
        flux = dot(grad[0], pair) + dot(grad[1], pair)
        c = coef[part]
        f_h, f_l = halves(flux * jnp.concatenate([c, c], 0))
        rows.append(dot(back[0], f_h) + (dot(back[0], f_l) + dot(back[1], f_h)))
    out = jnp.concatenate(rows, 0)
    flux_z = mul_z(high, low, grad_z) * coef
    return out + mul_z(*halves(flux_z), back_z) + react * v


def join_z(f):
    lane = lax.broadcasted_iota(jnp.int32, (1, COLS), 1)
    upper = ((lane % 8) == 7) & (lane != COLS - 1)
    lower = ((lane % 8) == 0) & (lane != 0)
    nxt = pltpu.roll(f, COLS - 1, 1)
    prv = pltpu.roll(f, 1, 1)
    return f + jnp.where(upper, nxt, jnp.where(lower, prv, 0.0))


def corner_lines(v_ref, cf, cz, rz, fv_ref, grad_f, back_f, grad_z, back_z):
    for x in range(16):
        r = 16 * x
        fv_ref[x:x + 1, :] = v_ref[r + 15:r + 16, :]
        fv_ref[16 + x:17 + x, :] = v_ref[r:r + 1, :]
    fv_ref[32:48, :] = v_ref[240:256, :]
    fv_ref[48:64, :] = v_ref[0:16, :]
    pair = jnp.concatenate(halves(fv_ref[...]), 0)
    flux = (dot(grad_f[0], pair) + dot(grad_f[1], pair)) * cf
    pair = jnp.concatenate(halves(flux), 0)
    ends = dot(back_f[0], pair) + dot(back_f[1], pair)
    for row, r in enumerate((255, 15, 240, 0, 255, 15, 240, 0)):
        fv_ref[row:row + 1, :] = v_ref[r:r + 1, :]
    at = fv_ref[0:8, :]
    flux_z = mul_z(*halves(at), grad_z) * cz
    return join_z(jnp.concatenate([ends, mul_z(*halves(flux_z), back_z) + rz * at], 0))


def join_rows(f, p_ref):
    p_ref[...] = join_z(f)
    p_ref[112:128, :] = p_ref[112:128, :] + p_ref[128:144, :]
    p_ref[128:144, :] = p_ref[112:128, :]
    for x in range(16):
        r = 16 * x
        mid = p_ref[r + 7:r + 8, :] + p_ref[r + 8:r + 9, :]
        p_ref[r + 7:r + 8, :] = mid
        p_ref[r + 8:r + 9, :] = mid


def put_y(p_ref, low, high, base):
    for x in range(16):
        r = 16 * x
        low[base + x:base + x + 1, :] = p_ref[r:r + 1, :]
        high[base + x:base + x + 1, :] = p_ref[r + 15:r + 16, :]


def add_row(ref, row, line):
    ref[row:row + 1, :] = ref[row:row + 1, :] + line


def emit_partial(f, lines, ctl_ref, p_ref, faces, st_ref):
    even, odd, low_y, high_y = faces
    join_rows(f, p_ref)
    st_ref[0:16, :] = p_ref[0:16, :]
    st_ref[16:32, :] = p_ref[240:256, :]
    put_y(p_ref, low_y, high_y, 0)
    ln = [lines[i:i + 1] for i in range(12)]
    add_row(st_ref, 15, ln[0])
    add_row(st_ref, 31, ln[1])
    add_row(st_ref, 0, ln[2])
    add_row(st_ref, 16, ln[3])
    add_row(low_y, 15, ln[4])
    add_row(high_y, 15, ln[5])
    add_row(low_y, 0, ln[6])
    add_row(high_y, 0, ln[7])
    for i, r in enumerate((255, 15, 240, 0)):
        add_row(p_ref, r, ln[8 + i])
    is_odd = ctl_ref[0:1, :] > 0.5
    low, high = st_ref[0:16, :], st_ref[16:32, :]
    even[...] = jnp.where(is_odd, low, high)
    odd[...] = jnp.where(is_odd, high, low)
    low_y[...] = ctl_ref[1:2, :] * low_y[...]
    high_y[...] = ctl_ref[2:3, :] * high_y[...]


def pick(ctl_ref, even, odd):
    is_odd = ctl_ref[0:1, :] > 0.5
    return jnp.where(is_odd, even, odd), jnp.where(is_odd, odd, even)


def take_sum(p_ref, recv, s_ref):
    left, right, below, above = recv
    s_ref[...] = p_ref[...]
    s_ref[0:16, :] = s_ref[0:16, :] + left
    s_ref[240:256, :] = s_ref[240:256, :] + right
    for x in range(16):
        r = 16 * x
        s_ref[r:r + 1, :] = s_ref[r:r + 1, :] + below[x:x + 1, :]
        s_ref[r + 15:r + 16, :] = s_ref[r + 15:r + 16, :] + above[x:x + 1, :]
    return s_ref[...]


def fold(prod):
    part = prod.reshape(ROWS // 8, 8, COLS).sum(axis=0)
    return part[:, 0:128] + part[:, 128:256] + part[:, 256:384] + part[:, 384:512]


def first_kernel(ctl_ref, table_hbm, load_hbm, cond_hbm, flags_hbm, region_hbm, sq_hbm, sqz_hbm, wr_hbm, wz_hbm,
                 gf_hbm, bf_hbm,
                 coef_ref, react_ref, keep_ref, pl_ref, pd_ref, even_ref, odd_ref, yl_ref, yh_ref, gf_ref, bf_ref,
                 table_ref, load_ref, cond_ref, flags_ref, region_ref, sq_ref, sqz_ref, wr_ref, wz_ref, sems, st_ref):
    flags_tile = flags_hbm.at[:, :, pl.ds(0, 128)]
    pairs = ((cond_hbm, cond_ref), (wr_hbm, wr_ref), (wz_hbm, wz_ref), (region_hbm, region_ref), (table_hbm, table_ref),
             (sq_hbm, sq_ref), (sqz_hbm, sqz_ref), (load_hbm, load_ref), (flags_tile, flags_ref),
             (gf_hbm, gf_ref), (bf_hbm, bf_ref))
    copies = [pltpu.make_async_copy(src, dst, sems.at[i]) for i, (src, dst) in enumerate(pairs)]
    for copy in copies:
        copy.start()
    for copy in copies[:5]:
        copy.wait()
    w_row = wr_ref[...]
    w_row = jnp.concatenate([w_row] * 4, axis=1)
    quad_z = wz_ref[...]
    coef = (w_row * quad_z) * cond_ref[...].reshape(ROWS, COLS).astype(F32)
    coef_ref[...] = coef
    elem = lax.broadcasted_iota(jnp.int32, (COLS // 8, COLS), 0)
    lane = lax.broadcasted_iota(jnp.int32, (COLS // 8, COLS), 1)
    spread = (lane // 8 == elem).astype(F32)
    for ex in range(2):
        ids = region_ref[ex]
        kappa = jnp.zeros(ids.shape, F32)
        for k in range(NREG):
            kappa = kappa + jnp.where(ids == k, table_ref[k], 0.0)
        kappa = lax.dot_general(kappa, spread, (((1,), (0,)), ((), ())),
                                precision=lax.Precision.HIGHEST, preferred_element_type=F32)
        for x in range(8):
            for ey in range(2):
                r = (ex * 8 + x) * 16 + ey * 8
                react_ref[r:r + 8, :] = (w_row[r:r + 8] * quad_z) * kappa[ey:ey + 1, :]
    for copy in copies[5:]:
        copy.wait()
    keep_ref[...] = (1 - flags_ref[...].reshape(ROWS, 128)).astype(F32)
    high, low = halves(coef)
    rows = []
    for e in range(2):
        part = slice(128 * e, 128 * (e + 1))
        pair = jnp.concatenate([high[part], low[part]], 0)
        rows.append(dot(sq_ref[0], pair) + dot(sq_ref[1], pair))
    diag = jnp.concatenate(rows, 0) + mul_z(high, low, sqz_ref[...]) + react_ref[...]
    join_rows(load_ref[...].reshape(ROWS, COLS), pl_ref)
    join_rows(diag, pd_ref)
    for i, src in enumerate((pl_ref, pd_ref, coef_ref)):
        st_ref[0, 16 * i:16 * i + 16, :] = src[0:16, :]
        st_ref[1, 16 * i:16 * i + 16, :] = src[240:256, :]
        put_y(src, yl_ref, yh_ref, 16 * i)
    zeros = jnp.zeros((8, COLS), F32)
    for side, r in enumerate((0, 240)):
        st_ref[side, 48:56, :] = zeros
        st_ref[side, 48:49, :] = react_ref[r:r + 1, :]
        st_ref[side, 49:50, :] = react_ref[r + 15:r + 16, :]
    yl_ref[48:56, :] = zeros
    yh_ref[48:56, :] = zeros
    is_odd = ctl_ref[0:1, :] > 0.5
    even_ref[...] = jnp.where(is_odd, st_ref[0], st_ref[1])
    odd_ref[...] = jnp.where(is_odd, st_ref[1], st_ref[0])


def corner_kernel(ctl_ref, even_ref, odd_ref, lin_ref, hin_ref, low_ref, high_ref, x_ref):
    x_ref[0], x_ref[1] = pick(ctl_ref, even_ref[...], odd_ref[...])
    for src, out, row in ((lin_ref, low_ref, 0), (hin_ref, high_ref, 15)):
        out[...] = src[...]
        for base in (0, 16):
            add_row(out, base, x_ref[0, base + row:base + row + 1, :])
            add_row(out, base + 15, x_ref[1, base + row:base + row + 1, :])
        line = 48 if row == 0 else 49
        out[48:49, :] = x_ref[0, 32 + row:33 + row, :]
        out[49:50, :] = x_ref[1, 32 + row:33 + row, :]
        out[50:51, :] = x_ref[0, line:line + 1, :]
        out[51:52, :] = x_ref[1, line:line + 1, :]
    low_ref[...] = ctl_ref[1:2, :] * low_ref[...]
    high_ref[...] = ctl_ref[2:3, :] * high_ref[...]


def second_kernel(ctl_ref, pl_ref, pd_ref, xe_ref, xo_ref, yb_ref, ya_ref, keep_ref, coef_ref, react_ref,
                  grad_ref, back_ref, gz_ref, bz_ref, gf_ref, bf_ref,
                  r_ref, dinv_ref, cf_ref, cz_ref, rz_ref, p_ref, even, odd, low_y, high_y, s_ref, fv_ref, st_ref):
    left, right = pick(ctl_ref, xe_ref[...], xo_ref[...])
    below, above = yb_ref[...], ya_ref[...]
    diag = take_sum(pd_ref, (left[16:32], right[16:32], below[16:32], above[16:32]), s_ref)
    dinv_ref[...] = 1.0 / diag
    keep = keep_ref[...]
    dinv_ref[:, 0:128] = keep * dinv_ref[:, 0:128]
    r = take_sum(pl_ref, (left[0:16], right[0:16], below[0:16], above[0:16]), s_ref)
    r_ref[...] = r
    r_ref[:, 0:128] = keep * r_ref[:, 0:128]
    cf_ref[0:16, :] = above[32:48]
    cf_ref[16:32, :] = below[32:48]
    cf_ref[32:48, :] = right[32:48]
    cf_ref[48:64, :] = left[32:48]
    for out, base in ((cz_ref, 48), (rz_ref, 50)):
        out[0:1, :] = above[base + 1:base + 2]
        out[1:2, :] = above[base:base + 1]
        out[2:3, :] = below[base + 1:base + 2]
        out[3:4, :] = below[base:base + 1]
        out[4:8, :] = jnp.zeros((4, COLS), F32)
    a0 = dinv_ref[...] * r_ref[...] * (1.0 / CENTER)
    s_ref[...] = a0
    lines = corner_lines(s_ref, cf_ref[...], cz_ref[...], rz_ref[...], fv_ref, gf_ref, bf_ref, gz_ref[...], bz_ref[...])
    f = local_op(a0, coef_ref[...], react_ref[...], grad_ref, back_ref, gz_ref[...], bz_ref[...])
    emit_partial(f, lines, ctl_ref, p_ref, (even, odd, low_y, high_y), st_ref)


def sweep1_kernel(ctl_ref, pin_ref, xe_ref, xo_ref, yb_ref, ya_ref, r_ref, dinv_ref, coef_ref, react_ref,
                  cf_ref, cz_ref, rz_ref, grad_ref, back_ref, gz_ref, bz_ref, gf_ref, bf_ref,
                  a1_ref, p_ref, even, odd, low_y, high_y, s_ref, fv_ref, st_ref):
    image = take_sum(pin_ref, (*pick(ctl_ref, xe_ref[...], xo_ref[...]), yb_ref[...], ya_ref[...]), s_ref)
    dinv, r = dinv_ref[...], r_ref[...]
    a0 = dinv * r * (1.0 / CENTER)
    a1 = (1.0 + MIX1) * a0 + GAIN1 * (dinv * (r - image))
    a1_ref[...] = a1
    lines = corner_lines(a1_ref, cf_ref[...], cz_ref[...], rz_ref[...], fv_ref, gf_ref, bf_ref, gz_ref[...], bz_ref[...])
    f = local_op(a1, coef_ref[...], react_ref[...], grad_ref, back_ref, gz_ref[...], bz_ref[...])
    emit_partial(f, lines, ctl_ref, p_ref, (even, odd, low_y, high_y), st_ref)


def sweep2(image, a1, r, dinv):
    a0 = dinv * r * (1.0 / CENTER)
    return a1 + (MIX2 * (a1 - a0) + GAIN2 * (dinv * (r - image)))


def third_kernel(ctl_ref, pin_ref, xe_ref, xo_ref, yb_ref, ya_ref, r_ref, dinv_ref, a1_ref, load_ref, coef_ref, react_ref,
                 cf_ref, cz_ref, rz_ref, grad_ref, back_ref, gz_ref, bz_ref, gf_ref, bf_ref,
                 z_ref, p_ref, even, odd, low_y, high_y, dots_ref, s_ref, fv_ref, st_ref):
    image = take_sum(pin_ref, (*pick(ctl_ref, xe_ref[...], xo_ref[...]), yb_ref[...], ya_ref[...]), s_ref)
    z = sweep2(image, a1_ref[...], r_ref[...], dinv_ref[...])
    z_ref[...] = z
    dots_ref[0] = fold(load_ref[...].reshape(ROWS, COLS) * z)
    lines = corner_lines(z_ref, cf_ref[...], cz_ref[...], rz_ref[...], fv_ref, gf_ref, bf_ref, gz_ref[...], bz_ref[...])
    f = local_op(z, coef_ref[...], react_ref[...], grad_ref, back_ref, gz_ref[...], bz_ref[...])
    dots_ref[1] = fold(f * z)
    emit_partial(f, lines, ctl_ref, p_ref, (even, odd, low_y, high_y), st_ref)


def fourth_kernel(ctl_ref, pin_ref, xe_ref, xo_ref, yb_ref, ya_ref, dinv_ref, z_ref, coef_ref, react_ref,
                  cf_ref, cz_ref, rz_ref, grad_ref, back_ref, gz_ref, bz_ref, gf_ref, bf_ref,
                  im_ref, p_ref, even, odd, low_y, high_y, dots_ref, s_ref, fv_ref, st_ref):
    image = take_sum(pin_ref, (*pick(ctl_ref, xe_ref[...], xo_ref[...]), yb_ref[...], ya_ref[...]), s_ref)
    dinv = dinv_ref[...]
    im = jnp.where(dinv != 0.0, image, 0.0)
    im_ref[...] = im
    b0 = dinv * im * (1.0 / CENTER)
    s_ref[...] = b0
    lines = corner_lines(s_ref, cf_ref[...], cz_ref[...], rz_ref[...], fv_ref, gf_ref, bf_ref, gz_ref[...], bz_ref[...])
    f = local_op(b0, coef_ref[...], react_ref[...], grad_ref, back_ref, gz_ref[...], bz_ref[...])
    dots_ref[...] = fold(f * z_ref[...])
    emit_partial(f, lines, ctl_ref, p_ref, (even, odd, low_y, high_y), st_ref)


def fifth_kernel(ctl_ref, pin_ref, xe_ref, xo_ref, yb_ref, ya_ref, im_ref, dinv_ref, z_ref, d34_ref, d5_ref, coef_ref, react_ref,
                 cf_ref, cz_ref, rz_ref, grad_ref, back_ref, gz_ref, bz_ref, gf_ref, bf_ref,
                 b1_ref, p_ref, even, odd, low_y, high_y, dots_ref, s_ref, fv_ref, st_ref):
    image = take_sum(pin_ref, (*pick(ctl_ref, xe_ref[...], xo_ref[...]), yb_ref[...], ya_ref[...]), s_ref)
    dinv, im = dinv_ref[...], im_ref[...]
    b0 = dinv * im * (1.0 / CENTER)
    b1 = (1.0 + MIX1) * b0 + GAIN1 * (dinv * (im - image))
    b1_ref[...] = b1
    lines = corner_lines(b1_ref, cf_ref[...], cz_ref[...], rz_ref[...], fv_ref, gf_ref, bf_ref, gz_ref[...], bz_ref[...])
    f = local_op(b1, coef_ref[...], react_ref[...], grad_ref, back_ref, gz_ref[...], bz_ref[...])
    emit_partial(f, lines, ctl_ref, p_ref, (even, odd, low_y, high_y), st_ref)
    last = fold(f * ((1.0 + MIX2) * z_ref[...] - (CENTER * GAIN2) * b0))
    both = last + (CENTER * GAIN2 - MIX2) * d5_ref[...]
    lane = lax.broadcasted_iota(jnp.int32, (1, 128), 1)
    sums = jnp.where(
        lane == 0, jnp.sum(d34_ref[0]), jnp.where(lane == 1, jnp.sum(d34_ref[1]), jnp.sum(both)))
    dots_ref[...] = jnp.broadcast_to(sums, dots_ref.shape)


def last_kernel(dots_ref, ctl_ref, pin_ref, xe_ref, xo_ref, yb_ref, ya_ref, im_ref, dinv_ref, b1_ref, z_ref, r_ref,
                sol_hbm, res_hbm, dir_hbm, s_ref, sol_ref, res_ref, dir_ref, sems):
    first, curv, quad = dots_ref[0], dots_ref[1], dots_ref[2]
    step = first / curv
    ratio = (first - 2.0 * step * curv + step * step * quad) / first
    shape = (16, 16, COLS)
    copies = [pltpu.make_async_copy(src, dst, sems.at[i])
              for i, (src, dst) in enumerate(((sol_ref, sol_hbm), (res_ref, res_hbm), (dir_ref, dir_hbm)))]
    z, im = z_ref[...], im_ref[...]
    sol_ref[...] = (step * z).reshape(shape)
    copies[0].start()
    res_ref[...] = (r_ref[...] - step * im).reshape(shape)
    copies[1].start()
    image = take_sum(pin_ref, (*pick(ctl_ref, xe_ref[...], xo_ref[...]), yb_ref[...], ya_ref[...]), s_ref)
    b2 = sweep2(image, b1_ref[...], im, dinv_ref[...])
    dir_ref[...] = ((z - step * b2) + ratio * z).reshape(shape)
    copies[2].start()
    for copy in copies:
        copy.wait()


VM = pl.BlockSpec(memory_space=pltpu.VMEM)
SM = pl.BlockSpec(memory_space=pltpu.SMEM)
HB = pl.BlockSpec(memory_space=pl.ANY)
BIG = jax.ShapeDtypeStruct((ROWS, COLS), F32)
FACE = jax.ShapeDtypeStruct((16, COLS), F32)
PART = (BIG, FACE, FACE, FACE, FACE)
MESSAGE = jax.ShapeDtypeStruct((56, COLS), F32)
PARAMS = pltpu.CompilerParams(vmem_limit_bytes=24 << 20)


def call(kernel, outs, specs, scratch):
    return pl.pallas_call(
        kernel, out_shape=outs, in_specs=specs, out_specs=jax.tree.map(lambda _: VM, outs),
        scratch_shapes=scratch, compiler_params=PARAMS)


def step_call(kernel, outs, n_in):
    scratch = [pltpu.VMEM((rows, COLS), F32) for rows in (ROWS, 64, 32)]
    return call(kernel, outs, [VM] * (n_in + 1), scratch)


def swaps(first, count):
    pairs = [(i, i + 1) for i in range(first, count - 1, 2)]
    return pairs + [(j, i) for i, j in pairs]


def per_device(load, conductivity, flags, region, kappa_table):
    k = {name: jnp.asarray(value) for name, value in constants().items()}
    n_x, n_y = lax.axis_size("gx"), lax.axis_size("gy")
    at_x, at_y = lax.axis_index("gx"), lax.axis_index("gy")
    ctl = jnp.stack([at_x % 2 == 1, at_y != 0, at_y != n_y - 1, at_y < 0]).astype(F32)
    ctl = jnp.broadcast_to(ctl[:, None], (4, COLS))
    up_y = [(i, (i + 1) % n_y) for i in range(n_y)]
    down_y = [(j, i) for i, j in up_y]

    def along_x(even, odd):
        return lax.ppermute(even, "gx", swaps(0, n_x)), lax.ppermute(odd, "gx", swaps(1, n_x))

    def along_y(low, high):
        return lax.ppermute(high, "gy", up_y), lax.ppermute(low, "gy", down_y)

    def exchange(faces):
        even, odd, low_y, high_y = faces
        return (*along_x(even, odd), *along_y(low_y, high_y))

    keep_shape = jax.ShapeDtypeStruct((ROWS, 128), F32)
    inputs = (kappa_table, load, conductivity, flags, region, k["sq"], k["sq_z"], k["w_rows"], k["w_z"],
              k["grad_f"], k["back_f"])
    inputs = tuple(pltpu.with_memory_space_constraint(v, pltpu.HBM) for v in inputs)
    buffers = [pltpu.VMEM(v.shape, v.dtype) for v in inputs[:9]]
    buffers[0] = pltpu.SMEM(kappa_table.shape, F32)
    buffers[3] = pltpu.VMEM((16, 16, 128), jnp.int32)
    buffers += [pltpu.SemaphoreType.DMA((len(inputs),)), pltpu.VMEM((2, 56, COLS), F32)]
    small = tuple(jax.ShapeDtypeStruct(v.shape, v.dtype) for v in inputs[9:])
    coef, react, keep, part_l, part_d, even, odd, low_y, high_y, grad_f, back_f = call(
        first_kernel, (BIG, BIG, keep_shape, BIG, BIG) + (MESSAGE,) * 4 + small, [VM] + [HB] * len(inputs),
        buffers)(ctl, *inputs)
    mats = (k["grad"], k["back"], k["grad_z"], k["back_z"], grad_f, back_f)
    even, odd = along_x(even, odd)
    low_y, high_y = call(corner_kernel, (MESSAGE, MESSAGE), [VM] * 5, [pltpu.VMEM((2, 56, COLS), F32)])(
        ctl, even, odd, low_y, high_y)
    recv = (even, odd, *along_y(low_y, high_y))
    line = jax.ShapeDtypeStruct((8, COLS), F32)
    r, dinv, cf, cz, rz, part, *faces = step_call(
        second_kernel, (BIG, BIG, jax.ShapeDtypeStruct((64, COLS), F32), line, line) + PART, 15)(
        ctl, part_l, part_d, *recv, keep, coef, react, *mats)
    tail = (coef, react, cf, cz, rz, *mats)
    recv = exchange(faces)
    a1, part, *faces = step_call(sweep1_kernel, (BIG,) + PART, 18)(ctl, part, *recv, r, dinv, *tail)
    recv = exchange(faces)
    d34_shape = jax.ShapeDtypeStruct((2, 8, 128), F32)
    z, part, *faces, d34 = step_call(third_kernel, (BIG,) + PART + (d34_shape,), 20)(
        ctl, part, *recv, r, dinv, a1, load, *tail)
    recv = exchange(faces)
    d5_shape = jax.ShapeDtypeStruct((8, 128), F32)
    im, part, *faces, d5 = step_call(fourth_kernel, (BIG,) + PART + (d5_shape,), 18)(
        ctl, part, *recv, dinv, z, *tail)
    recv = exchange(faces)
    dots_shape = jax.ShapeDtypeStruct((n_y, 128), F32)
    b1, part, *faces, dots = step_call(fifth_kernel, (BIG,) + PART + (dots_shape,), 21)(
        ctl, part, *recv, im, dinv, z, d34, d5, *tail)
    total = lax.all_to_all(dots, "gy", 0, 0, tiled=True).sum(0)
    recv = exchange(faces)
    total = lax.all_to_all(jnp.broadcast_to(total, (n_x, 128)), "gx", 0, 0, tiled=True).sum(0)
    shape = jax.ShapeDtypeStruct((16, 16, COLS), F32)
    scratch = [pltpu.VMEM((ROWS, COLS), F32)] + [pltpu.VMEM((16, 16, COLS), F32)] * 3 + [pltpu.SemaphoreType.DMA((3,))]
    return pl.pallas_call(
        last_kernel, out_shape=(shape, shape, shape), in_specs=[SM] + [VM] * 11, out_specs=(HB, HB, HB),
        scratch_shapes=scratch, compiler_params=PARAMS)(total, ctl, part, *recv, im, dinv, b1, z, r)


def solution(mesh):
    placed = P("gx", "gy", None)
    return jax.shard_map(
        per_device,
        mesh=mesh,
        in_specs=(placed, placed, placed, placed, P()),
        out_specs=(placed, placed, placed),
        check_vma=False,
    )
```

```python
import jax
import jax.numpy as jnp
import ml_dtypes
import numpy as np
from jax import lax
from jax.experimental import pallas as pl
from jax.experimental.pallas import tpu as pltpu
from jax.sharding import PartitionSpec as P

NREG = 3
CENTER = 24.0
HALF = 23.0
RHO0 = HALF / CENTER
RHO1 = 1.0 / (2.0 * CENTER / HALF - RHO0)
RHO2 = 1.0 / (2.0 * CENTER / HALF - RHO1)
MIX1, GAIN1 = RHO1 * RHO0, 2.0 * RHO1 / HALF
MIX2, GAIN2 = RHO2 * RHO1, 2.0 * RHO2 / HALF

F32 = jnp.float32
BF16 = jnp.bfloat16
ROWS, COLS = 256, 512


def gll_tables():
    nodes = np.array(
        [
            -1.0,
            -0.8717401485096066,
            -0.5917001814331423,
            -0.2092992179024789,
            0.2092992179024789,
            0.5917001814331423,
            0.8717401485096066,
            1.0,
        ]
    )
    prev = np.ones(8)
    now = nodes.copy()
    for degree in range(1, 7):
        prev, now = now, ((2 * degree + 1) * nodes * now - degree * prev) / (degree + 1)
    weights = 2.0 / (56.0 * now**2)
    table = np.zeros((8, 8))
    for a in range(8):
        for b in range(8):
            if a != b:
                table[a, b] = now[a] / (now[b] * (nodes[a] - nodes[b]))
    table[0, 0] = -14.0
    table[7, 7] = 14.0
    return table, weights


def split_np(mat):
    high = mat.astype(ml_dtypes.bfloat16)
    low = (mat - high.astype(np.float64)).astype(ml_dtypes.bfloat16)
    return high, low


def left_pair(mat):
    high, low = split_np(mat)
    return np.stack([np.concatenate([high, high], 1), np.concatenate([low, low], 1)])


def right_pair(mat):
    high, low = split_np(mat)
    both = np.concatenate([high, low], 1)
    return np.concatenate([both, both], 0)


def constants():
    table, weights = gll_tables()
    table = table.astype(np.float32).astype(np.float64)
    weights = weights.astype(np.float32)
    eye8, eye2, eye16 = np.eye(8), np.eye(2), np.eye(16)
    d_x = np.kron(table, eye16)
    d_y = np.kron(eye8, np.kron(eye2, table))
    square = (table * table).astype(np.float32).astype(np.float64)
    q_x = np.kron(square, eye16)
    q_y = np.kron(eye8, np.kron(eye2, square))
    d_z = np.kron(eye16, table)
    q_z = np.kron(eye16, square)
    grad = left_pair(np.concatenate([d_x, d_y], 0))
    back_h, back_l = split_np(np.concatenate([d_x.T, d_y.T], 1))
    back = np.stack([back_h, back_l])
    sq = left_pair(q_x.T + q_y.T)
    grad_z = right_pair(d_z.T)
    back_z = right_pair(d_z)
    sq_z = right_pair(q_z)
    lines = np.zeros((8, 64))
    for face in range(4):
        lines[2 * face, 16 * face:16 * face + 8] = table[:, 0]
        lines[2 * face + 1, 16 * face + 8:16 * face + 16] = table[:, 7]
    grad_f = left_pair(np.kron(np.eye(8), table))
    back_f = left_pair(lines)
    w_xy = (weights[:, None] * weights[None, :]).astype(np.float32)
    w_xy = np.tile(w_xy, (2, 2)).reshape(ROWS, 1)
    w_rows = np.ascontiguousarray(np.broadcast_to(w_xy, (ROWS, 128)))
    w_z = np.tile(weights, COLS // 8).reshape(1, COLS).astype(np.float32)
    return dict(grad=grad, back=back, sq=sq, grad_z=grad_z, back_z=back_z, grad_f=grad_f, back_f=back_f, sq_z=sq_z, w_rows=w_rows, w_z=w_z)


def dot(a, b):
    return lax.dot_general(a, b, (((1,), (0,)), ((), ())), preferred_element_type=F32)


def halves(v):
    high = v.astype(BF16)
    low = (v - high.astype(F32)).astype(BF16)
    return high, low


def mul_z(high, low, mat):
    outs = []
    for k in range(COLS // 128):
        part = slice(128 * k, 128 * (k + 1))
        both = dot(jnp.concatenate([high[:, part], low[:, part]], 1), mat)
        outs.append(both[:, :128] + both[:, 128:])
    return jnp.concatenate(outs, 1)


def local_op(v, coef, react, grad, back, grad_z, back_z):
    high, low = halves(v)
    rows = []
    for e in range(2):
        part = slice(128 * e, 128 * (e + 1))
        pair = jnp.concatenate([high[part], low[part]], 0)
        flux = dot(grad[0], pair) + dot(grad[1], pair)
        c = coef[part]
        f_h, f_l = halves(flux * jnp.concatenate([c, c], 0))
        rows.append(dot(back[0], f_h) + (dot(back[0], f_l) + dot(back[1], f_h)))
    out = jnp.concatenate(rows, 0)
    flux_z = mul_z(high, low, grad_z) * coef
    return out + mul_z(*halves(flux_z), back_z) + react * v


def join_z(f):
    lane = lax.broadcasted_iota(jnp.int32, (1, COLS), 1)
    upper = ((lane % 8) == 7) & (lane != COLS - 1)
    lower = ((lane % 8) == 0) & (lane != 0)
    nxt = pltpu.roll(f, COLS - 1, 1)
    prv = pltpu.roll(f, 1, 1)
    return f + jnp.where(upper, nxt, jnp.where(lower, prv, 0.0))


def corner_lines(v_ref, cf, cz, rz, fv_ref, grad_f, back_f, grad_z, back_z):
    for x in range(16):
        r = 16 * x
        fv_ref[x:x + 1, :] = v_ref[r + 15:r + 16, :]
        fv_ref[16 + x:17 + x, :] = v_ref[r:r + 1, :]
    fv_ref[32:48, :] = v_ref[240:256, :]
    fv_ref[48:64, :] = v_ref[0:16, :]
    pair = jnp.concatenate(halves(fv_ref[...]), 0)
    flux = (dot(grad_f[0], pair) + dot(grad_f[1], pair)) * cf
    pair = jnp.concatenate(halves(flux), 0)
    ends = dot(back_f[0], pair) + dot(back_f[1], pair)
    for row, r in enumerate((255, 15, 240, 0, 255, 15, 240, 0)):
        fv_ref[row:row + 1, :] = v_ref[r:r + 1, :]
    at = fv_ref[0:8, :]
    flux_z = mul_z(*halves(at), grad_z) * cz
    return join_z(jnp.concatenate([ends, mul_z(*halves(flux_z), back_z) + rz * at], 0))


def join_rows(f, p_ref):
    p_ref[...] = join_z(f)
    p_ref[112:128, :] = p_ref[112:128, :] + p_ref[128:144, :]
    p_ref[128:144, :] = p_ref[112:128, :]
    for x in range(16):
        r = 16 * x
        mid = p_ref[r + 7:r + 8, :] + p_ref[r + 8:r + 9, :]
        p_ref[r + 7:r + 8, :] = mid
        p_ref[r + 8:r + 9, :] = mid


def put_y(p_ref, low, high, base):
    for x in range(16):
        r = 16 * x
        low[base + x:base + x + 1, :] = p_ref[r:r + 1, :]
        high[base + x:base + x + 1, :] = p_ref[r + 15:r + 16, :]


def add_row(ref, row, line):
    ref[row:row + 1, :] = ref[row:row + 1, :] + line


def emit_partial(f, lines, ctl_ref, p_ref, faces, st_ref):
    even, odd, low_y, high_y = faces
    join_rows(f, p_ref)
    st_ref[0:16, :] = p_ref[0:16, :]
    st_ref[16:32, :] = p_ref[240:256, :]
    put_y(p_ref, low_y, high_y, 0)
    ln = [lines[i:i + 1] for i in range(12)]
    add_row(st_ref, 15, ln[0])
    add_row(st_ref, 31, ln[1])
    add_row(st_ref, 0, ln[2])
    add_row(st_ref, 16, ln[3])
    add_row(low_y, 15, ln[4])
    add_row(high_y, 15, ln[5])
    add_row(low_y, 0, ln[6])
    add_row(high_y, 0, ln[7])
    for i, r in enumerate((255, 15, 240, 0)):
        add_row(p_ref, r, ln[8 + i])
    is_odd = ctl_ref[0:1, :] > 0.5
    low, high = st_ref[0:16, :], st_ref[16:32, :]
    even[...] = jnp.where(is_odd, low, high)
    odd[...] = jnp.where(is_odd, high, low)
    low_y[...] = ctl_ref[1:2, :] * low_y[...]
    high_y[...] = ctl_ref[2:3, :] * high_y[...]


def pick(ctl_ref, even, odd):
    is_odd = ctl_ref[0:1, :] > 0.5
    return jnp.where(is_odd, even, odd), jnp.where(is_odd, odd, even)


def take_sum(p_ref, recv, s_ref):
    left, right, below, above = recv
    s_ref[...] = p_ref[...]
    s_ref[0:16, :] = s_ref[0:16, :] + left
    s_ref[240:256, :] = s_ref[240:256, :] + right
    for x in range(16):
        r = 16 * x
        s_ref[r:r + 1, :] = s_ref[r:r + 1, :] + below[x:x + 1, :]
        s_ref[r + 15:r + 16, :] = s_ref[r + 15:r + 16, :] + above[x:x + 1, :]
    return s_ref[...]


def fold(prod):
    part = prod.reshape(ROWS // 8, 8, COLS).sum(axis=0)
    return part[:, 0:128] + part[:, 128:256] + part[:, 256:384] + part[:, 384:512]


def first_kernel(ctl_ref, table_hbm, load_hbm, cond_hbm, flags_hbm, region_hbm, sq_hbm, sqz_hbm, wr_hbm, wz_hbm,
                 gf_hbm, bf_hbm,
                 coef_ref, react_ref, keep_ref, pl_ref, pd_ref, even_ref, odd_ref, yl_ref, yh_ref, gf_ref, bf_ref,
                 table_ref, load_ref, cond_ref, flags_ref, region_ref, sq_ref, sqz_ref, wr_ref, wz_ref, sems, st_ref):
    flags_tile = flags_hbm.at[:, :, pl.ds(0, 128)]
    pairs = ((cond_hbm, cond_ref), (wr_hbm, wr_ref), (wz_hbm, wz_ref), (region_hbm, region_ref), (table_hbm, table_ref),
             (sq_hbm, sq_ref), (sqz_hbm, sqz_ref), (load_hbm, load_ref), (flags_tile, flags_ref),
             (gf_hbm, gf_ref), (bf_hbm, bf_ref))
    copies = [pltpu.make_async_copy(src, dst, sems.at[i]) for i, (src, dst) in enumerate(pairs)]
    for copy in copies:
        copy.start()
    for copy in copies[:5]:
        copy.wait()
    w_row = wr_ref[...]
    w_row = jnp.concatenate([w_row] * 4, axis=1)
    quad_z = wz_ref[...]
    coef = (w_row * quad_z) * cond_ref[...].reshape(ROWS, COLS).astype(F32)
    coef_ref[...] = coef
    elem = lax.broadcasted_iota(jnp.int32, (COLS // 8, COLS), 0)
    lane = lax.broadcasted_iota(jnp.int32, (COLS // 8, COLS), 1)
    spread = (lane // 8 == elem).astype(F32)
    for ex in range(2):
        ids = region_ref[ex]
        kappa = jnp.zeros(ids.shape, F32)
        for k in range(NREG):
            kappa = kappa + jnp.where(ids == k, table_ref[k], 0.0)
        kappa = lax.dot_general(kappa, spread, (((1,), (0,)), ((), ())),
                                precision=lax.Precision.HIGHEST, preferred_element_type=F32)
        for x in range(8):
            for ey in range(2):
                r = (ex * 8 + x) * 16 + ey * 8
                react_ref[r:r + 8, :] = (w_row[r:r + 8] * quad_z) * kappa[ey:ey + 1, :]
    for copy in copies[5:]:
        copy.wait()
    keep_ref[...] = (1 - flags_ref[...].reshape(ROWS, 128)).astype(F32)
    high, low = halves(coef)
    rows = []
    for e in range(2):
        part = slice(128 * e, 128 * (e + 1))
        pair = jnp.concatenate([high[part], low[part]], 0)
        rows.append(dot(sq_ref[0], pair) + dot(sq_ref[1], pair))
    diag = jnp.concatenate(rows, 0) + mul_z(high, low, sqz_ref[...]) + react_ref[...]
    join_rows(load_ref[...].reshape(ROWS, COLS), pl_ref)
    join_rows(diag, pd_ref)
    for i, src in enumerate((pl_ref, pd_ref, coef_ref)):
        st_ref[0, 16 * i:16 * i + 16, :] = src[0:16, :]
        st_ref[1, 16 * i:16 * i + 16, :] = src[240:256, :]
        put_y(src, yl_ref, yh_ref, 16 * i)
    zeros = jnp.zeros((8, COLS), F32)
    for side, r in enumerate((0, 240)):
        st_ref[side, 48:56, :] = zeros
        st_ref[side, 48:49, :] = react_ref[r:r + 1, :]
        st_ref[side, 49:50, :] = react_ref[r + 15:r + 16, :]
    yl_ref[48:56, :] = zeros
    yh_ref[48:56, :] = zeros
    is_odd = ctl_ref[0:1, :] > 0.5
    even_ref[...] = jnp.where(is_odd, st_ref[0], st_ref[1])
    odd_ref[...] = jnp.where(is_odd, st_ref[1], st_ref[0])


def corner_kernel(ctl_ref, even_ref, odd_ref, lin_ref, hin_ref, low_ref, high_ref, x_ref):
    x_ref[0], x_ref[1] = pick(ctl_ref, even_ref[...], odd_ref[...])
    for src, out, row in ((lin_ref, low_ref, 0), (hin_ref, high_ref, 15)):
        out[...] = src[...]
        for base in (0, 16):
            add_row(out, base, x_ref[0, base + row:base + row + 1, :])
            add_row(out, base + 15, x_ref[1, base + row:base + row + 1, :])
        line = 48 if row == 0 else 49
        out[48:49, :] = x_ref[0, 32 + row:33 + row, :]
        out[49:50, :] = x_ref[1, 32 + row:33 + row, :]
        out[50:51, :] = x_ref[0, line:line + 1, :]
        out[51:52, :] = x_ref[1, line:line + 1, :]
    low_ref[...] = ctl_ref[1:2, :] * low_ref[...]
    high_ref[...] = ctl_ref[2:3, :] * high_ref[...]


def second_kernel(ctl_ref, pl_ref, pd_ref, xe_ref, xo_ref, yb_ref, ya_ref, keep_ref, coef_ref, react_ref,
                  grad_ref, back_ref, gz_ref, bz_ref, gf_ref, bf_ref,
                  r_ref, dinv_ref, cf_ref, cz_ref, rz_ref, p_ref, even, odd, low_y, high_y, s_ref, fv_ref, st_ref):
    left, right = pick(ctl_ref, xe_ref[...], xo_ref[...])
    below, above = yb_ref[...], ya_ref[...]
    diag = take_sum(pd_ref, (left[16:32], right[16:32], below[16:32], above[16:32]), s_ref)
    dinv_ref[...] = 1.0 / diag
    keep = keep_ref[...]
    dinv_ref[:, 0:128] = keep * dinv_ref[:, 0:128]
    r = take_sum(pl_ref, (left[0:16], right[0:16], below[0:16], above[0:16]), s_ref)
    r_ref[...] = r
    r_ref[:, 0:128] = keep * r_ref[:, 0:128]
    cf_ref[0:16, :] = above[32:48]
    cf_ref[16:32, :] = below[32:48]
    cf_ref[32:48, :] = right[32:48]
    cf_ref[48:64, :] = left[32:48]
    for out, base in ((cz_ref, 48), (rz_ref, 50)):
        out[0:1, :] = above[base + 1:base + 2]
        out[1:2, :] = above[base:base + 1]
        out[2:3, :] = below[base + 1:base + 2]
        out[3:4, :] = below[base:base + 1]
        out[4:8, :] = jnp.zeros((4, COLS), F32)
    a0 = dinv_ref[...] * r_ref[...] * (1.0 / CENTER)
    s_ref[...] = a0
    lines = corner_lines(s_ref, cf_ref[...], cz_ref[...], rz_ref[...], fv_ref, gf_ref, bf_ref, gz_ref[...], bz_ref[...])
    f = local_op(a0, coef_ref[...], react_ref[...], grad_ref, back_ref, gz_ref[...], bz_ref[...])
    emit_partial(f, lines, ctl_ref, p_ref, (even, odd, low_y, high_y), st_ref)


def sweep1_kernel(ctl_ref, pin_ref, xe_ref, xo_ref, yb_ref, ya_ref, r_ref, dinv_ref, coef_ref, react_ref,
                  cf_ref, cz_ref, rz_ref, grad_ref, back_ref, gz_ref, bz_ref, gf_ref, bf_ref,
                  a1_ref, p_ref, even, odd, low_y, high_y, s_ref, fv_ref, st_ref):
    image = take_sum(pin_ref, (*pick(ctl_ref, xe_ref[...], xo_ref[...]), yb_ref[...], ya_ref[...]), s_ref)
    dinv, r = dinv_ref[...], r_ref[...]
    a0 = dinv * r * (1.0 / CENTER)
    a1 = (1.0 + MIX1) * a0 + GAIN1 * (dinv * (r - image))
    a1_ref[...] = a1
    lines = corner_lines(a1_ref, cf_ref[...], cz_ref[...], rz_ref[...], fv_ref, gf_ref, bf_ref, gz_ref[...], bz_ref[...])
    f = local_op(a1, coef_ref[...], react_ref[...], grad_ref, back_ref, gz_ref[...], bz_ref[...])
    emit_partial(f, lines, ctl_ref, p_ref, (even, odd, low_y, high_y), st_ref)


def sweep2(image, a1, r, dinv):
    a0 = dinv * r * (1.0 / CENTER)
    return a1 + (MIX2 * (a1 - a0) + GAIN2 * (dinv * (r - image)))


def third_kernel(ctl_ref, pin_ref, xe_ref, xo_ref, yb_ref, ya_ref, r_ref, dinv_ref, a1_ref, load_ref, coef_ref, react_ref,
                 cf_ref, cz_ref, rz_ref, grad_ref, back_ref, gz_ref, bz_ref, gf_ref, bf_ref,
                 z_ref, p_ref, even, odd, low_y, high_y, dots_ref, s_ref, fv_ref, st_ref):
    image = take_sum(pin_ref, (*pick(ctl_ref, xe_ref[...], xo_ref[...]), yb_ref[...], ya_ref[...]), s_ref)
    z = sweep2(image, a1_ref[...], r_ref[...], dinv_ref[...])
    z_ref[...] = z
    dots_ref[0] = fold(load_ref[...].reshape(ROWS, COLS) * z)
    lines = corner_lines(z_ref, cf_ref[...], cz_ref[...], rz_ref[...], fv_ref, gf_ref, bf_ref, gz_ref[...], bz_ref[...])
    f = local_op(z, coef_ref[...], react_ref[...], grad_ref, back_ref, gz_ref[...], bz_ref[...])
    dots_ref[1] = fold(f * z)
    emit_partial(f, lines, ctl_ref, p_ref, (even, odd, low_y, high_y), st_ref)


def fourth_kernel(ctl_ref, pin_ref, xe_ref, xo_ref, yb_ref, ya_ref, dinv_ref, z_ref, coef_ref, react_ref,
                  cf_ref, cz_ref, rz_ref, grad_ref, back_ref, gz_ref, bz_ref, gf_ref, bf_ref,
                  im_ref, p_ref, even, odd, low_y, high_y, dots_ref, s_ref, fv_ref, st_ref):
    image = take_sum(pin_ref, (*pick(ctl_ref, xe_ref[...], xo_ref[...]), yb_ref[...], ya_ref[...]), s_ref)
    dinv = dinv_ref[...]
    im = jnp.where(dinv != 0.0, image, 0.0)
    im_ref[...] = im
    b0 = dinv * im * (1.0 / CENTER)
    s_ref[...] = b0
    lines = corner_lines(s_ref, cf_ref[...], cz_ref[...], rz_ref[...], fv_ref, gf_ref, bf_ref, gz_ref[...], bz_ref[...])
    f = local_op(b0, coef_ref[...], react_ref[...], grad_ref, back_ref, gz_ref[...], bz_ref[...])
    dots_ref[...] = fold(f * z_ref[...])
    emit_partial(f, lines, ctl_ref, p_ref, (even, odd, low_y, high_y), st_ref)


def fifth_kernel(ctl_ref, pin_ref, xe_ref, xo_ref, yb_ref, ya_ref, im_ref, dinv_ref, z_ref, d34_ref, d5_ref, coef_ref, react_ref,
                 cf_ref, cz_ref, rz_ref, grad_ref, back_ref, gz_ref, bz_ref, gf_ref, bf_ref,
                 b1_ref, p_ref, even, odd, low_y, high_y, dots_ref, s_ref, fv_ref, st_ref):
    image = take_sum(pin_ref, (*pick(ctl_ref, xe_ref[...], xo_ref[...]), yb_ref[...], ya_ref[...]), s_ref)
    dinv, im = dinv_ref[...], im_ref[...]
    b0 = dinv * im * (1.0 / CENTER)
    b1 = (1.0 + MIX1) * b0 + GAIN1 * (dinv * (im - image))
    b1_ref[...] = b1
    lines = corner_lines(b1_ref, cf_ref[...], cz_ref[...], rz_ref[...], fv_ref, gf_ref, bf_ref, gz_ref[...], bz_ref[...])
    f = local_op(b1, coef_ref[...], react_ref[...], grad_ref, back_ref, gz_ref[...], bz_ref[...])
    emit_partial(f, lines, ctl_ref, p_ref, (even, odd, low_y, high_y), st_ref)
    last = fold(f * ((1.0 + MIX2) * z_ref[...] - (CENTER * GAIN2) * b0))
    both = last + (CENTER * GAIN2 - MIX2) * d5_ref[...]
    lane = lax.broadcasted_iota(jnp.int32, (1, 128), 1)
    rows = [part.sum(axis=0, keepdims=True) for part in (d34_ref[0], d34_ref[1], both)]
    sums = jnp.sum(jnp.concatenate(rows + [jnp.zeros((5, 128), F32)], 0), axis=1, keepdims=True)
    sums = jnp.where(lane == 0, sums[0:1], jnp.where(lane == 1, sums[1:2], sums[2:3]))
    dots_ref[...] = jnp.broadcast_to(sums, dots_ref.shape)


def last_kernel(dots_ref, ctl_ref, pin_ref, xe_ref, xo_ref, yb_ref, ya_ref, im_ref, dinv_ref, b1_ref, z_ref, r_ref,
                sol_hbm, res_hbm, dir_hbm, s_ref, sol_ref, res_ref, dir_ref, sems):
    first, curv, quad = dots_ref[0], dots_ref[1], dots_ref[2]
    step = first / curv
    ratio = (first - 2.0 * step * curv + step * step * quad) / first
    shape = (16, 16, COLS)
    copies = [pltpu.make_async_copy(src, dst, sems.at[i])
              for i, (src, dst) in enumerate(((sol_ref, sol_hbm), (res_ref, res_hbm), (dir_ref, dir_hbm)))]
    z, im = z_ref[...], im_ref[...]
    sol_ref[...] = (step * z).reshape(shape)
    copies[0].start()
    res_ref[...] = (r_ref[...] - step * im).reshape(shape)
    copies[1].start()
    image = take_sum(pin_ref, (*pick(ctl_ref, xe_ref[...], xo_ref[...]), yb_ref[...], ya_ref[...]), s_ref)
    b2 = sweep2(image, b1_ref[...], im, dinv_ref[...])
    dir_ref[...] = ((z - step * b2) + ratio * z).reshape(shape)
    copies[2].start()
    for copy in copies:
        copy.wait()


VM = pl.BlockSpec(memory_space=pltpu.VMEM)
SM = pl.BlockSpec(memory_space=pltpu.SMEM)
HB = pl.BlockSpec(memory_space=pl.ANY)
BIG = jax.ShapeDtypeStruct((ROWS, COLS), F32)
FACE = jax.ShapeDtypeStruct((16, COLS), F32)
PART = (BIG, FACE, FACE, FACE, FACE)
MESSAGE = jax.ShapeDtypeStruct((56, COLS), F32)
PARAMS = pltpu.CompilerParams(vmem_limit_bytes=24 << 20)


def call(kernel, outs, specs, scratch):
    return pl.pallas_call(
        kernel, out_shape=outs, in_specs=specs, out_specs=jax.tree.map(lambda _: VM, outs),
        scratch_shapes=scratch, compiler_params=PARAMS)


def step_call(kernel, outs, n_in):
    scratch = [pltpu.VMEM((rows, COLS), F32) for rows in (ROWS, 64, 32)]
    return call(kernel, outs, [VM] * (n_in + 1), scratch)


def swaps(first, count):
    pairs = [(i, i + 1) for i in range(first, count - 1, 2)]
    return pairs + [(j, i) for i, j in pairs]


def per_device(load, conductivity, flags, region, kappa_table):
    k = {name: jnp.asarray(value) for name, value in constants().items()}
    n_x, n_y = lax.axis_size("gx"), lax.axis_size("gy")
    at_x, at_y = lax.axis_index("gx"), lax.axis_index("gy")
    ctl = jnp.stack([at_x % 2 == 1, at_y != 0, at_y != n_y - 1, at_y < 0]).astype(F32)
    ctl = jnp.broadcast_to(ctl[:, None], (4, COLS))
    up_y = [(i, (i + 1) % n_y) for i in range(n_y)]
    down_y = [(j, i) for i, j in up_y]

    def along_x(even, odd):
        return lax.ppermute(even, "gx", swaps(0, n_x)), lax.ppermute(odd, "gx", swaps(1, n_x))

    def along_y(low, high):
        return lax.ppermute(high, "gy", up_y), lax.ppermute(low, "gy", down_y)

    def exchange(faces):
        even, odd, low_y, high_y = faces
        return (*along_x(even, odd), *along_y(low_y, high_y))

    keep_shape = jax.ShapeDtypeStruct((ROWS, 128), F32)
    inputs = (kappa_table, load, conductivity, flags, region, k["sq"], k["sq_z"], k["w_rows"], k["w_z"],
              k["grad_f"], k["back_f"])
    inputs = tuple(pltpu.with_memory_space_constraint(v, pltpu.HBM) for v in inputs)
    buffers = [pltpu.VMEM(v.shape, v.dtype) for v in inputs[:9]]
    buffers[0] = pltpu.SMEM(kappa_table.shape, F32)
    buffers[3] = pltpu.VMEM((16, 16, 128), jnp.int32)
    buffers += [pltpu.SemaphoreType.DMA((len(inputs),)), pltpu.VMEM((2, 56, COLS), F32)]
    small = tuple(jax.ShapeDtypeStruct(v.shape, v.dtype) for v in inputs[9:])
    coef, react, keep, part_l, part_d, even, odd, low_y, high_y, grad_f, back_f = call(
        first_kernel, (BIG, BIG, keep_shape, BIG, BIG) + (MESSAGE,) * 4 + small, [VM] + [HB] * len(inputs),
        buffers)(ctl, *inputs)
    mats = (k["grad"], k["back"], k["grad_z"], k["back_z"], grad_f, back_f)
    even, odd = along_x(even, odd)
    low_y, high_y = call(corner_kernel, (MESSAGE, MESSAGE), [VM] * 5, [pltpu.VMEM((2, 56, COLS), F32)])(
        ctl, even, odd, low_y, high_y)
    recv = (even, odd, *along_y(low_y, high_y))
    line = jax.ShapeDtypeStruct((8, COLS), F32)
    r, dinv, cf, cz, rz, part, *faces = step_call(
        second_kernel, (BIG, BIG, jax.ShapeDtypeStruct((64, COLS), F32), line, line) + PART, 15)(
        ctl, part_l, part_d, *recv, keep, coef, react, *mats)
    tail = (coef, react, cf, cz, rz, *mats)
    recv = exchange(faces)
    a1, part, *faces = step_call(sweep1_kernel, (BIG,) + PART, 18)(ctl, part, *recv, r, dinv, *tail)
    recv = exchange(faces)
    d34_shape = jax.ShapeDtypeStruct((2, 8, 128), F32)
    z, part, *faces, d34 = step_call(third_kernel, (BIG,) + PART + (d34_shape,), 20)(
        ctl, part, *recv, r, dinv, a1, load, *tail)
    recv = exchange(faces)
    d5_shape = jax.ShapeDtypeStruct((8, 128), F32)
    im, part, *faces, d5 = step_call(fourth_kernel, (BIG,) + PART + (d5_shape,), 18)(
        ctl, part, *recv, dinv, z, *tail)
    recv = exchange(faces)
    dots_shape = jax.ShapeDtypeStruct((n_y, 128), F32)
    b1, part, *faces, dots = step_call(fifth_kernel, (BIG,) + PART + (dots_shape,), 21)(
        ctl, part, *recv, im, dinv, z, d34, d5, *tail)
    total = lax.all_to_all(dots, "gy", 0, 0, tiled=True).sum(0)
    recv = exchange(faces)
    total = lax.all_to_all(jnp.broadcast_to(total, (n_x, 128)), "gx", 0, 0, tiled=True).sum(0)
    shape = jax.ShapeDtypeStruct((16, 16, COLS), F32)
    scratch = [pltpu.VMEM((ROWS, COLS), F32)] + [pltpu.VMEM((16, 16, COLS), F32)] * 3 + [pltpu.SemaphoreType.DMA((3,))]
    return pl.pallas_call(
        last_kernel, out_shape=(shape, shape, shape), in_specs=[SM] + [VM] * 11, out_specs=(HB, HB, HB),
        scratch_shapes=scratch, compiler_params=PARAMS)(total, ctl, part, *recv, im, dinv, b1, z, r)


def solution(mesh):
    placed = P("gx", "gy", None)
    return jax.shard_map(
        per_device,
        mesh=mesh,
        in_specs=(placed, placed, placed, placed, P()),
        out_specs=(placed, placed, placed),
        check_vma=False,
    )
```
